32 devices in a mesh: rows: 8 (over z, y), mp: 4 (over x, core).
Axes of the slice: x: 2, y: 2, z: 4, core: 2. Of those that a mesh axis runs over, the one named last changes fastest.
Arguments:
- calib: bfloat16 [512, 8192], P('rows', 'mp'), may hold values from -40 to 40
- weight: bfloat16 [8192, 8192], P('rows', 'mp'), may hold values from -6 to 6
- inverse_factor: float32 [8192, 8192], P('rows', 'mp'), may hold values from -10 to 12, as said below
- pruned_blocks: int32 [7], replicated, may hold values from 0 to 63, as said below
Outputs:
- pruned_weight: bfloat16 [8192, 8192], P('rows', 'mp')
- next_gram: float32 [8192, 8192], P('rows', 'mp')
The draws below stay inside these ranges and needn't reach their ends.
Inputs may be any that keep to these rules, and one draw needn't show every extreme that they name: `pruned_blocks`: 7 distinct block numbers in any order; block b holds rows b * 128 to b * 128 + 127. `inverse_factor`: symmetric and positive definite.
All inputs are finite; a program needn't handle non-finite values.
Results may differ from the reference program's by a relative error of at most 0.0095.
Values may be sent and summed in bfloat16 or wider, within the bound.
A program may use at most 128 MiB of HBM per device.

```python
import jax
import jax.numpy as jnp
from jax import lax

D = 8192
BLOCK = 128
NB = 7
TOKENS = 512


def draw_calib(key, part):
    first, second, third = jax.random.split(jax.random.fold_in(key, 31), 3)
    row_scale = jnp.exp(jax.random.uniform(first, (TOKENS, 1), jnp.float32, jnp.log(0.3), jnp.log(3.0)))
    col_scale = jnp.exp(jax.random.uniform(second, (1, D), jnp.float32, jnp.log(0.5), jnp.log(2.0)))
    values = jax.random.normal(third, (TOKENS, D), jnp.float32)
    return jnp.clip(values * row_scale * col_scale, -40.0, 40.0).astype(jnp.bfloat16)


def draw_inverse_factor(key, part):
    first, second, third = jax.random.split(jax.random.fold_in(key, 11), 3)
    factor_rank = max(NB * BLOCK // 4, 4)
    coeff = 0.003 / jnp.sqrt(2.0 * D)
    noise = jax.random.normal(first, (D, D), jnp.float32)
    diagonal = jnp.exp(jax.random.uniform(second, (D,), jnp.float32, jnp.log(0.02), jnp.log(2.0)))
    loadings = jnp.clip(jax.random.normal(third, (D, factor_rank), jnp.float32), -3.0, 3.0)
    noise = jnp.clip(noise, -6.0, 6.0)
    shared = jnp.dot(loadings, loadings.T, precision=lax.Precision.HIGHEST) * (1.0 / factor_rank)
    shared = 0.5 * (shared + shared.T)
    return (noise + noise.T) * coeff + shared + jnp.diag(diagonal)


def draw_pruned_blocks(key, part):
    first, second = jax.random.split(jax.random.fold_in(key, 5), 2)
    inner = jax.random.permutation(first, D // BLOCK - 2)[:NB - 2].astype(jnp.int32) + 1
    ends = jnp.array([0, D // BLOCK - 1], dtype=jnp.int32)
    blocks = jnp.concatenate([ends, inner])
    order = jax.random.permutation(second, NB)
    return blocks[order].astype(jnp.int32)


def levels(key, extent, shards, smallest, high):
    def one(axis_at, parts):
        draws = jax.random.uniform(jax.random.fold_in(jax.random.fold_in(key, 6), axis_at), (parts,), jnp.float32, smallest / len(shards), high / len(shards))
        return jnp.repeat(jnp.exp(draws), extent[axis_at] // parts).reshape((-1,) + (1,) * (len(extent) - axis_at - 1))

    level = one(*shards[0])
    for cut in shards[1:]:
        level = level * one(*cut)
    return level


def scatter_about(own_key, extent, width, reach, cuts=(), kind=jnp.bfloat16):
    values = jax.random.normal(own_key, extent, jnp.float32) * width
    if len(cuts) > 0:
        values = levels(own_key, extent, cuts, -0.22, 0.18) * values
    return jnp.clip(values, min=-reach, max=reach).astype(kind)


def setup_inputs(seed: int = 0) -> dict:
    streams_of = jax.random.split(jax.random.key(seed), 5)
    return {
        "calib": draw_calib(jax.random.fold_in(streams_of[4], 71), 0),
        "weight": scatter_about(streams_of[1], (D, D), 1.0, 6.0, ((0, 8), (1, 4))),
        "inverse_factor": draw_inverse_factor(jax.random.fold_in(streams_of[4], 71), 0),
        "pruned_blocks": draw_pruned_blocks(jax.random.fold_in(streams_of[4], 71), 0),
    }


def spd_solve(chol_lower, right_side):
    forward = lax.linalg.triangular_solve(chol_lower, right_side, left_side=True, lower=True)
    return lax.linalg.triangular_solve(chol_lower, forward, left_side=True, lower=True, transpose_a=True)

def reference(calib, weight, inverse_factor, pruned_blocks):
    row_numbers = (pruned_blocks[:, None] * BLOCK + jnp.arange(BLOCK, dtype=jnp.int32)[None, :]).reshape(-1).astype(jnp.int32)
    columns = jnp.take(inverse_factor, row_numbers, axis=1)
    square = jnp.take(columns, row_numbers, axis=0)
    kept_rows = jnp.take(weight, row_numbers, axis=0).astype(jnp.float32)
    chol_lower = jnp.linalg.cholesky(square)
    solved = spd_solve(chol_lower, kept_rows)
    update = jnp.dot(columns, solved, precision=lax.Precision.HIGHEST)
    block_ids = jnp.arange(D, dtype=jnp.int32) // BLOCK
    kept_mask = 1.0 - jnp.any(block_ids[:, None] == pruned_blocks[None, :], axis=1).astype(jnp.float32)
    pruned_weight = ((weight.astype(jnp.float32) - update) * kept_mask[:, None]).astype(jnp.bfloat16)
    projected = jnp.dot(calib.astype(jnp.float32), pruned_weight.T.astype(jnp.float32), preferred_element_type=jnp.float32)
    outputs = (projected * float(D) ** (-0.5)).astype(jnp.bfloat16)
    next_gram = jnp.dot(outputs.T.astype(jnp.float32), outputs.astype(jnp.float32), preferred_element_type=jnp.float32) / TOKENS
    return (pruned_weight, next_gram)
```

```python
import functools

import jax
import jax.numpy as jnp
from jax import lax
from jax.experimental import pallas as pl
from jax.experimental.pallas import tpu as pltpu
from jax.sharding import PartitionSpec as P

BLOCK = 128
SUB = 8
GROUP = 4
MIB = 1024 * 1024
VMEM = pl.BlockSpec(memory_space=pltpu.VMEM)
SMEM = pl.BlockSpec(memory_space=pltpu.SMEM)


def split3(value):
    first = value.astype(jnp.bfloat16)
    rest = value - first.astype(jnp.float32)
    second = rest.astype(jnp.bfloat16)
    third = (rest - second.astype(jnp.float32)).astype(jnp.bfloat16)
    return first, second, third


def sweep_block(tiles):
    lane = lax.broadcasted_iota(jnp.int32, (SUB, BLOCK), 1)
    sublane = lax.broadcasted_iota(jnp.int32, (SUB, BLOCK), 0)
    wide = (SUB, BLOCK)
    for p in range(0, BLOCK, GROUP):
        own, s = p // SUB, p % SUB
        rows = [
            jnp.broadcast_to(tiles[own][s + a : s + a + 1, :], wide) for a in range(GROUP)
        ]
        small = {}
        for a in range(GROUP):
            for b in range(a, GROUP):
                small[a, b] = jnp.broadcast_to(rows[a][:, p + b : p + b + 1], wide)
        for k in range(GROUP):
            inv = 1.0 / small[k, k]
            old = {a: small[min(a, k), max(a, k)] for a in range(GROUP) if a != k}
            scaled = {a: value * inv for a, value in old.items()}
            for a in old:
                for b in old:
                    if a <= b:
                        small[a, b] = small[a, b] - old[a] * scaled[b]
                small[min(a, k), max(a, k)] = scaled[a]
            small[k, k] = -inv
        pivots = [lane == p + a for a in range(GROUP)]
        updates = []
        for a in range(GROUP):
            update = -small[0, a] * rows[0]
            for b in range(1, GROUP):
                update = update - small[min(a, b), max(a, b)] * rows[b]
            for b in range(GROUP):
                update = jnp.where(pivots[b], small[min(a, b), max(a, b)], update)
            updates.append(update)
        inside = (lane >= p) & (lane < p + GROUP)
        new = []
        for t in range(len(tiles)):
            value = jnp.where(inside, 0.0, tiles[t])
            for a in range(GROUP):
                column = jnp.broadcast_to(tiles[t][:, p + a : p + a + 1], wide)
                value = value - column * updates[a]
            if t == own:
                for a in range(GROUP):
                    value = jnp.where(sublane == s + a, updates[a], value)
            new.append(value)
        tiles = new
    return tiles


def bits_of(count):
    return count.bit_length() - 1


def flip(index, k):
    return index + (1 - 2 * ((index // 2**k) % 2)) * 2**k


def reversed_bits(index, count):
    value = 0
    for k in range(bits_of(count)):
        value = value * 2 + (index // 2**k) % 2
    return value


def ordered_bits(index, order):
    value = 0
    for k in order:
        value = value * 2 + (index // 2**k) % 2
    return value


def span(start, size, unit):
    return pl.ds(pl.multiple_of(start, unit), size)


class Links:
    def __init__(self, send_sem, recv_sem):
        self.send_sem = send_sem
        self.recv_sem = recv_sem
        self.used = 0

    def copy(self, src, dst, device):
        at = self.used
        self.used += 1
        return lambda: pltpu.make_async_remote_copy(
            src_ref=src,
            dst_ref=dst,
            send_sem=self.send_sem.at[at],
            recv_sem=self.recv_sem.at[at],
            device_id=device,
            device_id_type=pl.DeviceIdType.MESH,
        )


def greet(devices):
    barrier = pltpu.get_barrier_semaphore()
    for device in devices:
        pl.semaphore_signal(
            barrier, inc=1, device_id=device, device_id_type=pl.DeviceIdType.MESH
        )
    pl.semaphore_wait(barrier, len(devices))


def everyone():
    row_parts, mp_parts = lax.axis_size("rows"), lax.axis_size("mp")
    r, m = lax.axis_index("rows"), lax.axis_index("mp")
    devices = [{"mp": flip(m, k)} for k in range(bits_of(mp_parts))]
    devices += [{"rows": lax.rem(r + d, row_parts)} for d in range(1, row_parts)]
    return devices


def add_rows(out_ref, out_at, left_ref, left_at, right_ref, right_at, size, unit):
    chunk = unit

    def body(t, carry):
        step = pl.multiple_of(t * chunk, chunk)
        a = left_ref[span(left_at + step, chunk, 16), :].astype(jnp.float32)
        b = right_ref[span(right_at + step, chunk, 16), :].astype(jnp.float32)
        out_ref[span(out_at + step, chunk, 16), :] = (a + b).astype(out_ref.dtype)
        return carry

    lax.fori_loop(0, size // chunk, body, 0)


def reduce_sizes(piece, row_parts, mp_parts):
    size = piece * row_parts * mp_parts
    return (size - piece * row_parts) + (row_parts - 1) * piece


def reduce_count(row_parts, mp_parts):
    return 2 * bits_of(mp_parts) + 2 * (row_parts - 1)


def reduce_steps(links, src, acc, recv, out, piece):
    row_parts, mp_parts = lax.axis_size("rows"), lax.axis_size("mp")
    r, m = lax.axis_index("rows"), lax.axis_index("mp")
    stages = []
    size, base, off = piece * row_parts * mp_parts, 0, 0
    held = []
    for k in range(bits_of(mp_parts)):
        held.append((base, size))
        size //= 2
        bit = (m // 2**k) % 2
        keep, send = base + bit * size, base + (1 - bit) * size
        source = src if k == 0 else acc
        copy = links.copy(
            source.at[span(send, size, 16)],
            recv.at[pl.ds(off, size)],
            {"mp": flip(m, k)},
        )

        def merge(source=source, keep=keep, off=off, size=size):
            add_rows(acc, keep, source, keep, recv, off, size, piece)

        stages.append(([copy], merge))
        base, off = keep, off + size
    copies = []
    for d in range(1, row_parts):
        to = lax.rem(r + d, row_parts)
        copies.append(
            links.copy(
                acc.at[span(base + to * piece, piece, 16)],
                recv.at[pl.ds(off + (d - 1) * piece, piece)],
                {"rows": to},
            )
        )

    def total(base=base, off=off):
        mine = span(base + r * piece, piece, 16)
        value = acc[mine, :].astype(jnp.float32)
        for d in range(1, row_parts):
            value = value + recv[pl.ds(off + (d - 1) * piece, piece), :].astype(jnp.float32)
        out[mine, :] = value.astype(out.dtype)

    stages.append((copies, total))
    copies = []
    for d in range(1, row_parts):
        mine = out.at[span(base + r * piece, piece, 16)]
        copies.append(links.copy(mine, mine, {"rows": lax.rem(r + d, row_parts)}))
    stages.append((copies, None))
    for k in reversed(range(bits_of(mp_parts))):
        mine = out.at[span(base, size, 16)]
        stages.append(([links.copy(mine, mine, {"mp": flip(m, k)})], None))
        base, size = held[k]
    return stages


def steps_of(stages):
    steps = []
    for s in range(len(stages) + 1):

        def step(s=s):
            if s > 0:
                for copy in stages[s - 1][0]:
                    copy().wait()
                if stages[s - 1][1] is not None:
                    stages[s - 1][1]()
            if s < len(stages):
                for copy in stages[s][0]:
                    copy().start()

        steps.append(step)
    return steps


def run_steps(*lists):
    for s in range(max(len(one) for one in lists)):
        for one in lists:
            if s < len(one):
                one[s]()


def sum_low_kernel(src_ref, out_ref, acc_ref, recv_ref, send_sem, recv_sem):
    greet(everyone())
    links = Links(send_sem, recv_sem)
    pieces = lax.axis_size("rows") * lax.axis_size("mp")
    piece = src_ref.shape[0] // pieces
    run_steps(steps_of(reduce_steps(links, src_ref, acc_ref, recv_ref, out_ref, piece)))


def sum_low(low):
    row_parts, mp_parts = lax.axis_size("rows"), lax.axis_size("mp")
    piece = low.shape[0] // (row_parts * mp_parts)
    count = reduce_count(row_parts, mp_parts)
    return pl.pallas_call(
        sum_low_kernel,
        out_shape=jax.ShapeDtypeStruct(low.shape, low.dtype),
        in_specs=[VMEM],
        out_specs=VMEM,
        scratch_shapes=[
            pltpu.VMEM(low.shape, low.dtype),
            pltpu.VMEM((reduce_sizes(piece, row_parts, mp_parts), BLOCK), low.dtype),
            pltpu.SemaphoreType.DMA((count,)),
            pltpu.SemaphoreType.DMA((count,)),
        ],
        compiler_params=pltpu.CompilerParams(
            collective_id=1, has_side_effects=True, vmem_limit_bytes=16 * MIB
        ),
    )(low)


def scatter_steps(links, src, acc, recv, out):
    m, mp_parts = lax.axis_index("mp"), lax.axis_size("mp")
    stages = []
    size, base, off = mp_parts, 0, 0
    depth = bits_of(mp_parts)
    for k in range(depth):
        size //= 2
        bit = (m // 2**k) % 2
        keep, send = base + bit * size, base + (1 - bit) * size
        source = src if k == 0 else acc
        copy = links.copy(
            source.at[pl.ds(send, size)], recv.at[pl.ds(off, size)], {"mp": flip(m, k)}
        )

        def merge(source=source, keep=keep, off=off, size=size, k=k):
            for t in range(size):
                a = source[keep + t].astype(jnp.float32)
                b = recv[off + t].astype(jnp.float32)
                if k == depth - 1:
                    out[...] = a + b
                else:
                    acc[keep + t] = (a + b).astype(acc.dtype)

        stages.append(([copy], merge))
        base, off = keep, off + size
    return stages


def sum_outputs_kernel(
    y_ref, sel_ref, own_ref, all_ref, y_acc, y_recv, acc_ref, recv_ref, send_sem, recv_sem
):
    greet(everyone())
    links = Links(send_sem, recv_sem)
    piece = sel_ref.shape[0] // (lax.axis_size("rows") * lax.axis_size("mp"))
    run_steps(
        steps_of(reduce_steps(links, sel_ref, acc_ref, recv_ref, all_ref, piece)),
        steps_of(scatter_steps(links, y_ref, y_acc, y_recv, own_ref)),
    )


def sum_outputs(y, selected):
    row_parts, mp_parts = lax.axis_size("rows"), lax.axis_size("mp")
    piece = selected.shape[0] // (row_parts * mp_parts)
    count = reduce_count(row_parts, mp_parts) + bits_of(mp_parts)
    _, tokens, part = y.shape
    return pl.pallas_call(
        sum_outputs_kernel,
        out_shape=(
            jax.ShapeDtypeStruct((tokens, part), jnp.float32),
            jax.ShapeDtypeStruct(selected.shape, selected.dtype),
        ),
        in_specs=[VMEM, VMEM],
        out_specs=(VMEM, VMEM),
        scratch_shapes=[
            pltpu.VMEM(y.shape, y.dtype),
            pltpu.VMEM((mp_parts - 1, tokens, part), y.dtype),
            pltpu.VMEM(selected.shape, selected.dtype),
            pltpu.VMEM((reduce_sizes(piece, row_parts, mp_parts), BLOCK), selected.dtype),
            pltpu.SemaphoreType.DMA((count,)),
            pltpu.SemaphoreType.DMA((count,)),
        ],
        compiler_params=pltpu.CompilerParams(
            collective_id=2, has_side_effects=True, vmem_limit_bytes=32 * MIB
        ),
    )(y, selected)


def pick_columns_kernel(places_ref, factor_ref, columns_ref, low_ref):
    j = pl.program_id(0)
    count = places_ref.shape[1]
    used = count * (count + 1) // 2 * BLOCK
    mp_parts = lax.axis_size("mp")
    part = factor_ref.shape[0] // mp_parts
    own = places_ref[1, j] != 0
    for at in range(mp_parts):
        q = reversed_bits(at, mp_parts)
        value = factor_ref[q * part : (q + 1) * part, :]
        columns_ref[at * part : (at + 1) * part, :] = jnp.where(own, value, 0.0)
    if low_ref.shape[0] > used:
        low_ref[used:, :] = jnp.zeros((low_ref.shape[0] - used, BLOCK), low_ref.dtype)
    for i in range(count):

        @pl.when(i >= j)
        def _():
            rows = pl.ds(pl.multiple_of(places_ref[2, i] * BLOCK, BLOCK), BLOCK)
            to = pl.ds(pl.multiple_of((i * (i + 1) // 2 + j) * BLOCK, BLOCK), BLOCK)
            both = (places_ref[3, i] != 0) & own
            low_ref[to, :] = jnp.where(both, factor_ref[rows, :], 0.0)


def padded(used):
    pieces = lax.axis_size("rows") * lax.axis_size("mp")
    return -(-used // (pieces * 16)) * pieces * 16


def pick_columns(places, factor):
    count = places.shape[1]
    rows = factor.shape[0]
    low_rows = padded(count * (count + 1) // 2 * BLOCK)
    return pl.pallas_call(
        pick_columns_kernel,
        out_shape=(
            jax.ShapeDtypeStruct((rows, count * BLOCK), jnp.float32),
            jax.ShapeDtypeStruct((low_rows, BLOCK), jnp.float32),
        ),
        grid_spec=pltpu.PrefetchScalarGridSpec(
            num_scalar_prefetch=1,
            grid=(count,),
            in_specs=[pl.BlockSpec((rows, BLOCK), lambda j, places: (0, places[0, j]))],
            out_specs=(
                pl.BlockSpec((rows, BLOCK), lambda j, places: (0, j)),
                pl.BlockSpec((low_rows, BLOCK), lambda j, places: (0, 0)),
            ),
        ),
    )(places, factor)


def pick_rows_kernel(places_ref, weight_ref, out_ref):
    inside = places_ref[3, pl.program_id(0)] != 0
    value = weight_ref[...].astype(jnp.float32)
    out_ref[...] = jnp.where(inside, value, 0.0).astype(jnp.bfloat16)


def pick_rows(places, weight):
    count = places.shape[1]
    width = weight.shape[1]
    return pl.pallas_call(
        pick_rows_kernel,
        out_shape=jax.ShapeDtypeStruct((count * BLOCK, width), jnp.bfloat16),
        grid_spec=pltpu.PrefetchScalarGridSpec(
            num_scalar_prefetch=1,
            grid=(count,),
            in_specs=[pl.BlockSpec((BLOCK, width), lambda i, places: (places[2, i], 0))],
            out_specs=pl.BlockSpec((BLOCK, width), lambda i, places: (i, 0)),
        ),
    )(places, weight)


def project_kernel(scale, places_ref, calib_ref, weight_ref, y_ref, sel_ref):
    step = pl.program_id(0)
    count = places_ref.shape[1]
    tokens = calib_ref.shape[0]
    tile = weight_ref.shape[0]
    part = y_ref.shape[2]

    @pl.when(step == 0)
    def _():
        sel_ref[...] = jnp.zeros(sel_ref.shape, sel_ref.dtype)

    value = lax.dot_general(
        calib_ref[...],
        weight_ref[...],
        (((1,), (1,)), ((), ())),
        preferred_element_type=jnp.float32,
    )
    value = (value * scale).astype(jnp.bfloat16)
    for s in range(tile // part):
        y_ref[s] = value[:, s * part : (s + 1) * part]
    for i in range(count):
        for s in range(tile // BLOCK):
            here = step * (tile // BLOCK) + s

            @pl.when((places_ref[3, i] != 0) & (places_ref[2, i] == here))
            def _():
                sel_ref[i * tokens : (i + 1) * tokens, :] = value[:, s * BLOCK : (s + 1) * BLOCK]


def project(places, calib, weight, scale):
    count = places.shape[1]
    tokens, width = calib.shape
    rows = weight.shape[0]
    mp_parts = lax.axis_size("mp")
    part = rows // mp_parts
    tile = max(part, BLOCK)
    sel_rows = padded(count * tokens)
    return pl.pallas_call(
        functools.partial(project_kernel, scale),
        out_shape=(
            jax.ShapeDtypeStruct((mp_parts, tokens, part), jnp.bfloat16),
            jax.ShapeDtypeStruct((sel_rows, BLOCK), jnp.bfloat16),
        ),
        grid_spec=pltpu.PrefetchScalarGridSpec(
            num_scalar_prefetch=1,
            grid=(rows // tile,),
            in_specs=[
                pl.BlockSpec((tokens, width), lambda i, places: (0, 0)),
                pl.BlockSpec((tile, width), lambda i, places: (i, 0)),
            ],
            out_specs=(
                pl.BlockSpec((tile // part, tokens, part), lambda i, places: (i, 0, 0)),
                pl.BlockSpec((sel_rows, BLOCK), lambda i, places: (0, 0)),
            ),
        ),
        compiler_params=pltpu.CompilerParams(vmem_limit_bytes=32 * MIB),
    )(places, calib, weight)


def invert(low_ref, out_ref, neg_ref, rhs_ref, pivot_ref):
    count = out_ref.shape[0] // BLOCK
    at = 0
    for i in range(count):
        for j in range(i + 1):
            block = low_ref[at : at + BLOCK, :]
            at += BLOCK
            out_ref[i * BLOCK : (i + 1) * BLOCK, j * BLOCK : (j + 1) * BLOCK] = block
            if j < i:
                out_ref[j * BLOCK : (j + 1) * BLOCK, i * BLOCK : (i + 1) * BLOCK] = block.T

    def stage(k, carry):
        here = pl.ds(pl.multiple_of(k * BLOCK, BLOCK), BLOCK)
        diag = out_ref[here, here]
        tiles = [diag[t * SUB : (t + 1) * SUB, :] for t in range(BLOCK // SUB)]
        tiles = sweep_block(tiles)
        for t in range(BLOCK // SUB):
            neg_ref[t * SUB : (t + 1) * SUB, :] = tiles[t]
        neg = neg_ref[...]
        r1, r2, r3 = split3(out_ref[here, :])
        a1, a2, a3 = split3(-neg)
        pivot_ref[...] = jnp.dot(
            jnp.concatenate([a1, a1, a2, a2, a1, a3], axis=1),
            jnp.concatenate([r1, r2, r1, r2, r3, r1], axis=0),
            preferred_element_type=jnp.float32,
        )
        pivot_ref[:, here] = neg
        b1, b2, b3 = split3(pivot_ref[...])
        for slot, part in enumerate((b1, b2, b1, b2, b3, b1)):
            rhs_ref[slot * BLOCK : (slot + 1) * BLOCK, :] = part

        def update(i, inner):
            rows = pl.ds(pl.multiple_of(i * BLOCK, BLOCK), BLOCK)
            c1, c2, c3 = split3(out_ref[rows, here])
            out_ref[rows, here] = jnp.zeros((BLOCK, BLOCK), jnp.float32)
            out_ref[rows, :] -= jnp.dot(
                jnp.concatenate([c1, c1, c2, c2, c1, c3], axis=1),
                rhs_ref[...],
                preferred_element_type=jnp.float32,
            )
            return inner

        lax.fori_loop(0, count, update, 0)
        out_ref[here, :] = pivot_ref[...]
        return carry

    lax.fori_loop(0, count, stage, 0)


def outputs_from(square_ref, columns_ref, y_ref, sel_ref, keep_ref, total_ref, factor_ref, out_ref):
    count = square_ref.shape[0] // BLOCK
    tokens = y_ref.shape[0]
    total_ref[...] = jnp.zeros(total_ref.shape, jnp.float32)

    def body(k, carry):
        here = pl.ds(pl.multiple_of(k * BLOCK, BLOCK), BLOCK)
        c1, c2, c3 = split3(columns_ref[:, here])
        n1, n2, n3 = split3(square_ref[here, :])
        total_ref[...] -= jnp.dot(
            jnp.concatenate([c1, c1, c2, c2, c1, c3], axis=1),
            jnp.concatenate([n1, n2, n1, n2, n3, n1], axis=0),
            preferred_element_type=jnp.float32,
        )
        return carry

    lax.fori_loop(0, count, body, 0)
    factor_ref[...] = total_ref[...].astype(jnp.bfloat16)
    selected = jnp.concatenate(
        [sel_ref[i * tokens : (i + 1) * tokens, :] for i in range(count)], axis=1
    )
    update = lax.dot_general(
        selected, factor_ref[...], (((1,), (1,)), ((), ())), preferred_element_type=jnp.float32
    )
    value = jnp.where(keep_ref[...] != 0.0, y_ref[...] - update, 0.0)
    out_ref[...] = value.astype(jnp.bfloat16)


def solve_kernel(
    low_ref, columns_ref, y_ref, sel_ref, keep_ref, factor_ref, out_ref,
    square_ref, neg_ref, rhs_ref, pivot_ref, total_ref,
):
    invert(low_ref, square_ref, neg_ref, rhs_ref, pivot_ref)
    outputs_from(
        square_ref, columns_ref, y_ref, sel_ref, keep_ref, total_ref, factor_ref, out_ref
    )


def solve(low, own_columns, own_y, selected, keep):
    part, order = own_columns.shape
    tokens = own_y.shape[0]
    return pl.pallas_call(
        solve_kernel,
        out_shape=(
            jax.ShapeDtypeStruct((part, order), jnp.bfloat16),
            jax.ShapeDtypeStruct((tokens, part), jnp.bfloat16),
        ),
        in_specs=[VMEM] * 5,
        out_specs=(VMEM, VMEM),
        scratch_shapes=[
            pltpu.VMEM((order, order), jnp.float32),
            pltpu.VMEM((BLOCK, BLOCK), jnp.float32),
            pltpu.VMEM((6 * BLOCK, order), jnp.bfloat16),
            pltpu.VMEM((BLOCK, order), jnp.float32),
            pltpu.VMEM((part, order), jnp.float32),
        ],
        compiler_params=pltpu.CompilerParams(vmem_limit_bytes=40 * MIB),
        cost_estimate=pl.CostEstimate(
            flops=60_000_000_000, bytes_accessed=2 * order * order * 4, transcendentals=0
        ),
    )(low, own_columns, own_y, selected, keep)


def moved_to(r, m, row_parts, mp_parts):
    per = row_parts // mp_parts
    return ((m + 1) % mp_parts) * per + r % per, r // per


def right_orders(row_parts):
    count = bits_of(row_parts)
    first = list(range(count))
    second = [1, 0] + first[2:] if count > 1 else first
    return first, second


def exchange_kernel(out_ref, factor_ref, left_ref, right_ref, all_factor_ref, send_sem, recv_sem):
    row_parts, mp_parts = lax.axis_size("rows"), lax.axis_size("mp")
    r, m = lax.axis_index("rows"), lax.axis_index("mp")
    per = row_parts // mp_parts
    tokens = out_ref.shape[0]
    to_row, to_mp = moved_to(r, m, row_parts, mp_parts)
    from_row = m * per + r % per
    from_mp = lax.rem(r // per + mp_parts - 1, mp_parts)
    devices = [{"mp": flip(m, k)} for k in range(bits_of(mp_parts))]
    devices += [{"rows": flip(r, k)} for k in range(bits_of(row_parts))]
    target = {"rows": to_row, "mp": to_mp}
    devices += [target, {"rows": from_row, "mp": from_mp}]
    greet(devices)
    links = Links(send_sem, recv_sem)
    mine = reversed_bits(m, mp_parts)

    orders = right_orders(row_parts)
    lists = []
    for h, order in enumerate(orders):
        half = tokens // 2
        slot = ordered_bits(to_row, order)
        copy = links.copy(
            out_ref.at[pl.ds(h * half, half)], right_ref.at[h, slot], target
        )
        stages = [([copy], None)]
        base, size = ordered_bits(r, order), 1
        for k in reversed(order):
            region = right_ref.at[h, pl.ds(base, size)]
            stages.append(([links.copy(region, region, {"rows": flip(r, k)})], None))
            base = base - ((base // size) % 2) * size
            size *= 2
        lists.append(steps_of(stages))
    for src, dst in ((out_ref, left_ref), (factor_ref, all_factor_ref)):
        stages = []
        base, size = mine, 1
        for k in reversed(range(bits_of(mp_parts))):
            region = dst.at[pl.ds(base, size)]
            source = src if size == 1 else region
            sink = dst.at[base] if size == 1 else region
            stages.append(([links.copy(source, sink, {"mp": flip(m, k)})], None))
            base = base - ((base // size) % 2) * size
            size *= 2
        lists.append(steps_of(stages))
    left_ref[mine] = out_ref[...]
    all_factor_ref[mine] = factor_ref[...]
    run_steps(*lists)


def exchange(outputs, factor):
    row_parts, mp_parts = lax.axis_size("rows"), lax.axis_size("mp")
    tokens, part = outputs.shape
    order = factor.shape[1]
    count = 2 * (1 + bits_of(row_parts)) + 2 * bits_of(mp_parts)
    return pl.pallas_call(
        exchange_kernel,
        out_shape=(
            jax.ShapeDtypeStruct((mp_parts, tokens, part), jnp.bfloat16),
            jax.ShapeDtypeStruct((2, row_parts, tokens // 2, part), jnp.bfloat16),
            jax.ShapeDtypeStruct((mp_parts, part, order), jnp.bfloat16),
        ),
        in_specs=[VMEM, VMEM],
        out_specs=(VMEM, VMEM, VMEM),
        scratch_shapes=[
            pltpu.SemaphoreType.DMA((count,)),
            pltpu.SemaphoreType.DMA((count,)),
        ],
        compiler_params=pltpu.CompilerParams(
            collective_id=3, has_side_effects=True, vmem_limit_bytes=32 * MIB
        ),
    )(outputs, factor)


def gram_kernel(row_parts, mp_parts, left_ref, right_ref, out_ref):
    per = row_parts // mp_parts
    tokens, part = left_ref.shape[1:]
    first, second = right_orders(row_parts)
    left = left_ref[0]
    for at in range(row_parts):
        source_mp = (at // per - 1) % mp_parts
        column = (at % per) * mp_parts + reversed_bits(source_mp, mp_parts)
        right = jnp.concatenate(
            [right_ref[0, ordered_bits(at, first)], right_ref[1, ordered_bits(at, second)]], axis=0
        )
        value = lax.dot_general(
            left, right, (((0,), (0,)), ((), ())), preferred_element_type=jnp.float32
        )
        out_ref[:, column * part : (column + 1) * part] = value / tokens


def gram_of(left, right):
    mp_parts, tokens, part = left.shape
    row_parts = right.shape[1]
    width = row_parts * part
    return pl.pallas_call(
        functools.partial(gram_kernel, row_parts, mp_parts),
        grid=(mp_parts,),
        in_specs=[pl.BlockSpec((1, tokens, part), lambda i: (i, 0, 0)), VMEM],
        out_specs=pl.BlockSpec((part, width), lambda i: (i, 0)),
        out_shape=jax.ShapeDtypeStruct((mp_parts * part, width), jnp.float32),
        compiler_params=pltpu.CompilerParams(vmem_limit_bytes=32 * MIB),
    )(left, right)


def prune_kernel(flags_ref, weight_ref, factor_ref, kept_ref, out_ref):
    step = pl.program_id(0)
    tile, width = weight_ref.shape
    chunk = min(width, 512)
    for c in range(width // chunk):
        lanes = slice(c * chunk, (c + 1) * chunk)
        update = jnp.dot(factor_ref[...], kept_ref[:, lanes], preferred_element_type=jnp.float32)
        value = weight_ref[:, lanes].astype(jnp.float32) - update
        for s in range(tile // BLOCK):
            gone = flags_ref[step * (tile // BLOCK) + s] != 0
            rows = slice(s * BLOCK, (s + 1) * BLOCK)
            out_ref[rows, lanes] = jnp.where(gone, 0.0, value[rows, :]).astype(jnp.bfloat16)


def prune(flags, weight, factor, kept_rows):
    rows, width = weight.shape
    order = factor.shape[1]
    tile = min(rows, 256)
    return pl.pallas_call(
        prune_kernel,
        out_shape=jax.ShapeDtypeStruct((rows, width), jnp.bfloat16),
        grid_spec=pltpu.PrefetchScalarGridSpec(
            num_scalar_prefetch=1,
            grid=(rows // tile,),
            in_specs=[
                pl.BlockSpec((tile, width), lambda i, flags: (i, 0)),
                pl.BlockSpec((tile, order), lambda i, flags: (i, 0)),
                pl.BlockSpec((order, width), lambda i, flags: (0, 0)),
            ],
            out_specs=pl.BlockSpec((tile, width), lambda i, flags: (i, 0)),
        ),
        compiler_params=pltpu.CompilerParams(vmem_limit_bytes=32 * MIB),
    )(flags, weight, factor, kept_rows)


def shards(calib, weight, inverse_factor, pruned_blocks):
    rows_dev, width_dev = weight.shape
    mp_parts = lax.axis_size("mp")
    full_width = width_dev * mp_parts
    part = rows_dev // mp_parts
    m = lax.axis_index("mp")
    row_start = lax.axis_index("rows") * rows_dev
    col_start = m * width_dev
    starts = pruned_blocks * BLOCK
    col_offsets = starts - col_start
    row_offsets = starts - row_start
    places = jnp.stack(
        [
            jnp.clip(col_offsets, 0, width_dev - BLOCK) // BLOCK,
            ((col_offsets >= 0) & (col_offsets < width_dev)).astype(jnp.int32),
            jnp.clip(row_offsets, 0, rows_dev - BLOCK) // BLOCK,
            ((row_offsets >= 0) & (row_offsets < rows_dev)).astype(jnp.int32),
        ]
    ).astype(jnp.int32)
    block_ids = row_start // BLOCK + jnp.arange(rows_dev // BLOCK, dtype=jnp.int32)
    flags = jnp.any(block_ids[:, None] == pruned_blocks[None, :], axis=1).astype(jnp.int32)
    own_start = row_start + reversed_bits(m, mp_parts) * part
    own_ids = (own_start + jnp.arange(part, dtype=jnp.int32)) // BLOCK
    keep = 1.0 - jnp.any(own_ids[:, None] == pruned_blocks[None, :], axis=1).astype(jnp.float32)

    columns, own_low = pick_columns(places, inverse_factor)
    own_kept = pick_rows(places, weight)
    kept_rows = lax.psum(own_kept, "rows")
    all_calib = lax.all_gather(calib, "rows", axis=0, tiled=True)
    own_columns = lax.psum_scatter(columns, "mp", scatter_dimension=0, tiled=True)
    low = sum_low(own_low)
    y, own_selected = project(places, all_calib, weight, float(full_width) ** (-0.5))
    own_y, selected = sum_outputs(y, own_selected)
    factor, outputs = solve(low, own_columns, own_y, selected, keep[None, :])
    left, right, all_factor = exchange(outputs, factor)
    gram_block = gram_of(left, right)
    pruned_weight = prune(
        flags, weight, all_factor.reshape(rows_dev, factor.shape[1]), kept_rows
    )
    return (pruned_weight, gram_block)


def solution(mesh):
    return jax.shard_map(
        shards,
        mesh=mesh,
        in_specs=(P("rows", "mp"), P("rows", "mp"), P("rows", "mp"), P()),
        out_specs=(P("rows", "mp"), P("rows", "mp")),
        check_vma=False,
    )
```

```python
import functools

import jax
import jax.numpy as jnp
from jax import lax
from jax.experimental import pallas as pl
from jax.experimental.pallas import tpu as pltpu
from jax.sharding import PartitionSpec as P

BLOCK = 128
SUB = 8
GROUP = 4
MIB = 1024 * 1024
VMEM = pl.BlockSpec(memory_space=pltpu.VMEM)
SMEM = pl.BlockSpec(memory_space=pltpu.SMEM)


def split3(value):
    first = value.astype(jnp.bfloat16)
    rest = value - first.astype(jnp.float32)
    second = rest.astype(jnp.bfloat16)
    third = (rest - second.astype(jnp.float32)).astype(jnp.bfloat16)
    return first, second, third


def sweep_block(tiles):
    lane = lax.broadcasted_iota(jnp.int32, (SUB, BLOCK), 1)
    sublane = lax.broadcasted_iota(jnp.int32, (SUB, BLOCK), 0)
    wide = (SUB, BLOCK)
    for p in range(0, BLOCK, GROUP):
        own, s = p // SUB, p % SUB
        rows = [
            jnp.broadcast_to(tiles[own][s + a : s + a + 1, :], wide) for a in range(GROUP)
        ]
        small = {}
        for a in range(GROUP):
            for b in range(a, GROUP):
                small[a, b] = jnp.broadcast_to(rows[a][:, p + b : p + b + 1], wide)
        for k in range(GROUP):
            inv = 1.0 / small[k, k]
            old = {a: small[min(a, k), max(a, k)] for a in range(GROUP) if a != k}
            scaled = {a: value * inv for a, value in old.items()}
            for a in old:
                for b in old:
                    if a <= b:
                        small[a, b] = small[a, b] - old[a] * scaled[b]
                small[min(a, k), max(a, k)] = scaled[a]
            small[k, k] = -inv
        pivots = [lane == p + a for a in range(GROUP)]
        updates = []
        for a in range(GROUP):
            update = -small[0, a] * rows[0]
            for b in range(1, GROUP):
                update = update - small[min(a, b), max(a, b)] * rows[b]
            for b in range(GROUP):
                update = jnp.where(pivots[b], small[min(a, b), max(a, b)], update)
            updates.append(update)
        inside = (lane >= p) & (lane < p + GROUP)
        new = []
        for t in range(len(tiles)):
            value = jnp.where(inside, 0.0, tiles[t])
            for a in range(GROUP):
                column = jnp.broadcast_to(tiles[t][:, p + a : p + a + 1], wide)
                value = value - column * updates[a]
            if t == own:
                for a in range(GROUP):
                    value = jnp.where(sublane == s + a, updates[a], value)
            new.append(value)
        tiles = new
    return tiles


def bits_of(count):
    return count.bit_length() - 1


def flip(index, k):
    return index + (1 - 2 * ((index // 2**k) % 2)) * 2**k


def reversed_bits(index, count):
    value = 0
    for k in range(bits_of(count)):
        value = value * 2 + (index // 2**k) % 2
    return value


def ordered_bits(index, order):
    value = 0
    for k in order:
        value = value * 2 + (index // 2**k) % 2
    return value


def span(start, size, unit):
    return pl.ds(pl.multiple_of(start, unit), size)


class Links:
    def __init__(self, send_sem, recv_sem):
        self.send_sem = send_sem
        self.recv_sem = recv_sem
        self.used = 0

    def copy(self, src, dst, device):
        at = self.used
        self.used += 1
        return lambda: pltpu.make_async_remote_copy(
            src_ref=src,
            dst_ref=dst,
            send_sem=self.send_sem.at[at],
            recv_sem=self.recv_sem.at[at],
            device_id=device,
            device_id_type=pl.DeviceIdType.MESH,
        )


def greet(devices):
    barrier = pltpu.get_barrier_semaphore()
    for device in devices:
        pl.semaphore_signal(
            barrier, inc=1, device_id=device, device_id_type=pl.DeviceIdType.MESH
        )
    pl.semaphore_wait(barrier, len(devices))


def everyone():
    row_parts, mp_parts = lax.axis_size("rows"), lax.axis_size("mp")
    r, m = lax.axis_index("rows"), lax.axis_index("mp")
    devices = [{"mp": flip(m, k)} for k in range(bits_of(mp_parts))]
    devices += [{"rows": lax.rem(r + d, row_parts)} for d in range(1, row_parts)]
    return devices


def add_rows(out_ref, out_at, left_ref, left_at, right_ref, right_at, size, unit):
    chunk = unit

    def body(t, carry):
        step = pl.multiple_of(t * chunk, chunk)
        a = left_ref[span(left_at + step, chunk, 16), :].astype(jnp.float32)
        b = right_ref[span(right_at + step, chunk, 16), :].astype(jnp.float32)
        out_ref[span(out_at + step, chunk, 16), :] = (a + b).astype(out_ref.dtype)
        return carry

    lax.fori_loop(0, size // chunk, body, 0)


def reduce_sizes(piece, row_parts, mp_parts):
    size = piece * row_parts * mp_parts
    return (size - piece * row_parts) + (row_parts - 1) * piece


def reduce_count(row_parts, mp_parts):
    return 2 * bits_of(mp_parts) + 2 * (row_parts - 1)


def reduce_steps(links, src, acc, recv, out, piece):
    row_parts, mp_parts = lax.axis_size("rows"), lax.axis_size("mp")
    r, m = lax.axis_index("rows"), lax.axis_index("mp")
    stages = []
    size, base, off = piece * row_parts * mp_parts, 0, 0
    held = []
    for k in range(bits_of(mp_parts)):
        held.append((base, size))
        size //= 2
        bit = (m // 2**k) % 2
        keep, send = base + bit * size, base + (1 - bit) * size
        source = src if k == 0 else acc
        copy = links.copy(
            source.at[span(send, size, 16)],
            recv.at[pl.ds(off, size)],
            {"mp": flip(m, k)},
        )

        def merge(source=source, keep=keep, off=off, size=size):
            add_rows(acc, keep, source, keep, recv, off, size, piece)

        stages.append(([copy], merge))
        base, off = keep, off + size
    copies = []
    for d in range(1, row_parts):
        to = lax.rem(r + d, row_parts)
        copies.append(
            links.copy(
                acc.at[span(base + to * piece, piece, 16)],
                recv.at[pl.ds(off + (d - 1) * piece, piece)],
                {"rows": to},
            )
        )

    def total(base=base, off=off):
        mine = span(base + r * piece, piece, 16)
        value = acc[mine, :].astype(jnp.float32)
        for d in range(1, row_parts):
            value = value + recv[pl.ds(off + (d - 1) * piece, piece), :].astype(jnp.float32)
        out[mine, :] = value.astype(out.dtype)

    stages.append((copies, total))
    copies = []
    for d in range(1, row_parts):
        mine = out.at[span(base + r * piece, piece, 16)]
        copies.append(links.copy(mine, mine, {"rows": lax.rem(r + d, row_parts)}))
    stages.append((copies, None))
    for k in reversed(range(bits_of(mp_parts))):
        mine = out.at[span(base, size, 16)]
        stages.append(([links.copy(mine, mine, {"mp": flip(m, k)})], None))
        base, size = held[k]
    return stages


def steps_of(stages):
    steps = []
    for s in range(len(stages) + 1):

        def step(s=s):
            if s > 0:
                for copy in stages[s - 1][0]:
                    copy().wait()
                if stages[s - 1][1] is not None:
                    stages[s - 1][1]()
            if s < len(stages):
                for copy in stages[s][0]:
                    copy().start()

        steps.append(step)
    return steps


def joined(*lists):
    def step(s):
        for one in lists:
            if s < len(one):
                one[s]()

    return [functools.partial(step, s) for s in range(max(len(one) for one in lists))]


def spread(steps, gap):
    wide = []
    for step in steps:
        wide += [step] + [lambda: None] * (gap - 1)
    return wide[: len(wide) - gap + 1]


def run_steps(*lists):
    for step in joined(*lists):
        step()


def ring_place(r):
    row_parts = lax.axis_size("rows")
    return (1 - r % 2) * (r // 2) + (r % 2) * (row_parts - 1 - r // 2)


def ring_member(place):
    row_parts = lax.axis_size("rows")
    place = lax.rem(place + 2 * row_parts, row_parts)
    second = (2 * place) // row_parts
    return (1 - second) * 2 * place + second * (2 * (row_parts - 1 - place) + 1)


def ring_devices():
    place = ring_place(lax.axis_index("rows"))
    return [{"rows": ring_member(place + 1)}, {"rows": ring_member(place - 1)}]


def ring_sum_stages(links, src, recv, acc, out, sign, lanes):
    row_parts = lax.axis_size("rows")
    place = ring_place(lax.axis_index("rows"))
    to = {"rows": ring_member(place + sign)}
    size = src.shape[0] // row_parts

    def chunk(step):
        at = lax.rem(place - sign * step + 2 * row_parts, row_parts)
        return span(at * size, size, 16)

    stages = []
    for s in range(row_parts - 1):
        source = src.at[chunk(0), lanes] if s == 0 else acc.at[s - 1]
        last = s == row_parts - 2

        def merge(s=s, last=last, rows=chunk(s + 1)):
            value = src[rows, lanes] + recv[s]
            if last:
                out[rows, lanes] = value
            else:
                acc[s] = value

        stages.append(([links.copy(source, recv.at[s], to)], merge))
    for s in range(row_parts - 1):
        piece = out.at[chunk(s - 1), lanes]
        stages.append(([links.copy(piece, piece, to)], None))
    return stages


def ring_gather_stages(links, src, out, sign, hops):
    row_parts = lax.axis_size("rows")
    place = ring_place(lax.axis_index("rows"))
    to = {"rows": ring_member(place + sign)}
    size = src.shape[0]
    stages = []
    for s in range(hops):
        at = lax.rem(place - sign * s + 2 * row_parts, row_parts)
        piece = out.at[span(at * size, size, 16)]
        stages.append(([links.copy(src if s == 0 else piece, piece, to)], None))
    return stages


def gather_kernel(
    src_ref, calib_ref, out_ref, all_calib_ref, acc_ref, recv_ref, send_sem, recv_sem
):
    row_parts = lax.axis_size("rows")
    greet(everyone())
    links = Links(send_sem, recv_sem)
    piece = src_ref.shape[0] // (row_parts * lax.axis_size("mp"))
    steps = joined(
        steps_of(reduce_steps(links, src_ref, acc_ref, recv_ref, out_ref, piece)),
        steps_of(ring_gather_stages(links, calib_ref, all_calib_ref, 1, row_parts // 2)),
        steps_of(ring_gather_stages(links, calib_ref, all_calib_ref, -1, row_parts // 2 - 1)),
    )
    steps[0]()
    place = ring_place(lax.axis_index("rows"))
    size = calib_ref.shape[0]
    all_calib_ref[span(place * size, size, 16), :] = calib_ref[...]
    for step in steps[1:]:
        step()


def gather(low, calib):
    row_parts, mp_parts = lax.axis_size("rows"), lax.axis_size("mp")
    piece = low.shape[0] // (row_parts * mp_parts)
    count = reduce_count(row_parts, mp_parts) + row_parts - 1
    return pl.pallas_call(
        gather_kernel,
        out_shape=(
            jax.ShapeDtypeStruct(low.shape, low.dtype),
            jax.ShapeDtypeStruct((calib.shape[0] * row_parts, calib.shape[1]), calib.dtype),
        ),
        in_specs=[VMEM, VMEM],
        out_specs=(VMEM, VMEM),
        scratch_shapes=[
            pltpu.VMEM(low.shape, low.dtype),
            pltpu.VMEM((reduce_sizes(piece, row_parts, mp_parts), BLOCK), low.dtype),
            pltpu.SemaphoreType.DMA((count,)),
            pltpu.SemaphoreType.DMA((count,)),
        ],
        compiler_params=pltpu.CompilerParams(
            collective_id=1, has_side_effects=True, vmem_limit_bytes=24 * MIB
        ),
    )(low, calib)


def scatter_steps(links, src, acc, recv, out):
    m, mp_parts = lax.axis_index("mp"), lax.axis_size("mp")
    stages = []
    size, base, off = mp_parts, 0, 0
    depth = bits_of(mp_parts)
    for k in range(depth):
        size //= 2
        bit = (m // 2**k) % 2
        keep, send = base + bit * size, base + (1 - bit) * size
        source = src if k == 0 else acc
        copy = links.copy(
            source.at[pl.ds(send, size)], recv.at[pl.ds(off, size)], {"mp": flip(m, k)}
        )

        def merge(source=source, keep=keep, off=off, size=size, k=k):
            for t in range(size):
                a = source[keep + t].astype(jnp.float32)
                b = recv[off + t].astype(jnp.float32)
                if k == depth - 1:
                    out[...] = a + b
                else:
                    acc[keep + t] = (a + b).astype(acc.dtype)

        stages.append(([copy], merge))
        base, off = keep, off + size
    return stages


def pick_columns_kernel(places_ref, factor_ref, columns_ref, low_ref):
    j = pl.program_id(0)
    count = places_ref.shape[1]
    used = count * (count + 1) // 2 * BLOCK
    own = places_ref[1, j] != 0
    columns_ref[...] = jnp.where(own, factor_ref[...], 0.0)
    if low_ref.shape[0] > used:
        low_ref[used:, :] = jnp.zeros((low_ref.shape[0] - used, BLOCK), low_ref.dtype)
    for i in range(count):

        @pl.when(i >= j)
        def _():
            rows = pl.ds(pl.multiple_of(places_ref[2, i] * BLOCK, BLOCK), BLOCK)
            to = pl.ds(pl.multiple_of((i * (i + 1) // 2 + j) * BLOCK, BLOCK), BLOCK)
            both = (places_ref[3, i] != 0) & own
            low_ref[to, :] = jnp.where(both, factor_ref[rows, :], 0.0)


def padded(used):
    pieces = lax.axis_size("rows") * lax.axis_size("mp")
    return -(-used // (pieces * 16)) * pieces * 16


def pick_columns(places, factor):
    count = places.shape[1]
    rows = factor.shape[0]
    low_rows = padded(count * (count + 1) // 2 * BLOCK)
    return pl.pallas_call(
        pick_columns_kernel,
        out_shape=(
            jax.ShapeDtypeStruct((rows, count * BLOCK), jnp.float32),
            jax.ShapeDtypeStruct((low_rows, BLOCK), jnp.float32),
        ),
        grid_spec=pltpu.PrefetchScalarGridSpec(
            num_scalar_prefetch=1,
            grid=(count,),
            in_specs=[pl.BlockSpec((rows, BLOCK), lambda j, places: (0, places[0, j]))],
            out_specs=(
                pl.BlockSpec((rows, BLOCK), lambda j, places: (0, j)),
                pl.BlockSpec((low_rows, BLOCK), lambda j, places: (0, 0)),
            ),
        ),
    )(places, factor)


def pick_rows_kernel(places_ref, weight_ref, out_ref):
    step = pl.program_id(0)
    count = places_ref.shape[1]
    inside = (places_ref[3, jnp.minimum(step, count - 1)] != 0) & (step < count)
    value = weight_ref[...].astype(jnp.float32)
    out_ref[...] = jnp.where(inside, value, 0.0).astype(jnp.bfloat16)


def pick_rows(places, weight):
    count = places.shape[1]
    width = weight.shape[1]
    unit = 16 * lax.axis_size("rows")
    blocks = -(-(-(-count * BLOCK // unit) * unit) // BLOCK)
    return pl.pallas_call(
        pick_rows_kernel,
        out_shape=jax.ShapeDtypeStruct((blocks * BLOCK, width), jnp.bfloat16),
        grid_spec=pltpu.PrefetchScalarGridSpec(
            num_scalar_prefetch=1,
            grid=(blocks,),
            in_specs=[
                pl.BlockSpec(
                    (BLOCK, width), lambda i, places: (places[2, jnp.minimum(i, count - 1)], 0)
                )
            ],
            out_specs=pl.BlockSpec((BLOCK, width), lambda i, places: (i, 0)),
        ),
    )(places, weight)


def project_kernel(scale, places_ref, calib_ref, weight_ref, y_ref, sel_ref):
    step = pl.program_id(0)
    count = places_ref.shape[1]
    tokens = calib_ref.shape[0]
    tile = weight_ref.shape[0]
    part = y_ref.shape[2]

    @pl.when(step == 0)
    def _():
        sel_ref[...] = jnp.zeros(sel_ref.shape, sel_ref.dtype)

    value = lax.dot_general(
        calib_ref[...],
        weight_ref[...],
        (((1,), (1,)), ((), ())),
        preferred_element_type=jnp.float32,
    )
    value = (value * scale).astype(jnp.bfloat16)
    for s in range(tile // part):
        y_ref[s] = value[:, s * part : (s + 1) * part]
    for i in range(count):
        for s in range(tile // BLOCK):
            here = step * (tile // BLOCK) + s

            @pl.when((places_ref[3, i] != 0) & (places_ref[2, i] == here))
            def _():
                sel_ref[i * tokens : (i + 1) * tokens, :] = value[:, s * BLOCK : (s + 1) * BLOCK]


def project(places, calib, weight, scale):
    count = places.shape[1]
    tokens, width = calib.shape
    rows = weight.shape[0]
    mp_parts = lax.axis_size("mp")
    part = rows // mp_parts
    tile = max(part, BLOCK)
    sel_rows = padded(count * tokens)
    return pl.pallas_call(
        functools.partial(project_kernel, scale),
        out_shape=(
            jax.ShapeDtypeStruct((mp_parts, tokens, part), jnp.bfloat16),
            jax.ShapeDtypeStruct((sel_rows, BLOCK), jnp.bfloat16),
        ),
        grid_spec=pltpu.PrefetchScalarGridSpec(
            num_scalar_prefetch=1,
            grid=(rows // tile,),
            in_specs=[
                pl.BlockSpec((tokens, width), lambda i, places: (0, 0)),
                pl.BlockSpec((tile, width), lambda i, places: (i, 0)),
            ],
            out_specs=(
                pl.BlockSpec((tile // part, tokens, part), lambda i, places: (i, 0, 0)),
                pl.BlockSpec((sel_rows, BLOCK), lambda i, places: (0, 0)),
            ),
        ),
        compiler_params=pltpu.CompilerParams(vmem_limit_bytes=32 * MIB),
    )(places, calib, weight)


def invert(low_ref, out_ref, neg_ref, rhs_ref, pivot_ref, steps):
    count = out_ref.shape[0] // BLOCK
    at = 0
    for i in range(count):
        for j in range(i + 1):
            block = low_ref[at : at + BLOCK, :]
            at += BLOCK
            out_ref[i * BLOCK : (i + 1) * BLOCK, j * BLOCK : (j + 1) * BLOCK] = block
            if j < i:
                out_ref[j * BLOCK : (j + 1) * BLOCK, i * BLOCK : (i + 1) * BLOCK] = block.T

    def stage(k, carry):
        for s in range(0, min(2 * count, len(steps)), 2):
            pl.when(2 * k == s)(steps[s])
        here = pl.ds(pl.multiple_of(k * BLOCK, BLOCK), BLOCK)
        diag = out_ref[here, here]
        tiles = [diag[t * SUB : (t + 1) * SUB, :] for t in range(BLOCK // SUB)]
        tiles = sweep_block(tiles)
        for t in range(BLOCK // SUB):
            neg_ref[t * SUB : (t + 1) * SUB, :] = tiles[t]
        for s in range(1, min(2 * count, len(steps)), 2):
            pl.when(2 * k + 1 == s)(steps[s])
        neg = neg_ref[...]
        r1, r2, r3 = split3(out_ref[here, :])
        a1, a2, a3 = split3(-neg)
        pivot_ref[...] = jnp.dot(
            jnp.concatenate([a1, a1, a2, a2, a1, a3], axis=1),
            jnp.concatenate([r1, r2, r1, r2, r3, r1], axis=0),
            preferred_element_type=jnp.float32,
        )
        pivot_ref[:, here] = neg
        b1, b2, b3 = split3(pivot_ref[...])
        for slot, part in enumerate((b1, b2, b1, b2, b3, b1)):
            rhs_ref[slot * BLOCK : (slot + 1) * BLOCK, :] = part

        def update(i, inner):
            rows = pl.ds(pl.multiple_of(i * BLOCK, BLOCK), BLOCK)
            c1, c2, c3 = split3(out_ref[rows, here])
            out_ref[rows, here] = jnp.zeros((BLOCK, BLOCK), jnp.float32)
            out_ref[rows, :] -= jnp.dot(
                jnp.concatenate([c1, c1, c2, c2, c1, c3], axis=1),
                rhs_ref[...],
                preferred_element_type=jnp.float32,
            )
            return inner

        lax.fori_loop(0, count, update, 0)
        out_ref[here, :] = pivot_ref[...]
        return carry

    lax.fori_loop(0, count, stage, 0)
    for s in range(2 * count, len(steps)):
        steps[s]()


def outputs_from(square_ref, columns_ref, y_ref, sel_ref, keep_ref, total_ref, factor_ref, out_ref):
    count = square_ref.shape[0] // BLOCK
    tokens = y_ref.shape[0]
    total_ref[...] = jnp.zeros(total_ref.shape, jnp.float32)

    def body(k, carry):
        here = pl.ds(pl.multiple_of(k * BLOCK, BLOCK), BLOCK)
        c1, c2, c3 = split3(columns_ref[:, here])
        n1, n2, n3 = split3(square_ref[here, :])
        total_ref[...] -= jnp.dot(
            jnp.concatenate([c1, c1, c2, c2, c1, c3], axis=1),
            jnp.concatenate([n1, n2, n1, n2, n3, n1], axis=0),
            preferred_element_type=jnp.float32,
        )
        return carry

    lax.fori_loop(0, count, body, 0)
    factor_ref[...] = total_ref[...].astype(jnp.bfloat16)
    selected = jnp.concatenate(
        [sel_ref[i * tokens : (i + 1) * tokens, :] for i in range(count)], axis=1
    )
    update = lax.dot_general(
        selected, factor_ref[...], (((1,), (1,)), ((), ())), preferred_element_type=jnp.float32
    )
    value = jnp.where(keep_ref[...] != 0.0, y_ref[...] - update, 0.0)
    out_ref[...] = value.astype(jnp.bfloat16)


def solve_kernel(
    low_ref, columns_ref, y_ref, sel_ref, keep_ref, kept_ref,
    factor_ref, out_ref, all_kept_ref,
    square_ref, neg_ref, rhs_ref, pivot_ref, total_ref,
    own_columns_ref, c_acc, c_recv, own_ref, y_acc, y_recv, all_ref, acc_ref, recv_ref,
    k_acc, k_recv, send_sem, recv_sem,
):
    greet(everyone())
    links = Links(send_sem, recv_sem)
    piece = sel_ref.shape[0] // (lax.axis_size("rows") * lax.axis_size("mp"))
    half = kept_ref.shape[1] // 2
    sum_steps = joined(
        steps_of(reduce_steps(links, sel_ref, acc_ref, recv_ref, all_ref, piece)),
        steps_of(scatter_steps(links, y_ref, y_acc, y_recv, own_ref)),
    )
    steps = joined(
        steps_of(
            ring_sum_stages(
                links, kept_ref, k_recv.at[0], k_acc.at[0], all_kept_ref, 1, slice(0, half)
            )
        ),
        steps_of(
            ring_sum_stages(
                links, kept_ref, k_recv.at[1], k_acc.at[1], all_kept_ref, -1, slice(half, 2 * half)
            )
        ),
        spread(sum_steps, 2),
        spread(steps_of(scatter_steps(links, columns_ref, c_acc, c_recv, own_columns_ref)), 6),
    )
    invert(low_ref, square_ref, neg_ref, rhs_ref, pivot_ref, steps)
    outputs_from(
        square_ref, own_columns_ref, own_ref, all_ref, keep_ref, total_ref, factor_ref, out_ref
    )


def solve(low, columns, y, selected, keep, kept):
    row_parts, mp_parts = lax.axis_size("rows"), lax.axis_size("mp")
    piece = selected.shape[0] // (row_parts * mp_parts)
    copies = reduce_count(row_parts, mp_parts) + 2 * bits_of(mp_parts)
    copies += 4 * (row_parts - 1)
    chunk = (row_parts - 1, kept.shape[0] // row_parts, kept.shape[1] // 2)
    _, part, order = columns.shape
    tokens = y.shape[1]
    return pl.pallas_call(
        solve_kernel,
        out_shape=(
            jax.ShapeDtypeStruct((part, order), jnp.bfloat16),
            jax.ShapeDtypeStruct((tokens, part), jnp.bfloat16),
            jax.ShapeDtypeStruct(kept.shape, kept.dtype),
        ),
        in_specs=[VMEM] * 6,
        out_specs=(VMEM, VMEM, VMEM),
        scratch_shapes=[
            pltpu.VMEM((order, order), jnp.float32),
            pltpu.VMEM((BLOCK, BLOCK), jnp.float32),
            pltpu.VMEM((6 * BLOCK, order), jnp.bfloat16),
            pltpu.VMEM((BLOCK, order), jnp.float32),
            pltpu.VMEM((part, order), jnp.float32),
            pltpu.VMEM((part, order), jnp.float32),
            pltpu.VMEM(columns.shape, jnp.float32),
            pltpu.VMEM((mp_parts - 1, part, order), jnp.float32),
            pltpu.VMEM((tokens, part), jnp.float32),
            pltpu.VMEM(y.shape, y.dtype),
            pltpu.VMEM((mp_parts - 1, tokens, part), y.dtype),
            pltpu.VMEM(selected.shape, selected.dtype),
            pltpu.VMEM(selected.shape, selected.dtype),
            pltpu.VMEM((reduce_sizes(piece, row_parts, mp_parts), BLOCK), selected.dtype),
            pltpu.VMEM((2,) + chunk, kept.dtype),
            pltpu.VMEM((2,) + chunk, kept.dtype),
            pltpu.SemaphoreType.DMA((copies,)),
            pltpu.SemaphoreType.DMA((copies,)),
        ],
        compiler_params=pltpu.CompilerParams(
            collective_id=2, has_side_effects=True, vmem_limit_bytes=48 * MIB
        ),
        cost_estimate=pl.CostEstimate(
            flops=60_000_000_000, bytes_accessed=2 * order * order * 4, transcendentals=0
        ),
    )(low, columns, y, selected, keep, kept)


def moved_to(r, m, row_parts, mp_parts):
    per = row_parts // mp_parts
    return ((m + 1) % mp_parts) * per + r % per, r // per


def right_orders(row_parts):
    count = bits_of(row_parts)
    first = list(range(count))
    second = [1, 0] + first[2:] if count > 1 else first
    return first, second


def exchange_kernel(out_ref, factor_ref, left_ref, right_ref, all_factor_ref, send_sem, recv_sem):
    row_parts, mp_parts = lax.axis_size("rows"), lax.axis_size("mp")
    r, m = lax.axis_index("rows"), lax.axis_index("mp")
    per = row_parts // mp_parts
    tokens = out_ref.shape[0]
    to_row, to_mp = moved_to(r, m, row_parts, mp_parts)
    from_row = m * per + r % per
    from_mp = lax.rem(r // per + mp_parts - 1, mp_parts)
    devices = [{"mp": flip(m, k)} for k in range(bits_of(mp_parts))]
    devices += [{"rows": flip(r, k)} for k in range(bits_of(row_parts))]
    target = {"rows": to_row, "mp": to_mp}
    devices += [target, {"rows": from_row, "mp": from_mp}]
    greet(devices)
    links = Links(send_sem, recv_sem)
    mine = reversed_bits(m, mp_parts)

    orders = right_orders(row_parts)
    lists = []
    for h, order in enumerate(orders):
        half = tokens // 2
        slot = ordered_bits(to_row, order)
        copy = links.copy(
            out_ref.at[pl.ds(h * half, half)], right_ref.at[h, slot], target
        )
        stages = [([copy], None)]
        base, size = ordered_bits(r, order), 1
        for k in reversed(order):
            region = right_ref.at[h, pl.ds(base, size)]
            stages.append(([links.copy(region, region, {"rows": flip(r, k)})], None))
            base = base - ((base // size) % 2) * size
            size *= 2
        lists.append(steps_of(stages))
    for src, dst in ((out_ref, left_ref), (factor_ref, all_factor_ref)):
        stages = []
        base, size = mine, 1
        for k in reversed(range(bits_of(mp_parts))):
            region = dst.at[pl.ds(base, size)]
            source = src if size == 1 else region
            sink = dst.at[base] if size == 1 else region
            stages.append(([links.copy(source, sink, {"mp": flip(m, k)})], None))
            base = base - ((base // size) % 2) * size
            size *= 2
        lists.append(steps_of(stages))
    left_ref[mine] = out_ref[...]
    all_factor_ref[mine] = factor_ref[...]
    run_steps(*lists)


def exchange(outputs, factor):
    row_parts, mp_parts = lax.axis_size("rows"), lax.axis_size("mp")
    tokens, part = outputs.shape
    order = factor.shape[1]
    count = 2 * (1 + bits_of(row_parts)) + 2 * bits_of(mp_parts)
    return pl.pallas_call(
        exchange_kernel,
        out_shape=(
            jax.ShapeDtypeStruct((mp_parts, tokens, part), jnp.bfloat16),
            jax.ShapeDtypeStruct((2, row_parts, tokens // 2, part), jnp.bfloat16),
            jax.ShapeDtypeStruct((mp_parts, part, order), jnp.bfloat16),
        ),
        in_specs=[VMEM, VMEM],
        out_specs=(VMEM, VMEM, VMEM),
        scratch_shapes=[
            pltpu.SemaphoreType.DMA((count,)),
            pltpu.SemaphoreType.DMA((count,)),
        ],
        compiler_params=pltpu.CompilerParams(
            collective_id=3, has_side_effects=True, vmem_limit_bytes=32 * MIB
        ),
    )(outputs, factor)


def gram_kernel(row_parts, mp_parts, left_ref, right_ref, out_ref):
    per = row_parts // mp_parts
    tokens, part = left_ref.shape[1:]
    first, second = right_orders(row_parts)
    left = left_ref[0]
    for at in range(row_parts):
        source_mp = (at // per - 1) % mp_parts
        column = (at % per) * mp_parts + reversed_bits(source_mp, mp_parts)
        right = jnp.concatenate(
            [right_ref[0, ordered_bits(at, first)], right_ref[1, ordered_bits(at, second)]], axis=0
        )
        value = lax.dot_general(
            left, right, (((0,), (0,)), ((), ())), preferred_element_type=jnp.float32
        )
        out_ref[:, column * part : (column + 1) * part] = value / tokens


def gram_of(left, right):
    mp_parts, tokens, part = left.shape
    row_parts = right.shape[1]
    width = row_parts * part
    return pl.pallas_call(
        functools.partial(gram_kernel, row_parts, mp_parts),
        grid=(mp_parts,),
        in_specs=[pl.BlockSpec((1, tokens, part), lambda i: (i, 0, 0)), VMEM],
        out_specs=pl.BlockSpec((part, width), lambda i: (i, 0)),
        out_shape=jax.ShapeDtypeStruct((mp_parts * part, width), jnp.float32),
        compiler_params=pltpu.CompilerParams(vmem_limit_bytes=32 * MIB),
    )(left, right)


def prune_kernel(flags_ref, weight_ref, factor_ref, kept_ref, out_ref):
    step = pl.program_id(0)
    tile, width = weight_ref.shape
    chunk = min(width, 512)
    for c in range(width // chunk):
        lanes = slice(c * chunk, (c + 1) * chunk)
        update = jnp.dot(factor_ref[...], kept_ref[:, lanes], preferred_element_type=jnp.float32)
        value = weight_ref[:, lanes].astype(jnp.float32) - update
        for s in range(tile // BLOCK):
            gone = flags_ref[step * (tile // BLOCK) + s] != 0
            rows = slice(s * BLOCK, (s + 1) * BLOCK)
            out_ref[rows, lanes] = jnp.where(gone, 0.0, value[rows, :]).astype(jnp.bfloat16)


def prune(flags, weight, factor, kept_rows):
    rows, width = weight.shape
    order = factor.shape[1]
    tile = min(rows, 256)
    return pl.pallas_call(
        prune_kernel,
        out_shape=jax.ShapeDtypeStruct((rows, width), jnp.bfloat16),
        grid_spec=pltpu.PrefetchScalarGridSpec(
            num_scalar_prefetch=1,
            grid=(rows // tile,),
            in_specs=[
                pl.BlockSpec((tile, width), lambda i, flags: (i, 0)),
                pl.BlockSpec((tile, order), lambda i, flags: (i, 0)),
                pl.BlockSpec((order, width), lambda i, flags: (0, 0)),
            ],
            out_specs=pl.BlockSpec((tile, width), lambda i, flags: (i, 0)),
        ),
        compiler_params=pltpu.CompilerParams(vmem_limit_bytes=32 * MIB),
    )(flags, weight, factor, kept_rows)


def shards(calib, weight, inverse_factor, pruned_blocks):
    rows_dev, width_dev = weight.shape
    mp_parts = lax.axis_size("mp")
    full_width = width_dev * mp_parts
    part = rows_dev // mp_parts
    m = lax.axis_index("mp")
    row_start = lax.axis_index("rows") * rows_dev
    col_start = m * width_dev
    starts = pruned_blocks * BLOCK
    col_offsets = starts - col_start
    row_offsets = starts - row_start
    places = jnp.stack(
        [
            jnp.clip(col_offsets, 0, width_dev - BLOCK) // BLOCK,
            ((col_offsets >= 0) & (col_offsets < width_dev)).astype(jnp.int32),
            jnp.clip(row_offsets, 0, rows_dev - BLOCK) // BLOCK,
            ((row_offsets >= 0) & (row_offsets < rows_dev)).astype(jnp.int32),
        ]
    ).astype(jnp.int32)
    block_ids = row_start // BLOCK + jnp.arange(rows_dev // BLOCK, dtype=jnp.int32)
    flags = jnp.any(block_ids[:, None] == pruned_blocks[None, :], axis=1).astype(jnp.int32)
    own_start = row_start + reversed_bits(m, mp_parts) * part
    own_ids = (own_start + jnp.arange(part, dtype=jnp.int32)) // BLOCK
    keep = 1.0 - jnp.any(own_ids[:, None] == pruned_blocks[None, :], axis=1).astype(jnp.float32)

    own_kept = pick_rows(places, weight)
    columns, own_low = pick_columns(places, inverse_factor)
    columns = columns.reshape(mp_parts, part, columns.shape[1])
    low, all_calib = gather(own_low, calib)
    y, own_selected = project(places, all_calib, weight, float(full_width) ** (-0.5))
    factor, outputs, kept_rows = solve(low, columns, y, own_selected, keep[None, :], own_kept)
    left, right, all_factor = exchange(outputs, factor)
    gram_block = gram_of(left, right)
    pruned_weight = prune(
        flags, weight, all_factor.reshape(rows_dev, factor.shape[1]), kept_rows
    )
    return (pruned_weight, gram_block)


def solution(mesh):
    return jax.shard_map(
        shards,
        mesh=mesh,
        in_specs=(P("rows", "mp"), P("rows", "mp"), P("rows", "mp"), P()),
        out_specs=(P("rows", "mp"), P("rows", "mp")),
        check_vma=False,
    )
```

```python
import functools

import jax
import jax.numpy as jnp
from jax import lax
from jax.experimental import pallas as pl
from jax.experimental.pallas import tpu as pltpu
from jax.sharding import PartitionSpec as P

BLOCK = 128
SUB = 8
GROUP = 4
TICKS = 4
MIB = 1024 * 1024
VMEM = pl.BlockSpec(memory_space=pltpu.VMEM)
SMEM = pl.BlockSpec(memory_space=pltpu.SMEM)


def split3(value):
    first = value.astype(jnp.bfloat16)
    rest = value - first.astype(jnp.float32)
    second = rest.astype(jnp.bfloat16)
    third = (rest - second.astype(jnp.float32)).astype(jnp.bfloat16)
    return first, second, third


def sweep_block(tiles, between):
    lane = lax.broadcasted_iota(jnp.int32, (SUB, BLOCK), 1)
    sublane = lax.broadcasted_iota(jnp.int32, (SUB, BLOCK), 0)
    wide = (SUB, BLOCK)
    for p in range(0, BLOCK, GROUP):
        if p == BLOCK // 2:
            between()
        own, s = p // SUB, p % SUB
        rows = [
            jnp.broadcast_to(tiles[own][s + a : s + a + 1, :], wide) for a in range(GROUP)
        ]
        small = {}
        for a in range(GROUP):
            for b in range(a, GROUP):
                small[a, b] = jnp.broadcast_to(rows[a][:, p + b : p + b + 1], wide)
        for k in range(GROUP):
            inv = 1.0 / small[k, k]
            old = {a: small[min(a, k), max(a, k)] for a in range(GROUP) if a != k}
            scaled = {a: value * inv for a, value in old.items()}
            for a in old:
                for b in old:
                    if a <= b:
                        small[a, b] = small[a, b] - old[a] * scaled[b]
                small[min(a, k), max(a, k)] = scaled[a]
            small[k, k] = -inv
        pivots = [lane == p + a for a in range(GROUP)]
        updates = []
        for a in range(GROUP):
            update = -small[0, a] * rows[0]
            for b in range(1, GROUP):
                update = update - small[min(a, b), max(a, b)] * rows[b]
            for b in range(GROUP):
                update = jnp.where(pivots[b], small[min(a, b), max(a, b)], update)
            updates.append(update)
        inside = (lane >= p) & (lane < p + GROUP)
        new = []
        for t in range(len(tiles)):
            value = jnp.where(inside, 0.0, tiles[t])
            for a in range(GROUP):
                column = jnp.broadcast_to(tiles[t][:, p + a : p + a + 1], wide)
                value = value - column * updates[a]
            if t == own:
                for a in range(GROUP):
                    value = jnp.where(sublane == s + a, updates[a], value)
            new.append(value)
        tiles = new
    return tiles


def bits_of(count):
    return count.bit_length() - 1


def flip(index, k):
    return index + (1 - 2 * ((index // 2**k) % 2)) * 2**k


def reversed_bits(index, count):
    value = 0
    for k in range(bits_of(count)):
        value = value * 2 + (index // 2**k) % 2
    return value


def ordered_bits(index, order):
    value = 0
    for k in order:
        value = value * 2 + (index // 2**k) % 2
    return value


def span(start, size, unit):
    return pl.ds(pl.multiple_of(start, unit), size)


class Links:
    def __init__(self, send_sem, recv_sem):
        self.send_sem = send_sem
        self.recv_sem = recv_sem
        self.used = 0

    def copy(self, src, dst, device):
        at = self.used
        self.used += 1
        return lambda: pltpu.make_async_remote_copy(
            src_ref=src,
            dst_ref=dst,
            send_sem=self.send_sem.at[at],
            recv_sem=self.recv_sem.at[at],
            device_id=device,
            device_id_type=pl.DeviceIdType.MESH,
        )


def greet(devices):
    barrier = pltpu.get_barrier_semaphore()
    for device in devices:
        pl.semaphore_signal(
            barrier, inc=1, device_id=device, device_id_type=pl.DeviceIdType.MESH
        )
    pl.semaphore_wait(barrier, len(devices))


def everyone():
    row_parts, mp_parts = lax.axis_size("rows"), lax.axis_size("mp")
    r, m = lax.axis_index("rows"), lax.axis_index("mp")
    devices = [{"mp": flip(m, k)} for k in range(bits_of(mp_parts))]
    devices += [{"rows": lax.rem(r + d, row_parts)} for d in range(1, row_parts)]
    return devices


def reduce_plans(rows):
    pieces = lax.axis_size("rows") * lax.axis_size("mp")
    depth = bits_of(lax.axis_size("mp"))
    units = rows // (16 * pieces)
    first = max(1, min(units - 1, (2 * units + 1) // 3))
    order = [f"mp{k}" for k in range(depth)]
    plans = [(0, 16 * first, order + ["rows"])]
    if units > first:
        plans.append((16 * first * pieces, 16 * (units - first), order[:1] + ["rows"] + order[1:]))
    return plans


def reduce_sizes(rows):
    row_parts, mp_parts = lax.axis_size("rows"), lax.axis_size("mp")
    total = 0
    for _, piece, order in reduce_plans(rows):
        size = piece * row_parts * mp_parts
        for dim in order:
            parts = row_parts if dim == "rows" else 2
            total += size - size // parts
            size //= parts
    return total


def reduce_count():
    return 4 * (bits_of(lax.axis_size("mp")) + lax.axis_size("rows") - 1)


def reduce_lists(links, src, acc, recv, out):
    lists, off = [], 0
    for start, piece, order in reduce_plans(src.shape[0]):
        stages, off = reduce_stages(links, src, acc, recv, out, start, piece, order, off)
        lists.append(steps_of(stages))
    return joined(*lists)


def reduce_stages(links, src, acc, recv, out, start, piece, order, off):
    row_parts, mp_parts = lax.axis_size("rows"), lax.axis_size("mp")
    r, m = lax.axis_index("rows"), lax.axis_index("mp")
    stages, held = [], []
    base, size = start, piece * row_parts * mp_parts
    for at, dim in enumerate(order):
        parts = row_parts if dim == "rows" else 2
        k = None if dim == "rows" else int(dim[2:])
        size //= parts
        source = src if at == 0 else acc
        sink = out if at == len(order) - 1 else acc
        copies = []
        for d in range(1, parts):
            to = lax.rem(r + d, row_parts) if k is None else 1 - (m // 2**k) % 2
            device = {"rows": to} if k is None else {"mp": flip(m, k)}
            copies.append(
                links.copy(
                    source.at[span(base + to * size, size, 16)],
                    recv.at[pl.ds(off + (d - 1) * size, size)],
                    device,
                )
            )
        keep = base + (r if k is None else (m // 2**k) % 2) * size

        def merge(source=source, sink=sink, keep=keep, off=off, size=size, parts=parts):
            def body(t, carry):
                step = pl.multiple_of(t * piece, 16)
                value = source[span(keep + step, piece, 16), :].astype(jnp.float32)
                for d in range(1, parts):
                    landed = recv[span(off + (d - 1) * size + step, piece, 16), :]
                    value = value + landed.astype(jnp.float32)
                sink[span(keep + step, piece, 16), :] = value.astype(sink.dtype)
                return carry

            lax.fori_loop(0, size // piece, body, 0)

        stages.append((copies, merge))
        off += (parts - 1) * size
        base = keep
        held.append((dim, k, keep, size))
    for dim, k, keep, size in reversed(held):
        mine = out.at[span(keep, size, 16)]
        if k is None:
            devices = [{"rows": lax.rem(r + d, row_parts)} for d in range(1, row_parts)]
        else:
            devices = [{"mp": flip(m, k)}]
        stages.append(([links.copy(mine, mine, device) for device in devices], None))
    return stages, off


def steps_of(stages):
    steps = []
    for s in range(len(stages) + 1):

        def step(s=s):
            if s > 0:
                for copy in stages[s - 1][0]:
                    copy().wait()
                if stages[s - 1][1] is not None:
                    stages[s - 1][1]()
            if s < len(stages):
                for copy in stages[s][0]:
                    copy().start()

        steps.append(step)
    return steps


def joined(*lists):
    def step(s):
        for one in lists:
            if s < len(one):
                one[s]()

    return [functools.partial(step, s) for s in range(max(len(one) for one in lists))]


def spread(steps, gap):
    wide = []
    for step in steps:
        wide += [step] + [lambda: None] * (gap - 1)
    return wide[: len(wide) - gap + 1]


def run_steps(*lists):
    for step in joined(*lists):
        step()


def ring_place(r):
    row_parts = lax.axis_size("rows")
    return (1 - r % 2) * (r // 2) + (r % 2) * (row_parts - 1 - r // 2)


def ring_member(place):
    row_parts = lax.axis_size("rows")
    place = lax.rem(place + 2 * row_parts, row_parts)
    second = (2 * place) // row_parts
    return (1 - second) * 2 * place + second * (2 * (row_parts - 1 - place) + 1)


def ring_devices():
    place = ring_place(lax.axis_index("rows"))
    return [{"rows": ring_member(place + 1)}, {"rows": ring_member(place - 1)}]


def ring_sum_stages(links, src, recv, acc, out, sign, lanes):
    row_parts = lax.axis_size("rows")
    place = ring_place(lax.axis_index("rows"))
    to = {"rows": ring_member(place + sign)}
    size = src.shape[0] // row_parts

    def chunk(step):
        at = lax.rem(place - sign * step + 2 * row_parts, row_parts)
        return span(at * size, size, 16)

    stages = []
    for s in range(row_parts - 1):
        source = src.at[chunk(0), lanes] if s == 0 else acc.at[s - 1]
        last = s == row_parts - 2

        def merge(s=s, last=last, rows=chunk(s + 1)):
            value = src[rows, lanes] + recv[s]
            if last:
                out[rows, lanes] = value
            else:
                acc[s] = value

        stages.append(([links.copy(source, recv.at[s], to)], merge))
    for s in range(row_parts - 1):
        piece = out.at[chunk(s - 1), lanes]
        stages.append(([links.copy(piece, piece, to)], None))
    return stages


def ring_gather_stages(links, src, out, sign, hops):
    row_parts = lax.axis_size("rows")
    place = ring_place(lax.axis_index("rows"))
    to = {"rows": ring_member(place + sign)}
    size = src.shape[0]
    stages = []
    for s in range(hops):
        at = lax.rem(place - sign * s + 2 * row_parts, row_parts)
        piece = out.at[span(at * size, size, 16)]
        stages.append(([links.copy(src if s == 0 else piece, piece, to)], None))
    return stages


def gather_kernel(
    src_ref, calib_ref, out_ref, all_calib_ref, acc_ref, recv_ref, send_sem, recv_sem
):
    row_parts = lax.axis_size("rows")
    greet(everyone())
    links = Links(send_sem, recv_sem)
    steps = joined(
        reduce_lists(links, src_ref, acc_ref, recv_ref, out_ref),
        steps_of(ring_gather_stages(links, calib_ref, all_calib_ref, 1, row_parts // 2)),
        steps_of(ring_gather_stages(links, calib_ref, all_calib_ref, -1, row_parts // 2 - 1)),
    )
    steps[0]()
    place = ring_place(lax.axis_index("rows"))
    size = calib_ref.shape[0]
    all_calib_ref[span(place * size, size, 16), :] = calib_ref[...]
    for step in steps[1:]:
        step()


def gather(low, calib):
    row_parts = lax.axis_size("rows")
    count = reduce_count() + row_parts - 1
    return pl.pallas_call(
        gather_kernel,
        out_shape=(
            jax.ShapeDtypeStruct(low.shape, low.dtype),
            jax.ShapeDtypeStruct((calib.shape[0] * row_parts, calib.shape[1]), calib.dtype),
        ),
        in_specs=[VMEM, VMEM],
        out_specs=(VMEM, VMEM),
        scratch_shapes=[
            pltpu.VMEM(low.shape, low.dtype),
            pltpu.VMEM((reduce_sizes(low.shape[0]), BLOCK), low.dtype),
            pltpu.SemaphoreType.DMA((count,)),
            pltpu.SemaphoreType.DMA((count,)),
        ],
        compiler_params=pltpu.CompilerParams(
            collective_id=1, has_side_effects=True, vmem_limit_bytes=24 * MIB
        ),
    )(low, calib)


def scatter_steps(links, src, acc, recv, out):
    m, mp_parts = lax.axis_index("mp"), lax.axis_size("mp")
    stages = []
    size, base, off = mp_parts, 0, 0
    depth = bits_of(mp_parts)
    for k in range(depth):
        size //= 2
        bit = (m // 2**k) % 2
        keep, send = base + bit * size, base + (1 - bit) * size
        source = src if k == 0 else acc
        copy = links.copy(
            source.at[pl.ds(send, size)], recv.at[pl.ds(off, size)], {"mp": flip(m, k)}
        )

        def merge(source=source, keep=keep, off=off, size=size, k=k):
            for t in range(size):
                a = source[keep + t].astype(jnp.float32)
                b = recv[off + t].astype(jnp.float32)
                if k == depth - 1:
                    out[...] = a + b
                else:
                    acc[keep + t] = (a + b).astype(acc.dtype)

        stages.append(([copy], merge))
        base, off = keep, off + size
    return stages


def pick_columns_kernel(places_ref, factor_ref, columns_ref, low_ref):
    j = pl.program_id(0)
    count = places_ref.shape[1]
    used = count * (count + 1) // 2 * BLOCK
    own = places_ref[1, j] != 0
    columns_ref[...] = jnp.where(own, factor_ref[...], 0.0)
    if low_ref.shape[0] > used:
        low_ref[used:, :] = jnp.zeros((low_ref.shape[0] - used, BLOCK), low_ref.dtype)
    for i in range(count):

        @pl.when(i >= j)
        def _():
            rows = pl.ds(pl.multiple_of(places_ref[2, i] * BLOCK, BLOCK), BLOCK)
            to = pl.ds(pl.multiple_of((i * (i + 1) // 2 + j) * BLOCK, BLOCK), BLOCK)
            both = (places_ref[3, i] != 0) & own
            low_ref[to, :] = jnp.where(both, factor_ref[rows, :], 0.0)


def padded(used):
    pieces = lax.axis_size("rows") * lax.axis_size("mp")
    return -(-used // (pieces * 16)) * pieces * 16


def pick_columns(places, factor):
    count = places.shape[1]
    rows = factor.shape[0]
    low_rows = padded(count * (count + 1) // 2 * BLOCK)
    return pl.pallas_call(
        pick_columns_kernel,
        out_shape=(
            jax.ShapeDtypeStruct((rows, count * BLOCK), jnp.float32),
            jax.ShapeDtypeStruct((low_rows, BLOCK), jnp.float32),
        ),
        grid_spec=pltpu.PrefetchScalarGridSpec(
            num_scalar_prefetch=1,
            grid=(count,),
            in_specs=[pl.BlockSpec((rows, BLOCK), lambda j, places: (0, places[0, j]))],
            out_specs=(
                pl.BlockSpec((rows, BLOCK), lambda j, places: (0, j)),
                pl.BlockSpec((low_rows, BLOCK), lambda j, places: (0, 0)),
            ),
        ),
    )(places, factor)


def pick_rows_kernel(places_ref, weight_ref, out_ref):
    step = pl.program_id(0)
    count = places_ref.shape[1]
    inside = (places_ref[3, jnp.minimum(step, count - 1)] != 0) & (step < count)
    value = weight_ref[...].astype(jnp.float32)
    out_ref[...] = jnp.where(inside, value, 0.0).astype(jnp.bfloat16)


def pick_rows(places, weight):
    count = places.shape[1]
    width = weight.shape[1]
    unit = 16 * lax.axis_size("rows")
    blocks = -(-(-(-count * BLOCK // unit) * unit) // BLOCK)
    return pl.pallas_call(
        pick_rows_kernel,
        out_shape=jax.ShapeDtypeStruct((blocks * BLOCK, width), jnp.bfloat16),
        grid_spec=pltpu.PrefetchScalarGridSpec(
            num_scalar_prefetch=1,
            grid=(blocks,),
            in_specs=[
                pl.BlockSpec(
                    (BLOCK, width), lambda i, places: (places[2, jnp.minimum(i, count - 1)], 0)
                )
            ],
            out_specs=pl.BlockSpec((BLOCK, width), lambda i, places: (i, 0)),
        ),
    )(places, weight)


def project_kernel(scale, places_ref, calib_ref, weight_ref, y_ref, sel_ref):
    step = pl.program_id(0)
    count = places_ref.shape[1]
    tokens = calib_ref.shape[0]
    tile = weight_ref.shape[0]
    part = y_ref.shape[2]

    @pl.when(step == 0)
    def _():
        sel_ref[...] = jnp.zeros(sel_ref.shape, sel_ref.dtype)

    value = lax.dot_general(
        calib_ref[...],
        weight_ref[...],
        (((1,), (1,)), ((), ())),
        preferred_element_type=jnp.float32,
    )
    value = (value * scale).astype(jnp.bfloat16)
    for s in range(tile // part):
        y_ref[s] = value[:, s * part : (s + 1) * part]
    for i in range(count):
        for s in range(tile // BLOCK):
            here = step * (tile // BLOCK) + s

            @pl.when((places_ref[3, i] != 0) & (places_ref[2, i] == here))
            def _():
                sel_ref[i * tokens : (i + 1) * tokens, :] = value[:, s * BLOCK : (s + 1) * BLOCK]


def project(places, calib, weight, scale):
    count = places.shape[1]
    tokens, width = calib.shape
    rows = weight.shape[0]
    mp_parts = lax.axis_size("mp")
    part = rows // mp_parts
    tile = max(part, BLOCK)
    sel_rows = padded(count * tokens)
    return pl.pallas_call(
        functools.partial(project_kernel, scale),
        out_shape=(
            jax.ShapeDtypeStruct((mp_parts, tokens, part), jnp.bfloat16),
            jax.ShapeDtypeStruct((sel_rows, BLOCK), jnp.bfloat16),
        ),
        grid_spec=pltpu.PrefetchScalarGridSpec(
            num_scalar_prefetch=1,
            grid=(rows // tile,),
            in_specs=[
                pl.BlockSpec((tokens, width), lambda i, places: (0, 0)),
                pl.BlockSpec((tile, width), lambda i, places: (i, 0)),
            ],
            out_specs=(
                pl.BlockSpec((tile // part, tokens, part), lambda i, places: (i, 0, 0)),
                pl.BlockSpec((sel_rows, BLOCK), lambda i, places: (0, 0)),
            ),
        ),
        compiler_params=pltpu.CompilerParams(vmem_limit_bytes=32 * MIB),
    )(places, calib, weight)


def invert(low_ref, out_ref, neg_ref, rhs_ref, pivot_ref, steps):
    count = out_ref.shape[0] // BLOCK
    at = 0
    for i in range(count):
        for j in range(i + 1):
            block = low_ref[at : at + BLOCK, :]
            at += BLOCK
            out_ref[i * BLOCK : (i + 1) * BLOCK, j * BLOCK : (j + 1) * BLOCK] = block
            if j < i:
                out_ref[j * BLOCK : (j + 1) * BLOCK, i * BLOCK : (i + 1) * BLOCK] = block.T

    def tick(k, at):
        for s in range(at, min(TICKS * count, len(steps)), TICKS):
            pl.when(TICKS * k + at == s)(steps[s])

    def stage(k, carry):
        tick(k, 0)
        here = pl.ds(pl.multiple_of(k * BLOCK, BLOCK), BLOCK)
        diag = out_ref[here, here]
        tiles = [diag[t * SUB : (t + 1) * SUB, :] for t in range(BLOCK // SUB)]
        tiles = sweep_block(tiles, lambda: tick(k, 1))
        for t in range(BLOCK // SUB):
            neg_ref[t * SUB : (t + 1) * SUB, :] = tiles[t]
        tick(k, 2)
        neg = neg_ref[...]
        r1, r2, r3 = split3(out_ref[here, :])
        a1, a2, a3 = split3(-neg)
        pivot_ref[...] = jnp.dot(
            jnp.concatenate([a1, a1, a2, a2, a1, a3], axis=1),
            jnp.concatenate([r1, r2, r1, r2, r3, r1], axis=0),
            preferred_element_type=jnp.float32,
        )
        pivot_ref[:, here] = neg
        b1, b2, b3 = split3(pivot_ref[...])
        for slot, part in enumerate((b1, b2, b1, b2, b3, b1)):
            rhs_ref[slot * BLOCK : (slot + 1) * BLOCK, :] = part

        def update(i, inner):
            rows = pl.ds(pl.multiple_of(i * BLOCK, BLOCK), BLOCK)
            c1, c2, c3 = split3(out_ref[rows, here])
            out_ref[rows, here] = jnp.zeros((BLOCK, BLOCK), jnp.float32)
            out_ref[rows, :] -= jnp.dot(
                jnp.concatenate([c1, c1, c2, c2, c1, c3], axis=1),
                rhs_ref[...],
                preferred_element_type=jnp.float32,
            )
            return inner

        lax.fori_loop(0, count // 2, update, 0)
        tick(k, 3)
        lax.fori_loop(count // 2, count, update, 0)
        out_ref[here, :] = pivot_ref[...]
        return carry

    lax.fori_loop(0, count, stage, 0)
    for s in range(TICKS * count, len(steps)):
        steps[s]()


def outputs_from(square_ref, columns_ref, y_ref, sel_ref, keep_ref, total_ref, factor_ref, out_ref):
    count = square_ref.shape[0] // BLOCK
    tokens = y_ref.shape[0]
    total_ref[...] = jnp.zeros(total_ref.shape, jnp.float32)

    def body(k, carry):
        here = pl.ds(pl.multiple_of(k * BLOCK, BLOCK), BLOCK)
        c1, c2, c3 = split3(columns_ref[:, here])
        n1, n2, n3 = split3(square_ref[here, :])
        total_ref[...] -= jnp.dot(
            jnp.concatenate([c1, c1, c2, c2, c1, c3], axis=1),
            jnp.concatenate([n1, n2, n1, n2, n3, n1], axis=0),
            preferred_element_type=jnp.float32,
        )
        return carry

    lax.fori_loop(0, count, body, 0)
    factor_ref[...] = total_ref[...].astype(jnp.bfloat16)
    selected = jnp.concatenate(
        [sel_ref[i * tokens : (i + 1) * tokens, :] for i in range(count)], axis=1
    )
    update = lax.dot_general(
        selected, factor_ref[...], (((1,), (1,)), ((), ())), preferred_element_type=jnp.float32
    )
    value = jnp.where(keep_ref[...] != 0.0, y_ref[...] - update, 0.0)
    out_ref[...] = value.astype(jnp.bfloat16)


def solve_kernel(
    low_ref, columns_ref, y_ref, sel_ref, keep_ref, kept_ref,
    factor_ref, out_ref, all_kept_ref,
    square_ref, neg_ref, rhs_ref, pivot_ref, total_ref,
    own_columns_ref, c_acc, c_recv, own_ref, y_acc, y_recv, all_ref, acc_ref, recv_ref,
    k_acc, k_recv, send_sem, recv_sem,
):
    greet(everyone())
    links = Links(send_sem, recv_sem)
    sum_steps = joined(
        reduce_lists(links, sel_ref, acc_ref, recv_ref, all_ref),
        steps_of(scatter_steps(links, y_ref, y_acc, y_recv, own_ref)),
    )
    lanes = kept_ref.shape[1] // 4
    rings = []
    for at in range(4):
        stages = ring_sum_stages(
            links,
            kept_ref,
            k_recv.at[at],
            k_acc.at[at],
            all_kept_ref,
            1 - 2 * (at % 2),
            slice(at * lanes, (at + 1) * lanes),
        )
        rings.append([lambda: None] * (at // 2) + spread(steps_of(stages), 2))
    steps = joined(
        *rings,
        spread(sum_steps, TICKS),
        spread(steps_of(scatter_steps(links, columns_ref, c_acc, c_recv, own_columns_ref)), 3 * TICKS),
    )
    invert(low_ref, square_ref, neg_ref, rhs_ref, pivot_ref, steps)
    outputs_from(
        square_ref, own_columns_ref, own_ref, all_ref, keep_ref, total_ref, factor_ref, out_ref
    )


def solve(low, columns, y, selected, keep, kept):
    row_parts, mp_parts = lax.axis_size("rows"), lax.axis_size("mp")
    copies = reduce_count() + 2 * bits_of(mp_parts)
    copies += 8 * (row_parts - 1)
    chunk = (row_parts - 1, kept.shape[0] // row_parts, kept.shape[1] // 4)
    _, part, order = columns.shape
    tokens = y.shape[1]
    return pl.pallas_call(
        solve_kernel,
        out_shape=(
            jax.ShapeDtypeStruct((part, order), jnp.bfloat16),
            jax.ShapeDtypeStruct((tokens, part), jnp.bfloat16),
            jax.ShapeDtypeStruct(kept.shape, kept.dtype),
        ),
        in_specs=[VMEM] * 6,
        out_specs=(VMEM, VMEM, VMEM),
        scratch_shapes=[
            pltpu.VMEM((order, order), jnp.float32),
            pltpu.VMEM((BLOCK, BLOCK), jnp.float32),
            pltpu.VMEM((6 * BLOCK, order), jnp.bfloat16),
            pltpu.VMEM((BLOCK, order), jnp.float32),
            pltpu.VMEM((part, order), jnp.float32),
            pltpu.VMEM((part, order), jnp.float32),
            pltpu.VMEM(columns.shape, jnp.float32),
            pltpu.VMEM((mp_parts - 1, part, order), jnp.float32),
            pltpu.VMEM((tokens, part), jnp.float32),
            pltpu.VMEM(y.shape, y.dtype),
            pltpu.VMEM((mp_parts - 1, tokens, part), y.dtype),
            pltpu.VMEM(selected.shape, selected.dtype),
            pltpu.VMEM(selected.shape, selected.dtype),
            pltpu.VMEM((reduce_sizes(selected.shape[0]), BLOCK), selected.dtype),
            pltpu.VMEM((4,) + chunk, kept.dtype),
            pltpu.VMEM((4,) + chunk, kept.dtype),
            pltpu.SemaphoreType.DMA((copies,)),
            pltpu.SemaphoreType.DMA((copies,)),
        ],
        compiler_params=pltpu.CompilerParams(
            collective_id=2, has_side_effects=True, vmem_limit_bytes=48 * MIB
        ),
        cost_estimate=pl.CostEstimate(
            flops=60_000_000_000, bytes_accessed=2 * order * order * 4, transcendentals=0
        ),
    )(low, columns, y, selected, keep, kept)


def moved_to(r, m, row_parts, mp_parts):
    per = row_parts // mp_parts
    return ((m + 1) % mp_parts) * per + r % per, r // per


def right_orders(row_parts):
    count = bits_of(row_parts)
    first = list(range(count))
    second = [1, 0] + first[2:] if count > 1 else first
    return first, second


def exchange_kernel(out_ref, factor_ref, left_ref, right_ref, all_factor_ref, send_sem, recv_sem):
    row_parts, mp_parts = lax.axis_size("rows"), lax.axis_size("mp")
    r, m = lax.axis_index("rows"), lax.axis_index("mp")
    per = row_parts // mp_parts
    tokens = out_ref.shape[0]
    to_row, to_mp = moved_to(r, m, row_parts, mp_parts)
    from_row = m * per + r % per
    from_mp = lax.rem(r // per + mp_parts - 1, mp_parts)
    devices = [{"mp": flip(m, k)} for k in range(bits_of(mp_parts))]
    devices += [{"rows": flip(r, k)} for k in range(bits_of(row_parts))]
    target = {"rows": to_row, "mp": to_mp}
    devices += [target, {"rows": from_row, "mp": from_mp}]
    greet(devices)
    links = Links(send_sem, recv_sem)
    mine = reversed_bits(m, mp_parts)

    orders = right_orders(row_parts)
    lists = []
    for h, order in enumerate(orders):
        half = tokens // 2
        slot = ordered_bits(to_row, order)
        copy = links.copy(
            out_ref.at[pl.ds(h * half, half)], right_ref.at[h, slot], target
        )
        stages = [([copy], None)]
        base, size = ordered_bits(r, order), 1
        for k in reversed(order):
            region = right_ref.at[h, pl.ds(base, size)]
            stages.append(([links.copy(region, region, {"rows": flip(r, k)})], None))
            base = base - ((base // size) % 2) * size
            size *= 2
        lists.append(steps_of(stages))
    for src, dst in ((out_ref, left_ref), (factor_ref, all_factor_ref)):
        stages = []
        base, size = mine, 1
        for k in reversed(range(bits_of(mp_parts))):
            region = dst.at[pl.ds(base, size)]
            source = src if size == 1 else region
            sink = dst.at[base] if size == 1 else region
            stages.append(([links.copy(source, sink, {"mp": flip(m, k)})], None))
            base = base - ((base // size) % 2) * size
            size *= 2
        lists.append(steps_of(stages))
    left_ref[mine] = out_ref[...]
    all_factor_ref[mine] = factor_ref[...]
    run_steps(*lists)


def exchange(outputs, factor):
    row_parts, mp_parts = lax.axis_size("rows"), lax.axis_size("mp")
    tokens, part = outputs.shape
    order = factor.shape[1]
    count = 2 * (1 + bits_of(row_parts)) + 2 * bits_of(mp_parts)
    return pl.pallas_call(
        exchange_kernel,
        out_shape=(
            jax.ShapeDtypeStruct((mp_parts, tokens, part), jnp.bfloat16),
            jax.ShapeDtypeStruct((2, row_parts, tokens // 2, part), jnp.bfloat16),
            jax.ShapeDtypeStruct((mp_parts, part, order), jnp.bfloat16),
        ),
        in_specs=[VMEM, VMEM],
        out_specs=(VMEM, VMEM, VMEM),
        scratch_shapes=[
            pltpu.SemaphoreType.DMA((count,)),
            pltpu.SemaphoreType.DMA((count,)),
        ],
        compiler_params=pltpu.CompilerParams(
            collective_id=3, has_side_effects=True, vmem_limit_bytes=32 * MIB
        ),
    )(outputs, factor)


def gram_kernel(row_parts, mp_parts, left_ref, right_ref, out_ref):
    per = row_parts // mp_parts
    tokens, part = left_ref.shape[1:]
    first, second = right_orders(row_parts)
    left = left_ref[0]
    for at in range(row_parts):
        source_mp = (at // per - 1) % mp_parts
        column = (at % per) * mp_parts + reversed_bits(source_mp, mp_parts)
        right = jnp.concatenate(
            [right_ref[0, ordered_bits(at, first)], right_ref[1, ordered_bits(at, second)]], axis=0
        )
        value = lax.dot_general(
            left, right, (((0,), (0,)), ((), ())), preferred_element_type=jnp.float32
        )
        out_ref[:, column * part : (column + 1) * part] = value / tokens


def gram_of(left, right):
    mp_parts, tokens, part = left.shape
    row_parts = right.shape[1]
    width = row_parts * part
    return pl.pallas_call(
        functools.partial(gram_kernel, row_parts, mp_parts),
        grid=(mp_parts,),
        in_specs=[pl.BlockSpec((1, tokens, part), lambda i: (i, 0, 0)), VMEM],
        out_specs=pl.BlockSpec((part, width), lambda i: (i, 0)),
        out_shape=jax.ShapeDtypeStruct((mp_parts * part, width), jnp.float32),
        compiler_params=pltpu.CompilerParams(vmem_limit_bytes=32 * MIB),
    )(left, right)


def prune_kernel(flags_ref, weight_ref, factor_ref, kept_ref, out_ref):
    step = pl.program_id(0)
    tile, width = weight_ref.shape
    chunk = min(width, 512)
    for c in range(width // chunk):
        lanes = slice(c * chunk, (c + 1) * chunk)
        update = jnp.dot(factor_ref[...], kept_ref[:, lanes], preferred_element_type=jnp.float32)
        value = weight_ref[:, lanes].astype(jnp.float32) - update
        for s in range(tile // BLOCK):
            gone = flags_ref[step * (tile // BLOCK) + s] != 0
            rows = slice(s * BLOCK, (s + 1) * BLOCK)
            out_ref[rows, lanes] = jnp.where(gone, 0.0, value[rows, :]).astype(jnp.bfloat16)


def prune(flags, weight, factor, kept_rows):
    rows, width = weight.shape
    order = factor.shape[1]
    tile = min(rows, 256)
    return pl.pallas_call(
        prune_kernel,
        out_shape=jax.ShapeDtypeStruct((rows, width), jnp.bfloat16),
        grid_spec=pltpu.PrefetchScalarGridSpec(
            num_scalar_prefetch=1,
            grid=(rows // tile,),
            in_specs=[
                pl.BlockSpec((tile, width), lambda i, flags: (i, 0)),
                pl.BlockSpec((tile, order), lambda i, flags: (i, 0)),
                pl.BlockSpec((order, width), lambda i, flags: (0, 0)),
            ],
            out_specs=pl.BlockSpec((tile, width), lambda i, flags: (i, 0)),
        ),
        compiler_params=pltpu.CompilerParams(vmem_limit_bytes=32 * MIB),
    )(flags, weight, factor, kept_rows)


def shards(calib, weight, inverse_factor, pruned_blocks):
    rows_dev, width_dev = weight.shape
    mp_parts = lax.axis_size("mp")
    full_width = width_dev * mp_parts
    part = rows_dev // mp_parts
    m = lax.axis_index("mp")
    row_start = lax.axis_index("rows") * rows_dev
    col_start = m * width_dev
    starts = pruned_blocks * BLOCK
    col_offsets = starts - col_start
    row_offsets = starts - row_start
    places = jnp.stack(
        [
            jnp.clip(col_offsets, 0, width_dev - BLOCK) // BLOCK,
            ((col_offsets >= 0) & (col_offsets < width_dev)).astype(jnp.int32),
            jnp.clip(row_offsets, 0, rows_dev - BLOCK) // BLOCK,
            ((row_offsets >= 0) & (row_offsets < rows_dev)).astype(jnp.int32),
        ]
    ).astype(jnp.int32)
    block_ids = row_start // BLOCK + jnp.arange(rows_dev // BLOCK, dtype=jnp.int32)
    flags = jnp.any(block_ids[:, None] == pruned_blocks[None, :], axis=1).astype(jnp.int32)
    own_start = row_start + reversed_bits(m, mp_parts) * part
    own_ids = (own_start + jnp.arange(part, dtype=jnp.int32)) // BLOCK
    keep = 1.0 - jnp.any(own_ids[:, None] == pruned_blocks[None, :], axis=1).astype(jnp.float32)

    own_kept = pick_rows(places, weight)
    columns, own_low = pick_columns(places, inverse_factor)
    columns = columns.reshape(mp_parts, part, columns.shape[1])
    low, all_calib = gather(own_low, calib)
    y, own_selected = project(places, all_calib, weight, float(full_width) ** (-0.5))
    factor, outputs, kept_rows = solve(low, columns, y, own_selected, keep[None, :], own_kept)
    left, right, all_factor = exchange(outputs, factor)
    gram_block = gram_of(left, right)
    pruned_weight = prune(
        flags, weight, all_factor.reshape(rows_dev, factor.shape[1]), kept_rows
    )
    return (pruned_weight, gram_block)


def solution(mesh):
    return jax.shard_map(
        shards,
        mesh=mesh,
        in_specs=(P("rows", "mp"), P("rows", "mp"), P("rows", "mp"), P()),
        out_specs=(P("rows", "mp"), P("rows", "mp")),
        check_vma=False,
    )
```

```python
import functools
import math

import jax
import jax.numpy as jnp
from jax import lax
from jax.experimental import pallas as pl
from jax.experimental.pallas import tpu as pltpu
from jax.sharding import PartitionSpec as P

BLOCK = 128
SUB = 8
GROUP = 4
TICKS = 4
RING_GAP = 2
MIB = 1024 * 1024
VMEM = pl.BlockSpec(memory_space=pltpu.VMEM)
SMEM = pl.BlockSpec(memory_space=pltpu.SMEM)


def split3(value):
    first = value.astype(jnp.bfloat16)
    rest = value - first.astype(jnp.float32)
    second = rest.astype(jnp.bfloat16)
    third = (rest - second.astype(jnp.float32)).astype(jnp.bfloat16)
    return first, second, third


def sweep_block(tiles, between):
    lane = lax.broadcasted_iota(jnp.int32, (SUB, BLOCK), 1)
    sublane = lax.broadcasted_iota(jnp.int32, (SUB, BLOCK), 0)
    wide = (SUB, BLOCK)
    for p in range(0, BLOCK, GROUP):
        if p == BLOCK // 2:
            between()
        own, s = p // SUB, p % SUB
        rows = [
            jnp.broadcast_to(tiles[own][s + a : s + a + 1, :], wide) for a in range(GROUP)
        ]
        small = {}
        for a in range(GROUP):
            for b in range(a, GROUP):
                small[a, b] = jnp.broadcast_to(rows[a][:, p + b : p + b + 1], wide)
        for k in range(GROUP):
            inv = 1.0 / small[k, k]
            old = {a: small[min(a, k), max(a, k)] for a in range(GROUP) if a != k}
            scaled = {a: value * inv for a, value in old.items()}
            for a in old:
                for b in old:
                    if a <= b:
                        small[a, b] = small[a, b] - old[a] * scaled[b]
                small[min(a, k), max(a, k)] = scaled[a]
            small[k, k] = -inv
        pivots = [lane == p + a for a in range(GROUP)]
        updates = []
        for a in range(GROUP):
            update = -small[0, a] * rows[0]
            for b in range(1, GROUP):
                update = update - small[min(a, b), max(a, b)] * rows[b]
            for b in range(GROUP):
                update = jnp.where(pivots[b], small[min(a, b), max(a, b)], update)
            updates.append(update)
        inside = (lane >= p) & (lane < p + GROUP)
        new = []
        for t in range(len(tiles)):
            value = jnp.where(inside, 0.0, tiles[t])
            for a in range(GROUP):
                column = jnp.broadcast_to(tiles[t][:, p + a : p + a + 1], wide)
                value = value - column * updates[a]
            if t == own:
                for a in range(GROUP):
                    value = jnp.where(sublane == s + a, updates[a], value)
            new.append(value)
        tiles = new
    return tiles


def bits_of(count):
    return count.bit_length() - 1


def flip(index, k):
    return index + (1 - 2 * ((index // 2**k) % 2)) * 2**k


def reversed_bits(index, count):
    value = 0
    for k in range(bits_of(count)):
        value = value * 2 + (index // 2**k) % 2
    return value


def ordered_bits(index, order):
    value = 0
    for k in order:
        value = value * 2 + (index // 2**k) % 2
    return value


def span(start, size, unit):
    return pl.ds(pl.multiple_of(start, unit), size)


class Links:
    def __init__(self, send_sem, recv_sem):
        self.send_sem = send_sem
        self.recv_sem = recv_sem
        self.used = 0

    def copy(self, src, dst, device):
        at = self.used
        self.used += 1
        return lambda: pltpu.make_async_remote_copy(
            src_ref=src,
            dst_ref=dst,
            send_sem=self.send_sem.at[at],
            recv_sem=self.recv_sem.at[at],
            device_id=device,
            device_id_type=pl.DeviceIdType.MESH,
        )


def room(*arrays):
    total = 0
    for shape, dtype in arrays:
        width = jnp.dtype(dtype).itemsize
        tile = SUB * 4 // width
        lanes = -(-shape[-1] // BLOCK) * BLOCK
        rows = -(-shape[-2] // tile) * tile
        total += math.prod(shape[:-2]) * rows * lanes * width
    return min(63 * MIB, total + total // 32 + MIB)


def described(arrays):
    return [(a.shape, a.dtype) for a in arrays]


def greet(devices):
    barrier = pltpu.get_barrier_semaphore()
    for device in devices:
        pl.semaphore_signal(
            barrier, inc=1, device_id=device, device_id_type=pl.DeviceIdType.MESH
        )
    pl.semaphore_wait(barrier, len(devices))


def everyone():
    row_parts, mp_parts = lax.axis_size("rows"), lax.axis_size("mp")
    r, m = lax.axis_index("rows"), lax.axis_index("mp")
    devices = [{"mp": flip(m, k)} for k in range(bits_of(mp_parts))]
    devices += [{"rows": lax.rem(r + d, row_parts)} for d in range(1, row_parts)]
    return devices


def reduce_plans(rows):
    pieces = lax.axis_size("rows") * lax.axis_size("mp")
    depth = bits_of(lax.axis_size("mp"))
    units = rows // (16 * pieces)
    first = max(1, min(units - 1, (2 * units + 1) // 3))
    order = [f"mp{k}" for k in range(depth)]
    plans = [(0, 16 * first, order + ["rows"])]
    if units > first:
        plans.append((16 * first * pieces, 16 * (units - first), order[:1] + ["rows"] + order[1:]))
    return plans


def reduce_sizes(rows):
    row_parts, mp_parts = lax.axis_size("rows"), lax.axis_size("mp")
    total = 0
    for _, piece, order in reduce_plans(rows):
        size = piece * row_parts * mp_parts
        for dim in order:
            parts = row_parts if dim == "rows" else 2
            total += size - size // parts
            size //= parts
    return total


def reduce_count():
    return 4 * (bits_of(lax.axis_size("mp")) + lax.axis_size("rows") - 1)


def reduce_lists(links, src, acc, recv, out):
    lists, off = [], 0
    for start, piece, order in reduce_plans(src.shape[0]):
        stages, off = reduce_stages(links, src, acc, recv, out, start, piece, order, off)
        lists.append(steps_of(stages))
    return joined(*lists)


def reduce_stages(links, src, acc, recv, out, start, piece, order, off):
    row_parts, mp_parts = lax.axis_size("rows"), lax.axis_size("mp")
    r, m = lax.axis_index("rows"), lax.axis_index("mp")
    stages, held = [], []
    base, size = start, piece * row_parts * mp_parts
    for at, dim in enumerate(order):
        parts = row_parts if dim == "rows" else 2
        k = None if dim == "rows" else int(dim[2:])
        size //= parts
        source = src if at == 0 else acc
        sink = out if at == len(order) - 1 else acc
        copies = []
        for d in range(1, parts):
            to = lax.rem(r + d, row_parts) if k is None else 1 - (m // 2**k) % 2
            device = {"rows": to} if k is None else {"mp": flip(m, k)}
            copies.append(
                links.copy(
                    source.at[span(base + to * size, size, 16)],
                    recv.at[pl.ds(off + (d - 1) * size, size)],
                    device,
                )
            )
        keep = base + (r if k is None else (m // 2**k) % 2) * size

        def merge(source=source, sink=sink, keep=keep, off=off, size=size, parts=parts):
            def body(t, carry):
                step = pl.multiple_of(t * piece, 16)
                value = source[span(keep + step, piece, 16), :].astype(jnp.float32)
                for d in range(1, parts):
                    landed = recv[span(off + (d - 1) * size + step, piece, 16), :]
                    value = value + landed.astype(jnp.float32)
                sink[span(keep + step, piece, 16), :] = value.astype(sink.dtype)
                return carry

            lax.fori_loop(0, size // piece, body, 0)

        stages.append((copies, merge))
        off += (parts - 1) * size
        base = keep
        held.append((dim, k, keep, size))
    for dim, k, keep, size in reversed(held):
        mine = out.at[span(keep, size, 16)]
        if k is None:
            devices = [{"rows": lax.rem(r + d, row_parts)} for d in range(1, row_parts)]
        else:
            devices = [{"mp": flip(m, k)}]
        stages.append(([links.copy(mine, mine, device) for device in devices], None))
    return stages, off


def steps_of(stages):
    steps = []
    for s in range(len(stages) + 1):

        def step(s=s):
            if s > 0:
                for copy in stages[s - 1][0]:
                    copy().wait()
                if stages[s - 1][1] is not None:
                    stages[s - 1][1]()
            if s < len(stages):
                for copy in stages[s][0]:
                    copy().start()

        steps.append(step)
    return steps


def joined(*lists):
    def step(s):
        for one in lists:
            if s < len(one):
                one[s]()

    return [functools.partial(step, s) for s in range(max(len(one) for one in lists))]


def placed(ticks, steps, start, gap):
    for at, step in enumerate(steps):
        if start + at * gap >= len(ticks):
            return steps[at:]
        ticks[start + at * gap].append(step)
    return []


def run_steps(*lists):
    for step in joined(*lists):
        step()


def ring_place(r):
    row_parts = lax.axis_size("rows")
    return (1 - r % 2) * (r // 2) + (r % 2) * (row_parts - 1 - r // 2)


def ring_member(place):
    row_parts = lax.axis_size("rows")
    place = lax.rem(place + 2 * row_parts, row_parts)
    second = (2 * place) // row_parts
    return (1 - second) * 2 * place + second * (2 * (row_parts - 1 - place) + 1)


def ring_devices():
    place = ring_place(lax.axis_index("rows"))
    return [{"rows": ring_member(place + 1)}, {"rows": ring_member(place - 1)}]


def ring_sum_stages(links, src, recv, out, sign, lanes):
    row_parts = lax.axis_size("rows")
    place = ring_place(lax.axis_index("rows"))
    to = {"rows": ring_member(place + sign)}
    size = src.shape[0] // row_parts

    def chunk(step):
        at = lax.rem(place - sign * step + 2 * row_parts, row_parts)
        return span(at * size, size, 16)

    stages = []
    for s in range(row_parts - 1):
        source = src.at[chunk(0), lanes] if s == 0 else recv.at[s - 1]
        last = s == row_parts - 2

        def merge(s=s, last=last, rows=chunk(s + 1)):
            value = src[rows, lanes] + recv[s]
            if last:
                out[rows, lanes] = value
            else:
                recv[s] = value

        stages.append(([links.copy(source, recv.at[s], to)], merge))
    for s in range(row_parts - 1):
        piece = out.at[chunk(s - 1), lanes]
        stages.append(([links.copy(piece, piece, to)], None))
    return stages


def ring_gather_stages(links, src, out, sign, hops):
    row_parts = lax.axis_size("rows")
    place = ring_place(lax.axis_index("rows"))
    to = {"rows": ring_member(place + sign)}
    size = src.shape[0]
    stages = []
    for s in range(hops):
        at = lax.rem(place - sign * s + 2 * row_parts, row_parts)
        piece = out.at[span(at * size, size, 16)]
        stages.append(([links.copy(src if s == 0 else piece, piece, to)], None))
    return stages


def gather_kernel(
    scale, places_ref, src_ref, calib_ref, weight_ref, out_ref, kept_ref, y_ref, sel_ref,
    all_calib_ref, weight_vmem, chosen_ref, y_vmem, acc_ref, recv_ref, weight_sem, send_sem, recv_sem,
):
    row_parts = lax.axis_size("rows")
    weight_copy = pltpu.make_async_copy(weight_ref, weight_vmem, weight_sem)
    weight_copy.start()
    greet(everyone())
    links = Links(send_sem, recv_sem)
    steps = reduce_lists(links, src_ref, acc_ref, recv_ref, out_ref)
    rings = joined(
        steps_of(ring_gather_stages(links, calib_ref, all_calib_ref, 1, row_parts // 2)),
        steps_of(ring_gather_stages(links, calib_ref, all_calib_ref, -1, row_parts // 2 - 1)),
    )
    steps[0]()
    rings[0]()
    place = ring_place(lax.axis_index("rows"))
    size = calib_ref.shape[0]
    all_calib_ref[span(place * size, size, 16), :] = calib_ref[...]
    weight_copy.wait()
    for i in range(places_ref.shape[1]):
        at = lax.broadcasted_iota(jnp.int32, (BLOCK, weight_vmem.shape[0]), 1)
        row = lax.broadcasted_iota(jnp.int32, (BLOCK, weight_vmem.shape[0]), 0)
        chosen = jnp.where(at == row + places_ref[4, i], 1.0, 0.0).astype(jnp.bfloat16)
        chosen_ref[i * BLOCK : (i + 1) * BLOCK, :] = chosen

    def pick(t, carry):
        rows = pl.ds(pl.multiple_of(t * BLOCK, BLOCK), BLOCK)
        value = jnp.dot(chosen_ref[rows, :], weight_vmem[...], preferred_element_type=jnp.float32)
        kept_ref[rows, :] = value.astype(kept_ref.dtype)
        return carry

    count = places_ref.shape[1]
    used = count * BLOCK
    if kept_ref.shape[0] > used:
        kept_ref[used:, :] = jnp.zeros((kept_ref.shape[0] - used, kept_ref.shape[1]), kept_ref.dtype)
    steps[1]()
    for at in range(max(len(steps) - 2, len(rings) - 1)):
        if at + 2 < len(steps):
            steps[at + 2]()
        if at + 1 < len(rings):
            rings[at + 1]()
        low_at, high_at = at * count // 4, (at + 1) * count // 4
        if high_at <= count:
            lax.fori_loop(low_at, high_at, pick, 0)
    project(scale, chosen_ref, all_calib_ref, weight_vmem, y_vmem, y_ref, sel_ref)


def project(scale, chosen_ref, calib_ref, weight_ref, all_ref, y_ref, sel_ref):
    mp_parts, tokens, part = y_ref.shape
    tile = max(part, BLOCK)

    def body(t, carry):
        rows = pl.ds(pl.multiple_of(t * tile, tile), tile)
        value = lax.dot_general(
            calib_ref[...],
            weight_ref[rows, :],
            (((1,), (1,)), ((), ())),
            preferred_element_type=jnp.float32,
        )
        value = (value * scale).astype(jnp.bfloat16)
        all_ref[:, rows] = value
        for s in range(tile // part):
            y_ref[t * (tile // part) + s] = value[:, s * part : (s + 1) * part]
        return carry

    lax.fori_loop(0, weight_ref.shape[0] // tile, body, 0)
    count = chosen_ref.shape[0] // BLOCK
    for i in range(count):
        value = lax.dot_general(
            all_ref[...],
            chosen_ref[i * BLOCK : (i + 1) * BLOCK, :],
            (((1,), (1,)), ((), ())),
            preferred_element_type=jnp.float32,
        )
        sel_ref[i * tokens : (i + 1) * tokens, :] = value.astype(sel_ref.dtype)
    used = count * tokens
    if sel_ref.shape[0] > used:
        sel_ref[used:, :] = jnp.zeros((sel_ref.shape[0] - used, BLOCK), sel_ref.dtype)


def gather(places, low, calib, weight, scale):
    row_parts, mp_parts = lax.axis_size("rows"), lax.axis_size("mp")
    tokens = calib.shape[0] * row_parts
    count = reduce_count() + row_parts - 1
    unit = 16 * row_parts
    kept = -(-places.shape[1] * BLOCK // unit) * unit
    outs = (
        jax.ShapeDtypeStruct(low.shape, low.dtype),
        jax.ShapeDtypeStruct((kept, weight.shape[1]), weight.dtype),
        jax.ShapeDtypeStruct((mp_parts, tokens, weight.shape[0] // mp_parts), weight.dtype),
        jax.ShapeDtypeStruct((padded(places.shape[1] * tokens), BLOCK), weight.dtype),
    )
    scratch = [
        ((tokens, calib.shape[1]), calib.dtype),
        (weight.shape, weight.dtype),
        ((places.shape[1] * BLOCK, weight.shape[0]), weight.dtype),
        ((tokens, weight.shape[0]), weight.dtype),
        (low.shape, low.dtype),
        ((reduce_sizes(low.shape[0]), BLOCK), low.dtype),
    ]
    return pl.pallas_call(
        functools.partial(gather_kernel, scale),
        out_shape=outs,
        in_specs=[SMEM, VMEM, VMEM, pl.BlockSpec(memory_space=pltpu.HBM)],
        out_specs=(VMEM, VMEM, VMEM, VMEM),
        scratch_shapes=[pltpu.VMEM(*one) for one in scratch]
        + [
            pltpu.SemaphoreType.DMA,
            pltpu.SemaphoreType.DMA((count,)),
            pltpu.SemaphoreType.DMA((count,)),
        ],
        compiler_params=pltpu.CompilerParams(
            collective_id=1,
            has_side_effects=True,
            vmem_limit_bytes=room(*described(outs), *described((low, calib)), *scratch),
        ),
    )(places, low, calib, weight)


def scatter_steps(links, src, acc, recv, out):
    m, mp_parts = lax.axis_index("mp"), lax.axis_size("mp")
    stages = []
    size, base, off = mp_parts, 0, 0
    depth = bits_of(mp_parts)
    for k in range(depth):
        size //= 2
        bit = (m // 2**k) % 2
        keep, send = base + bit * size, base + (1 - bit) * size
        source = src if k == 0 else acc
        copy = links.copy(
            source.at[pl.ds(send, size)], recv.at[pl.ds(off, size)], {"mp": flip(m, k)}
        )

        def merge(source=source, keep=keep, off=off, size=size, k=k):
            for t in range(size):
                a = source[keep + t].astype(jnp.float32)
                b = recv[off + t].astype(jnp.float32)
                if k == depth - 1:
                    out[...] = a + b
                else:
                    acc[keep + t] = (a + b).astype(acc.dtype)

        stages.append(([copy], merge))
        base, off = keep, off + size
    return stages


def pick_columns_kernel(places_ref, factor_ref, columns_ref, low_ref):
    j = pl.program_id(0)
    count = places_ref.shape[1]
    used = count * (count + 1) // 2 * BLOCK
    own = places_ref[1, j] != 0
    columns_ref[...] = jnp.where(own, factor_ref[...], 0.0)
    if low_ref.shape[0] > used:
        low_ref[used:, :] = jnp.zeros((low_ref.shape[0] - used, BLOCK), low_ref.dtype)
    for i in range(count):

        @pl.when(i >= j)
        def _():
            rows = pl.ds(pl.multiple_of(places_ref[2, i] * BLOCK, BLOCK), BLOCK)
            to = pl.ds(pl.multiple_of((i * (i + 1) // 2 + j) * BLOCK, BLOCK), BLOCK)
            both = (places_ref[3, i] != 0) & own
            low_ref[to, :] = jnp.where(both, factor_ref[rows, :], 0.0)


def padded(used):
    pieces = lax.axis_size("rows") * lax.axis_size("mp")
    return -(-used // (pieces * 16)) * pieces * 16


def pick_columns(places, factor):
    count = places.shape[1]
    rows = factor.shape[0]
    low_rows = padded(count * (count + 1) // 2 * BLOCK)
    return pl.pallas_call(
        pick_columns_kernel,
        out_shape=(
            jax.ShapeDtypeStruct((rows, count * BLOCK), jnp.float32),
            jax.ShapeDtypeStruct((low_rows, BLOCK), jnp.float32),
        ),
        grid_spec=pltpu.PrefetchScalarGridSpec(
            num_scalar_prefetch=1,
            grid=(count,),
            in_specs=[pl.BlockSpec((rows, BLOCK), lambda j, places: (0, places[0, j]))],
            out_specs=(
                pl.BlockSpec((rows, BLOCK), lambda j, places: (0, j)),
                pl.BlockSpec((low_rows, BLOCK), lambda j, places: (0, 0)),
            ),
        ),
    )(places, factor)


def invert(low_ref, out_ref, neg_ref, rhs_ref, pivot_ref, ticks):
    count = out_ref.shape[0] // BLOCK
    at = 0
    for i in range(count):
        for j in range(i + 1):
            block = low_ref[at : at + BLOCK, :]
            at += BLOCK
            out_ref[i * BLOCK : (i + 1) * BLOCK, j * BLOCK : (j + 1) * BLOCK] = block
            if j < i:
                out_ref[j * BLOCK : (j + 1) * BLOCK, i * BLOCK : (i + 1) * BLOCK] = block.T

    def tick(k, at):
        for s in range(at, len(ticks), TICKS):
            if ticks[s]:
                pl.when(TICKS * k + at == s)(lambda s=s: [step() for step in ticks[s]] and None)

    def stage(k, carry):
        tick(k, 0)
        here = pl.ds(pl.multiple_of(k * BLOCK, BLOCK), BLOCK)
        diag = out_ref[here, here]
        tiles = [diag[t * SUB : (t + 1) * SUB, :] for t in range(BLOCK // SUB)]
        tiles = sweep_block(tiles, lambda: tick(k, 1))
        for t in range(BLOCK // SUB):
            neg_ref[t * SUB : (t + 1) * SUB, :] = tiles[t]
        tick(k, 2)
        neg = neg_ref[...]
        r1, r2, r3 = split3(out_ref[here, :])
        a1, a2, a3 = split3(-neg)
        pivot_ref[...] = jnp.dot(
            jnp.concatenate([a1, a1, a2, a2, a1, a3], axis=1),
            jnp.concatenate([r1, r2, r1, r2, r3, r1], axis=0),
            preferred_element_type=jnp.float32,
        )
        pivot_ref[:, here] = neg
        b1, b2, b3 = split3(pivot_ref[...])
        for slot, part in enumerate((b1, b2, b1, b2, b3, b1)):
            rhs_ref[slot * BLOCK : (slot + 1) * BLOCK, :] = part

        def update(i, inner):
            rows = pl.ds(pl.multiple_of(i * BLOCK, BLOCK), BLOCK)
            c1, c2, c3 = split3(out_ref[rows, here])
            out_ref[rows, here] = jnp.zeros((BLOCK, BLOCK), jnp.float32)
            out_ref[rows, :] -= jnp.dot(
                jnp.concatenate([c1, c1, c2, c2, c1, c3], axis=1),
                rhs_ref[...],
                preferred_element_type=jnp.float32,
            )
            return inner

        lax.fori_loop(0, count // 2, update, 0)
        tick(k, 3)
        lax.fori_loop(count // 2, count, update, 0)
        out_ref[here, :] = pivot_ref[...]
        return carry

    lax.fori_loop(0, count, stage, 0)


def outputs_from(square_ref, columns_ref, y_ref, sel_ref, gone, total_ref, factor_ref, out_ref):
    count = square_ref.shape[0] // BLOCK
    tokens = y_ref.shape[0]
    total_ref[...] = jnp.zeros(total_ref.shape, jnp.float32)

    def body(k, carry):
        here = pl.ds(pl.multiple_of(k * BLOCK, BLOCK), BLOCK)
        c1, c2, c3 = split3(columns_ref[:, here])
        n1, n2, n3 = split3(square_ref[here, :])
        total_ref[...] -= jnp.dot(
            jnp.concatenate([c1, c1, c2, c2, c1, c3], axis=1),
            jnp.concatenate([n1, n2, n1, n2, n3, n1], axis=0),
            preferred_element_type=jnp.float32,
        )
        return carry

    lax.fori_loop(0, count, body, 0)
    factor_ref[...] = total_ref[...].astype(jnp.bfloat16)
    selected = jnp.concatenate(
        [sel_ref[i * tokens : (i + 1) * tokens, :] for i in range(count)], axis=1
    )
    update = lax.dot_general(
        selected, factor_ref[...], (((1,), (1,)), ((), ())), preferred_element_type=jnp.float32
    )
    value = jnp.where(gone == 0, y_ref[...] - update, 0.0)
    out_ref[...] = value.astype(jnp.bfloat16)


def moved_to(r, m, row_parts, mp_parts):
    per = row_parts // mp_parts
    return ((m + 1) % mp_parts) * per + r % per, r // per


def right_orders(row_parts):
    count = bits_of(row_parts)
    first = list(range(count))
    second = [1, 0] + first[2:] if count > 1 else first
    return first, second


def exchange_lists(links, out_ref, factor_ref, left_ref, right_ref, all_factor_ref):
    row_parts, mp_parts = lax.axis_size("rows"), lax.axis_size("mp")
    r, m = lax.axis_index("rows"), lax.axis_index("mp")
    tokens = out_ref.shape[0]
    to_row, to_mp = moved_to(r, m, row_parts, mp_parts)
    target = {"rows": to_row, "mp": to_mp}
    lists = []
    for h, order in enumerate(right_orders(row_parts)):
        half = tokens // 2
        slot = ordered_bits(to_row, order)
        copy = links.copy(out_ref.at[pl.ds(h * half, half)], right_ref.at[h, slot], target)
        stages = [([copy], None)]
        base, size = ordered_bits(r, order), 1
        for k in reversed(order):
            region = right_ref.at[h, pl.ds(base, size)]
            stages.append(([links.copy(region, region, {"rows": flip(r, k)})], None))
            base = base - ((base // size) % 2) * size
            size *= 2
        lists.append(steps_of(stages))
    for src, dst in ((out_ref, left_ref), (factor_ref, all_factor_ref)):
        stages = []
        base, size = reversed_bits(m, mp_parts), 1
        for k in reversed(range(bits_of(mp_parts))):
            region = dst.at[pl.ds(base, size)]
            source = src if size == 1 else region
            sink = dst.at[base] if size == 1 else region
            stages.append(([links.copy(source, sink, {"mp": flip(m, k)})], None))
            base = base - ((base // size) % 2) * size
            size *= 2
        lists.append(steps_of(stages))
    return lists


def solve_kernel(
    blocks_ref, low_ref, columns_ref, y_ref, sel_ref, kept_ref,
    left_ref, right_ref, all_factor_ref, all_kept_ref,
    factor_ref, out_ref, square_ref, neg_ref, rhs_ref, pivot_ref, total_ref,
    own_columns_ref, c_acc, c_recv, own_ref, y_acc, y_recv, all_ref, acc_ref, recv_ref,
    k_recv, send_sem, recv_sem,
):
    row_parts, mp_parts = lax.axis_size("rows"), lax.axis_size("mp")
    r, m = lax.axis_index("rows"), lax.axis_index("mp")
    to_row, to_mp = moved_to(r, m, row_parts, mp_parts)
    from_row = m * (row_parts // mp_parts) + r % (row_parts // mp_parts)
    from_mp = lax.rem(r // (row_parts // mp_parts) + mp_parts - 1, mp_parts)
    greet(everyone() + [{"rows": to_row, "mp": to_mp}, {"rows": from_row, "mp": from_mp}])
    links = Links(send_sem, recv_sem)
    ticks = [[] for _ in range(TICKS * (square_ref.shape[0] // BLOCK))]
    sum_steps = joined(
        reduce_lists(links, sel_ref, acc_ref, recv_ref, all_ref),
        steps_of(scatter_steps(links, y_ref, y_acc, y_recv, own_ref)),
    )
    column_steps = steps_of(scatter_steps(links, columns_ref, c_acc, c_recv, own_columns_ref))
    late = placed(ticks, sum_steps, 0, TICKS) + placed(ticks, column_steps, 0, 3 * TICKS)
    lanes = kept_ref.shape[1] // 4
    rings = []
    for at in range(4):
        stages = ring_sum_stages(
            links,
            kept_ref,
            k_recv.at[at],
            all_kept_ref,
            1 - 2 * (at % 2),
            slice(at * lanes, (at + 1) * lanes),
        )
        rings.append(placed(ticks, steps_of(stages), RING_GAP // 2 * (at // 2), RING_GAP))
    invert(low_ref, square_ref, neg_ref, rhs_ref, pivot_ref, ticks)
    for step in late:
        step()
    part = own_ref.shape[1]
    start = (r * mp_parts + reversed_bits(m, mp_parts)) * part
    feature = start + lax.broadcasted_iota(jnp.int32, (1, part), 1)
    gone = jnp.zeros((1, part), jnp.int32)
    for i in range(blocks_ref.shape[0]):
        first = blocks_ref[i] * BLOCK
        gone = jnp.where((feature >= first) & (feature < first + BLOCK), 1, gone)
    outputs_from(
        square_ref, own_columns_ref, own_ref, all_ref, gone, total_ref, factor_ref, out_ref
    )
    lists = exchange_lists(links, out_ref, factor_ref, left_ref, right_ref, all_factor_ref)
    steps = joined(*lists, *rings)
    steps[0]()
    mine = reversed_bits(m, mp_parts)
    left_ref[mine] = out_ref[...]
    all_factor_ref[mine] = factor_ref[...]
    for step in steps[1:]:
        step()


def solve(blocks, low, columns, y, selected, kept):
    row_parts, mp_parts = lax.axis_size("rows"), lax.axis_size("mp")
    copies = reduce_count() + 4 * bits_of(mp_parts) + 8 * (row_parts - 1)
    copies += 2 * (1 + bits_of(row_parts))
    chunk = (row_parts - 1, kept.shape[0] // row_parts, kept.shape[1] // 4)
    _, part, order = columns.shape
    tokens = y.shape[1]
    outs = (
        jax.ShapeDtypeStruct((mp_parts, tokens, part), jnp.bfloat16),
        jax.ShapeDtypeStruct((2, row_parts, tokens // 2, part), jnp.bfloat16),
        jax.ShapeDtypeStruct((mp_parts, part, order), jnp.bfloat16),
        jax.ShapeDtypeStruct(kept.shape, kept.dtype),
    )
    scratch = [
        ((part, order), jnp.bfloat16),
        ((tokens, part), jnp.bfloat16),
        ((order, order), jnp.float32),
        ((BLOCK, BLOCK), jnp.float32),
        ((6 * BLOCK, order), jnp.bfloat16),
        ((BLOCK, order), jnp.float32),
        ((part, order), jnp.float32),
        ((part, order), jnp.float32),
        (columns.shape, jnp.float32),
        ((mp_parts - 1, part, order), jnp.float32),
        ((tokens, part), jnp.float32),
        (y.shape, y.dtype),
        ((mp_parts - 1, tokens, part), y.dtype),
        (selected.shape, selected.dtype),
        (selected.shape, selected.dtype),
        ((reduce_sizes(selected.shape[0]), BLOCK), selected.dtype),
        ((4,) + chunk, kept.dtype),
    ]
    return pl.pallas_call(
        solve_kernel,
        out_shape=outs,
        in_specs=[SMEM] + [VMEM] * 5,
        out_specs=(VMEM, VMEM, VMEM, VMEM),
        scratch_shapes=[pltpu.VMEM(*one) for one in scratch]
        + [pltpu.SemaphoreType.DMA((copies,)), pltpu.SemaphoreType.DMA((copies,))],
        compiler_params=pltpu.CompilerParams(
            collective_id=2,
            has_side_effects=True,
            vmem_limit_bytes=room(*described(outs), *described((low, columns, y, selected, kept)), *scratch),
        ),
        cost_estimate=pl.CostEstimate(
            flops=60_000_000_000, bytes_accessed=2 * order * order * 4, transcendentals=0
        ),
    )(blocks, low, columns, y, selected, kept)


def gram_kernel(row_parts, mp_parts, left_ref, right_ref, out_ref):
    per = row_parts // mp_parts
    tokens, part = left_ref.shape[1:]
    first, second = right_orders(row_parts)
    left = left_ref[0]
    for at in range(row_parts):
        source_mp = (at // per - 1) % mp_parts
        column = (at % per) * mp_parts + reversed_bits(source_mp, mp_parts)
        right = jnp.concatenate(
            [right_ref[0, ordered_bits(at, first)], right_ref[1, ordered_bits(at, second)]], axis=0
        )
        value = lax.dot_general(
            left, right, (((0,), (0,)), ((), ())), preferred_element_type=jnp.float32
        )
        out_ref[:, column * part : (column + 1) * part] = value / tokens


def gram_of(left, right):
    mp_parts, tokens, part = left.shape
    row_parts = right.shape[1]
    width = row_parts * part
    return pl.pallas_call(
        functools.partial(gram_kernel, row_parts, mp_parts),
        grid=(mp_parts,),
        in_specs=[pl.BlockSpec((1, tokens, part), lambda i: (i, 0, 0)), VMEM],
        out_specs=pl.BlockSpec((part, width), lambda i: (i, 0)),
        out_shape=jax.ShapeDtypeStruct((mp_parts * part, width), jnp.float32),
        compiler_params=pltpu.CompilerParams(vmem_limit_bytes=32 * MIB),
    )(left, right)


def prune_kernel(blocks_ref, weight_ref, factor_ref, kept_ref, out_ref):
    step = pl.program_id(0)
    tile, width = weight_ref.shape
    row_block = lax.axis_index("rows") * pl.num_programs(0) * (tile // BLOCK)
    chunk = min(width, 512)
    for c in range(width // chunk):
        lanes = slice(c * chunk, (c + 1) * chunk)
        update = jnp.dot(factor_ref[...], kept_ref[:, lanes], preferred_element_type=jnp.float32)
        value = weight_ref[:, lanes].astype(jnp.float32) - update
        for s in range(tile // BLOCK):
            here = row_block + step * (tile // BLOCK) + s
            gone = blocks_ref[0] == here
            for i in range(1, blocks_ref.shape[0]):
                gone = gone | (blocks_ref[i] == here)
            rows = slice(s * BLOCK, (s + 1) * BLOCK)
            out_ref[rows, lanes] = jnp.where(gone, 0.0, value[rows, :]).astype(jnp.bfloat16)


def prune(blocks, weight, factor, kept_rows):
    rows, width = weight.shape
    order = factor.shape[1]
    tile = min(rows, 256)
    return pl.pallas_call(
        prune_kernel,
        out_shape=jax.ShapeDtypeStruct((rows, width), jnp.bfloat16),
        grid_spec=pltpu.PrefetchScalarGridSpec(
            num_scalar_prefetch=1,
            grid=(rows // tile,),
            in_specs=[
                pl.BlockSpec((tile, width), lambda i, blocks: (i, 0)),
                pl.BlockSpec((tile, order), lambda i, blocks: (i, 0)),
                pl.BlockSpec((order, width), lambda i, blocks: (0, 0)),
            ],
            out_specs=pl.BlockSpec((tile, width), lambda i, blocks: (i, 0)),
        ),
        compiler_params=pltpu.CompilerParams(vmem_limit_bytes=32 * MIB),
    )(blocks, weight, factor, kept_rows)


def shards(calib, weight, inverse_factor, pruned_blocks):
    rows_dev, width_dev = weight.shape
    mp_parts = lax.axis_size("mp")
    full_width = width_dev * mp_parts
    part = rows_dev // mp_parts
    m = lax.axis_index("mp")
    row_start = lax.axis_index("rows") * rows_dev
    col_start = m * width_dev
    starts = pruned_blocks * BLOCK
    col_offsets = starts - col_start
    row_offsets = starts - row_start
    places = jnp.stack(
        [
            jnp.clip(col_offsets, 0, width_dev - BLOCK) // BLOCK,
            ((col_offsets >= 0) & (col_offsets < width_dev)).astype(jnp.int32),
            jnp.clip(row_offsets, 0, rows_dev - BLOCK) // BLOCK,
            ((row_offsets >= 0) & (row_offsets < rows_dev)).astype(jnp.int32),
            row_offsets,
        ]
    ).astype(jnp.int32)
    columns, own_low = pick_columns(places, inverse_factor)
    columns = columns.reshape(mp_parts, part, columns.shape[1])
    low, own_kept, y, own_selected = gather(
        places, own_low, calib, weight, float(full_width) ** (-0.5)
    )
    left, right, all_factor, kept_rows = solve(
        pruned_blocks, low, columns, y, own_selected, own_kept
    )
    gram_block = gram_of(left, right)
    pruned_weight = prune(
        pruned_blocks, weight, all_factor.reshape(rows_dev, all_factor.shape[2]), kept_rows
    )
    return (pruned_weight, gram_block)


def solution(mesh):
    return jax.shard_map(
        shards,
        mesh=mesh,
        in_specs=(P("rows", "mp"), P("rows", "mp"), P("rows", "mp"), P()),
        out_specs=(P("rows", "mp"), P("rows", "mp")),
        check_vma=False,
    )
```

```python
import functools
import math

import jax
import jax.numpy as jnp
from jax import lax
from jax.experimental import pallas as pl
from jax.experimental.pallas import tpu as pltpu
from jax.sharding import PartitionSpec as P

BLOCK = 128
SUB = 8
GROUP = 4
TICKS = 4
RING_GAP = 2
MIB = 1024 * 1024
VMEM = pl.BlockSpec(memory_space=pltpu.VMEM)
SMEM = pl.BlockSpec(memory_space=pltpu.SMEM)


def split3(value):
    first = value.astype(jnp.bfloat16)
    rest = value - first.astype(jnp.float32)
    second = rest.astype(jnp.bfloat16)
    third = (rest - second.astype(jnp.float32)).astype(jnp.bfloat16)
    return first, second, third


def sweep_block(tiles, between):
    lane = lax.broadcasted_iota(jnp.int32, (SUB, BLOCK), 1)
    sublane = lax.broadcasted_iota(jnp.int32, (SUB, BLOCK), 0)
    wide = (SUB, BLOCK)
    for p in range(0, BLOCK, GROUP):
        if p == BLOCK // 2:
            between()
        own, s = p // SUB, p % SUB
        rows = [
            jnp.broadcast_to(tiles[own][s + a : s + a + 1, :], wide) for a in range(GROUP)
        ]
        small = {}
        for a in range(GROUP):
            for b in range(a, GROUP):
                small[a, b] = jnp.broadcast_to(rows[a][:, p + b : p + b + 1], wide)
        for k in range(GROUP):
            inv = 1.0 / small[k, k]
            old = {a: small[min(a, k), max(a, k)] for a in range(GROUP) if a != k}
            scaled = {a: value * inv for a, value in old.items()}
            for a in old:
                for b in old:
                    if a <= b:
                        small[a, b] = small[a, b] - old[a] * scaled[b]
                small[min(a, k), max(a, k)] = scaled[a]
            small[k, k] = -inv
        pivots = [lane == p + a for a in range(GROUP)]
        updates = []
        for a in range(GROUP):
            update = -small[0, a] * rows[0]
            for b in range(1, GROUP):
                update = update - small[min(a, b), max(a, b)] * rows[b]
            for b in range(GROUP):
                update = jnp.where(pivots[b], small[min(a, b), max(a, b)], update)
            updates.append(update)
        inside = (lane >= p) & (lane < p + GROUP)
        new = []
        for t in range(len(tiles)):
            value = jnp.where(inside, 0.0, tiles[t])
            for a in range(GROUP):
                column = jnp.broadcast_to(tiles[t][:, p + a : p + a + 1], wide)
                value = value - column * updates[a]
            if t == own:
                for a in range(GROUP):
                    value = jnp.where(sublane == s + a, updates[a], value)
            new.append(value)
        tiles = new
    return tiles


def bits_of(count):
    return count.bit_length() - 1


def flip(index, k):
    return index + (1 - 2 * ((index // 2**k) % 2)) * 2**k


def reversed_bits(index, count):
    value = 0
    for k in range(bits_of(count)):
        value = value * 2 + (index // 2**k) % 2
    return value


def ordered_bits(index, order):
    value = 0
    for k in order:
        value = value * 2 + (index // 2**k) % 2
    return value


def span(start, size, unit):
    return pl.ds(pl.multiple_of(start, unit), size)


class Links:
    def __init__(self, send_sem, recv_sem):
        self.send_sem = send_sem
        self.recv_sem = recv_sem
        self.used = 0

    def copy(self, src, dst, device):
        at = self.used
        self.used += 1
        return lambda: pltpu.make_async_remote_copy(
            src_ref=src,
            dst_ref=dst,
            send_sem=self.send_sem.at[at],
            recv_sem=self.recv_sem.at[at],
            device_id=device,
            device_id_type=pl.DeviceIdType.MESH,
        )


def room(*arrays):
    total = 0
    for shape, dtype in arrays:
        width = jnp.dtype(dtype).itemsize
        tile = SUB * 4 // width
        lanes = -(-shape[-1] // BLOCK) * BLOCK
        rows = -(-shape[-2] // tile) * tile
        total += math.prod(shape[:-2]) * rows * lanes * width
    return min(63 * MIB, total + total // 32 + MIB)


def solve_room(passed, held):
    whole = room(*passed, *held)
    return whole if whole > 56 * MIB else room(*held)


def described(arrays):
    return [(a.shape, a.dtype) for a in arrays]


def greet(devices):
    barrier = pltpu.get_barrier_semaphore()
    for device in devices:
        pl.semaphore_signal(
            barrier, inc=1, device_id=device, device_id_type=pl.DeviceIdType.MESH
        )
    pl.semaphore_wait(barrier, len(devices))


def everyone():
    row_parts, mp_parts = lax.axis_size("rows"), lax.axis_size("mp")
    r, m = lax.axis_index("rows"), lax.axis_index("mp")
    devices = [{"mp": flip(m, k)} for k in range(bits_of(mp_parts))]
    devices += [{"rows": lax.rem(r + d, row_parts)} for d in range(1, row_parts)]
    return devices


def reduce_plans(rows, split):
    pieces = lax.axis_size("rows") * lax.axis_size("mp")
    depth = bits_of(lax.axis_size("mp"))
    units = rows // (16 * pieces)
    first = max(1, min(units - 1, (2 * units + 1) // 3)) if split else units
    order = [f"mp{k}" for k in range(depth)]
    plans = [(0, 16 * first, order + ["rows"])]
    if units > first:
        plans.append((16 * first * pieces, 16 * (units - first), order[:1] + ["rows"] + order[1:]))
    return plans


def reduce_sizes(rows, split):
    row_parts, mp_parts = lax.axis_size("rows"), lax.axis_size("mp")
    total = 0
    for _, piece, order in reduce_plans(rows, split):
        size = piece * row_parts * mp_parts
        for dim in order:
            parts = row_parts if dim == "rows" else 2
            total += size - size // parts
            size //= parts
    return total


def reduce_count():
    return 4 * (bits_of(lax.axis_size("mp")) + lax.axis_size("rows") - 1)


def reduce_lists(links, src, acc, recv, out, split):
    lists, off = [], 0
    for start, piece, order in reduce_plans(src.shape[0], split):
        stages, off = reduce_stages(links, src, acc, recv, out, start, piece, order, off)
        lists.append(steps_of(stages))
    return joined(*lists)


def reduce_stages(links, src, acc, recv, out, start, piece, order, off):
    row_parts, mp_parts = lax.axis_size("rows"), lax.axis_size("mp")
    r, m = lax.axis_index("rows"), lax.axis_index("mp")
    stages, held = [], []
    base, size = start, piece * row_parts * mp_parts
    for at, dim in enumerate(order):
        parts = row_parts if dim == "rows" else 2
        k = None if dim == "rows" else int(dim[2:])
        size //= parts
        source = src if at == 0 else acc
        sink = out if at == len(order) - 1 else acc
        copies = []
        for d in range(1, parts):
            to = lax.rem(r + d, row_parts) if k is None else 1 - (m // 2**k) % 2
            device = {"rows": to} if k is None else {"mp": flip(m, k)}
            copies.append(
                links.copy(
                    source.at[span(base + to * size, size, 16)],
                    recv.at[pl.ds(off + (d - 1) * size, size)],
                    device,
                )
            )
        keep = base + (r if k is None else (m // 2**k) % 2) * size

        def merge(source=source, sink=sink, keep=keep, off=off, size=size, parts=parts):
            def body(t, carry):
                step = pl.multiple_of(t * piece, 16)
                value = source[span(keep + step, piece, 16), :].astype(jnp.float32)
                for d in range(1, parts):
                    landed = recv[span(off + (d - 1) * size + step, piece, 16), :]
                    value = value + landed.astype(jnp.float32)
                sink[span(keep + step, piece, 16), :] = value.astype(sink.dtype)
                return carry

            lax.fori_loop(0, size // piece, body, 0)

        stages.append((copies, merge))
        off += (parts - 1) * size
        base = keep
        held.append((dim, k, keep, size))
    for dim, k, keep, size in reversed(held):
        mine = out.at[span(keep, size, 16)]
        if k is None:
            devices = [{"rows": lax.rem(r + d, row_parts)} for d in range(1, row_parts)]
        else:
            devices = [{"mp": flip(m, k)}]
        stages.append(([links.copy(mine, mine, device) for device in devices], None))
    return stages, off


def steps_of(stages):
    steps = []
    for s in range(len(stages) + 1):

        def step(s=s):
            if s > 0:
                for copy in stages[s - 1][0]:
                    copy().wait()
                if stages[s - 1][1] is not None:
                    stages[s - 1][1]()
            if s < len(stages):
                for copy in stages[s][0]:
                    copy().start()

        steps.append(step)
    return steps


def joined(*lists):
    def step(s):
        for one in lists:
            if s < len(one):
                one[s]()

    return [functools.partial(step, s) for s in range(max(len(one) for one in lists))]


def placed(ticks, steps, start, gap):
    for at, step in enumerate(steps):
        if start + at * gap >= len(ticks):
            return steps[at:]
        ticks[start + at * gap].append(step)
    return []


def run_steps(*lists):
    for step in joined(*lists):
        step()


def ring_place(r):
    row_parts = lax.axis_size("rows")
    return (1 - r % 2) * (r // 2) + (r % 2) * (row_parts - 1 - r // 2)


def ring_member(place):
    row_parts = lax.axis_size("rows")
    place = lax.rem(place + 2 * row_parts, row_parts)
    second = (2 * place) // row_parts
    return (1 - second) * 2 * place + second * (2 * (row_parts - 1 - place) + 1)


def ring_devices():
    place = ring_place(lax.axis_index("rows"))
    return [{"rows": ring_member(place + 1)}, {"rows": ring_member(place - 1)}]


def ring_sum_stages(links, src, recv, out, sign, lanes):
    row_parts = lax.axis_size("rows")
    place = ring_place(lax.axis_index("rows"))
    to = {"rows": ring_member(place + sign)}
    size = src.shape[0] // row_parts

    def chunk(step):
        at = lax.rem(place - sign * step + 2 * row_parts, row_parts)
        return span(at * size, size, 16)

    stages = []
    for s in range(row_parts - 1):
        source = src.at[chunk(0), lanes] if s == 0 else recv.at[s - 1]
        last = s == row_parts - 2

        def merge(s=s, last=last, rows=chunk(s + 1)):
            value = src[rows, lanes] + recv[s]
            if last:
                out[rows, lanes] = value
            else:
                recv[s] = value

        stages.append(([links.copy(source, recv.at[s], to)], merge))
    for s in range(row_parts - 1):
        piece = out.at[chunk(s - 1), lanes]
        stages.append(([links.copy(piece, piece, to)], None))
    return stages


def ring_gather_stages(links, src, out, sign, hops):
    row_parts = lax.axis_size("rows")
    place = ring_place(lax.axis_index("rows"))
    to = {"rows": ring_member(place + sign)}
    size = src.shape[0]
    stages = []
    for s in range(hops):
        at = lax.rem(place - sign * s + 2 * row_parts, row_parts)
        piece = out.at[span(at * size, size, 16)]
        stages.append(([links.copy(src if s == 0 else piece, piece, to)], None))
    return stages


def gather_kernel(
    scale, places_ref, src_ref, calib_ref, weight_ref, out_ref, kept_ref, y_ref, sel_ref,
    all_calib_ref, weight_vmem, chosen_ref, y_vmem, acc_ref, recv_ref, weight_sem, send_sem, recv_sem,
):
    row_parts = lax.axis_size("rows")
    weight_copy = pltpu.make_async_copy(weight_ref, weight_vmem, weight_sem)
    weight_copy.start()
    greet(everyone())
    links = Links(send_sem, recv_sem)
    steps = reduce_lists(links, src_ref, acc_ref, recv_ref, out_ref, True)
    rings = joined(
        steps_of(ring_gather_stages(links, calib_ref, all_calib_ref, 1, row_parts // 2)),
        steps_of(ring_gather_stages(links, calib_ref, all_calib_ref, -1, row_parts // 2 - 1)),
    )
    steps[0]()
    rings[0]()
    place = ring_place(lax.axis_index("rows"))
    size = calib_ref.shape[0]
    all_calib_ref[span(place * size, size, 16), :] = calib_ref[...]
    weight_copy.wait()
    for i in range(places_ref.shape[1]):
        at = lax.broadcasted_iota(jnp.int32, (BLOCK, weight_vmem.shape[0]), 1)
        row = lax.broadcasted_iota(jnp.int32, (BLOCK, weight_vmem.shape[0]), 0)
        chosen = jnp.where(at == row + places_ref[4, i], 1.0, 0.0).astype(jnp.bfloat16)
        chosen_ref[i * BLOCK : (i + 1) * BLOCK, :] = chosen

    def pick(t, carry):
        rows = pl.ds(pl.multiple_of(t * BLOCK, BLOCK), BLOCK)
        value = jnp.dot(chosen_ref[rows, :], weight_vmem[...], preferred_element_type=jnp.float32)
        kept_ref[rows, :] = value.astype(kept_ref.dtype)
        return carry

    count = places_ref.shape[1]
    used = count * BLOCK
    if kept_ref.shape[0] > used:
        kept_ref[used:, :] = jnp.zeros((kept_ref.shape[0] - used, kept_ref.shape[1]), kept_ref.dtype)
    steps[1]()
    for at in range(max(len(steps) - 2, len(rings) - 1)):
        if at + 2 < len(steps):
            steps[at + 2]()
        if at + 1 < len(rings):
            rings[at + 1]()
        low_at, high_at = at * count // 4, (at + 1) * count // 4
        if high_at <= count:
            lax.fori_loop(low_at, high_at, pick, 0)
    project(scale, chosen_ref, all_calib_ref, weight_vmem, y_vmem, y_ref, sel_ref)


def project(scale, chosen_ref, calib_ref, weight_ref, all_ref, y_ref, sel_ref):
    mp_parts, tokens, part = y_ref.shape
    tile = max(part, BLOCK)

    def body(t, carry):
        rows = pl.ds(pl.multiple_of(t * tile, tile), tile)
        value = lax.dot_general(
            calib_ref[...],
            weight_ref[rows, :],
            (((1,), (1,)), ((), ())),
            preferred_element_type=jnp.float32,
        )
        value = (value * scale).astype(jnp.bfloat16)
        all_ref[:, rows] = value
        for s in range(tile // part):
            y_ref[t * (tile // part) + s] = value[:, s * part : (s + 1) * part]
        return carry

    lax.fori_loop(0, weight_ref.shape[0] // tile, body, 0)
    count = chosen_ref.shape[0] // BLOCK
    for i in range(count):
        value = lax.dot_general(
            all_ref[...],
            chosen_ref[i * BLOCK : (i + 1) * BLOCK, :],
            (((1,), (1,)), ((), ())),
            preferred_element_type=jnp.float32,
        )
        sel_ref[i * tokens : (i + 1) * tokens, :] = value.astype(sel_ref.dtype)
    used = count * tokens
    if sel_ref.shape[0] > used:
        sel_ref[used:, :] = jnp.zeros((sel_ref.shape[0] - used, BLOCK), sel_ref.dtype)


def gather(places, low, calib, weight, scale):
    row_parts, mp_parts = lax.axis_size("rows"), lax.axis_size("mp")
    tokens = calib.shape[0] * row_parts
    count = reduce_count() + row_parts - 1
    unit = 16 * row_parts
    kept = -(-places.shape[1] * BLOCK // unit) * unit
    outs = (
        jax.ShapeDtypeStruct(low.shape, low.dtype),
        jax.ShapeDtypeStruct((kept, weight.shape[1]), weight.dtype),
        jax.ShapeDtypeStruct((mp_parts, tokens, weight.shape[0] // mp_parts), weight.dtype),
        jax.ShapeDtypeStruct((padded(places.shape[1] * tokens), BLOCK), weight.dtype),
    )
    scratch = [
        ((tokens, calib.shape[1]), calib.dtype),
        (weight.shape, weight.dtype),
        ((places.shape[1] * BLOCK, weight.shape[0]), weight.dtype),
        ((tokens, weight.shape[0]), weight.dtype),
        (low.shape, low.dtype),
        ((reduce_sizes(low.shape[0], True), BLOCK), low.dtype),
    ]
    return pl.pallas_call(
        functools.partial(gather_kernel, scale),
        out_shape=outs,
        in_specs=[SMEM, VMEM, VMEM, pl.BlockSpec(memory_space=pltpu.HBM)],
        out_specs=(VMEM, VMEM, VMEM, VMEM),
        scratch_shapes=[pltpu.VMEM(*one) for one in scratch]
        + [
            pltpu.SemaphoreType.DMA,
            pltpu.SemaphoreType.DMA((count,)),
            pltpu.SemaphoreType.DMA((count,)),
        ],
        compiler_params=pltpu.CompilerParams(
            collective_id=1,
            has_side_effects=True,
            vmem_limit_bytes=room(*described(outs), *described((low, calib)), *scratch),
        ),
    )(places, low, calib, weight)


def scatter_steps(links, src, acc, recv, out):
    m, mp_parts = lax.axis_index("mp"), lax.axis_size("mp")
    stages = []
    size, base, off = mp_parts, 0, 0
    depth = bits_of(mp_parts)
    for k in range(depth):
        size //= 2
        bit = (m // 2**k) % 2
        keep, send = base + bit * size, base + (1 - bit) * size
        source = src if k == 0 else acc
        copy = links.copy(
            source.at[pl.ds(send, size)], recv.at[pl.ds(off, size)], {"mp": flip(m, k)}
        )

        def merge(source=source, keep=keep, off=off, size=size, k=k):
            for t in range(size):
                a = source[keep + t].astype(jnp.float32)
                b = recv[off + t].astype(jnp.float32)
                if k == depth - 1:
                    out[...] = a + b
                else:
                    acc[keep + t] = (a + b).astype(acc.dtype)

        stages.append(([copy], merge))
        base, off = keep, off + size
    return stages


def pick_columns_kernel(places_ref, factor_ref, columns_ref, low_ref):
    j = pl.program_id(0)
    count = places_ref.shape[1]
    used = count * (count + 1) // 2 * BLOCK
    own = places_ref[1, j] != 0
    columns_ref[...] = jnp.where(own, factor_ref[...], 0.0)
    if low_ref.shape[0] > used:
        low_ref[used:, :] = jnp.zeros((low_ref.shape[0] - used, BLOCK), low_ref.dtype)
    for i in range(count):

        @pl.when(i >= j)
        def _():
            rows = pl.ds(pl.multiple_of(places_ref[2, i] * BLOCK, BLOCK), BLOCK)
            to = pl.ds(pl.multiple_of((i * (i + 1) // 2 + j) * BLOCK, BLOCK), BLOCK)
            both = (places_ref[3, i] != 0) & own
            low_ref[to, :] = jnp.where(both, factor_ref[rows, :], 0.0)


def padded(used):
    pieces = lax.axis_size("rows") * lax.axis_size("mp")
    return -(-used // (pieces * 16)) * pieces * 16


def pick_columns(places, factor):
    count = places.shape[1]
    rows = factor.shape[0]
    low_rows = padded(count * (count + 1) // 2 * BLOCK)
    return pl.pallas_call(
        pick_columns_kernel,
        out_shape=(
            jax.ShapeDtypeStruct((rows, count * BLOCK), jnp.float32),
            jax.ShapeDtypeStruct((low_rows, BLOCK), jnp.float32),
        ),
        grid_spec=pltpu.PrefetchScalarGridSpec(
            num_scalar_prefetch=1,
            grid=(count,),
            in_specs=[pl.BlockSpec((rows, BLOCK), lambda j, places: (0, places[0, j]))],
            out_specs=(
                pl.BlockSpec((rows, BLOCK), lambda j, places: (0, j)),
                pl.BlockSpec((low_rows, BLOCK), lambda j, places: (0, 0)),
            ),
        ),
    )(places, factor)


def invert(low_ref, out_ref, neg_ref, rhs_ref, pivot_ref, ticks):
    count = out_ref.shape[0] // BLOCK
    at = 0
    for i in range(count):
        for j in range(i + 1):
            block = low_ref[at : at + BLOCK, :]
            at += BLOCK
            out_ref[i * BLOCK : (i + 1) * BLOCK, j * BLOCK : (j + 1) * BLOCK] = block
            if j < i:
                out_ref[j * BLOCK : (j + 1) * BLOCK, i * BLOCK : (i + 1) * BLOCK] = block.T

    def tick(k, at):
        for s in range(at, len(ticks), TICKS):
            if ticks[s]:
                pl.when(TICKS * k + at == s)(lambda s=s: [step() for step in ticks[s]] and None)

    def stage(k, carry):
        tick(k, 0)
        here = pl.ds(pl.multiple_of(k * BLOCK, BLOCK), BLOCK)
        diag = out_ref[here, here]
        tiles = [diag[t * SUB : (t + 1) * SUB, :] for t in range(BLOCK // SUB)]
        tiles = sweep_block(tiles, lambda: tick(k, 1))
        for t in range(BLOCK // SUB):
            neg_ref[t * SUB : (t + 1) * SUB, :] = tiles[t]
        tick(k, 2)
        neg = neg_ref[...]
        r1, r2, r3 = split3(out_ref[here, :])
        a1, a2, a3 = split3(-neg)
        pivot_ref[...] = jnp.dot(
            jnp.concatenate([a1, a1, a2, a2, a1, a3], axis=1),
            jnp.concatenate([r1, r2, r1, r2, r3, r1], axis=0),
            preferred_element_type=jnp.float32,
        )
        pivot_ref[:, here] = neg
        b1, b2, b3 = split3(pivot_ref[...])
        for slot, part in enumerate((b1, b2, b1, b2, b3, b1)):
            rhs_ref[slot * BLOCK : (slot + 1) * BLOCK, :] = part

        def update(i, inner):
            rows = pl.ds(pl.multiple_of(i * BLOCK, BLOCK), BLOCK)
            c1, c2, c3 = split3(out_ref[rows, here])
            out_ref[rows, here] = jnp.zeros((BLOCK, BLOCK), jnp.float32)
            out_ref[rows, :] -= jnp.dot(
                jnp.concatenate([c1, c1, c2, c2, c1, c3], axis=1),
                rhs_ref[...],
                preferred_element_type=jnp.float32,
            )
            return inner

        lax.fori_loop(0, count // 2, update, 0)
        tick(k, 3)
        lax.fori_loop(count // 2, count, update, 0)
        out_ref[here, :] = pivot_ref[...]
        return carry

    lax.fori_loop(0, count, stage, 0)


def outputs_from(square_ref, columns_ref, y_ref, sel_ref, gone, total_ref, factor_ref, out_ref):
    count = square_ref.shape[0] // BLOCK
    tokens = y_ref.shape[0]
    total_ref[...] = jnp.zeros(total_ref.shape, jnp.float32)

    def body(k, carry):
        here = pl.ds(pl.multiple_of(k * BLOCK, BLOCK), BLOCK)
        c1, c2, c3 = split3(columns_ref[:, here])
        n1, n2, n3 = split3(square_ref[here, :])
        total_ref[...] -= jnp.dot(
            jnp.concatenate([c1, c1, c2, c2, c1, c3], axis=1),
            jnp.concatenate([n1, n2, n1, n2, n3, n1], axis=0),
            preferred_element_type=jnp.float32,
        )
        return carry

    lax.fori_loop(0, count, body, 0)
    factor_ref[...] = total_ref[...].astype(jnp.bfloat16)
    selected = jnp.concatenate(
        [sel_ref[i * tokens : (i + 1) * tokens, :] for i in range(count)], axis=1
    )
    update = lax.dot_general(
        selected, factor_ref[...], (((1,), (1,)), ((), ())), preferred_element_type=jnp.float32
    )
    value = jnp.where(gone == 0, y_ref[...] - update, 0.0)
    out_ref[...] = value.astype(jnp.bfloat16)


def moved_to(r, m, row_parts, mp_parts):
    per = row_parts // mp_parts
    return ((m + 1) % mp_parts) * per + r % per, r // per


def right_orders(row_parts):
    count = bits_of(row_parts)
    first = list(range(count))
    second = [1, 0] + first[2:] if count > 1 else first
    return first, second


def exchange_lists(links, out_ref, factor_ref, left_ref, right_ref, all_factor_ref):
    row_parts, mp_parts = lax.axis_size("rows"), lax.axis_size("mp")
    r, m = lax.axis_index("rows"), lax.axis_index("mp")
    tokens = out_ref.shape[0]
    to_row, to_mp = moved_to(r, m, row_parts, mp_parts)
    target = {"rows": to_row, "mp": to_mp}
    lists = []
    for h, order in enumerate(right_orders(row_parts)):
        half = tokens // 2
        slot = ordered_bits(to_row, order)
        copy = links.copy(out_ref.at[pl.ds(h * half, half)], right_ref.at[h, slot], target)
        stages = [([copy], None)]
        base, size = ordered_bits(r, order), 1
        for k in reversed(order):
            region = right_ref.at[h, pl.ds(base, size)]
            stages.append(([links.copy(region, region, {"rows": flip(r, k)})], None))
            base = base - ((base // size) % 2) * size
            size *= 2
        lists.append(steps_of(stages))
    for src, dst in ((out_ref, left_ref), (factor_ref, all_factor_ref)):
        stages = []
        base, size = reversed_bits(m, mp_parts), 1
        for k in reversed(range(bits_of(mp_parts))):
            region = dst.at[pl.ds(base, size)]
            source = src if size == 1 else region
            sink = dst.at[base] if size == 1 else region
            stages.append(([links.copy(source, sink, {"mp": flip(m, k)})], None))
            base = base - ((base // size) % 2) * size
            size *= 2
        lists.append(steps_of(stages))
    return lists


def solve_kernel(
    blocks_ref, low_ref, columns_ref, y_ref, sel_ref, kept_ref,
    left_ref, right_ref, all_factor_ref, all_kept_ref,
    factor_ref, out_ref, square_ref, neg_ref, rhs_ref, pivot_ref, total_ref,
    own_columns_ref, c_acc, c_recv, own_ref, y_acc, y_recv, all_ref, acc_ref, recv_ref,
    k_recv, send_sem, recv_sem,
):
    row_parts, mp_parts = lax.axis_size("rows"), lax.axis_size("mp")
    r, m = lax.axis_index("rows"), lax.axis_index("mp")
    to_row, to_mp = moved_to(r, m, row_parts, mp_parts)
    from_row = m * (row_parts // mp_parts) + r % (row_parts // mp_parts)
    from_mp = lax.rem(r // (row_parts // mp_parts) + mp_parts - 1, mp_parts)
    greet(everyone() + [{"rows": to_row, "mp": to_mp}, {"rows": from_row, "mp": from_mp}])
    links = Links(send_sem, recv_sem)
    ticks = [[] for _ in range(TICKS * (square_ref.shape[0] // BLOCK))]
    sum_steps = joined(
        reduce_lists(links, sel_ref, acc_ref, recv_ref, all_ref, False),
        steps_of(scatter_steps(links, y_ref, y_acc, y_recv, own_ref)),
    )
    column_steps = steps_of(scatter_steps(links, columns_ref, c_acc, c_recv, own_columns_ref))
    late = placed(ticks, sum_steps, 0, TICKS) + placed(ticks, column_steps, 0, 3 * TICKS)
    lanes = kept_ref.shape[1] // 4
    rings = []
    for at in range(4):
        stages = ring_sum_stages(
            links,
            kept_ref,
            k_recv.at[at],
            all_kept_ref,
            1 - 2 * (at % 2),
            slice(at * lanes, (at + 1) * lanes),
        )
        rings.append(placed(ticks, steps_of(stages), RING_GAP // 2 * (at // 2), RING_GAP))
    invert(low_ref, square_ref, neg_ref, rhs_ref, pivot_ref, ticks)
    for step in late:
        step()
    part = own_ref.shape[1]
    start = (r * mp_parts + reversed_bits(m, mp_parts)) * part
    feature = start + lax.broadcasted_iota(jnp.int32, (1, part), 1)
    gone = jnp.zeros((1, part), jnp.int32)
    for i in range(blocks_ref.shape[0]):
        first = blocks_ref[i] * BLOCK
        gone = jnp.where((feature >= first) & (feature < first + BLOCK), 1, gone)
    outputs_from(
        square_ref, own_columns_ref, own_ref, all_ref, gone, total_ref, factor_ref, out_ref
    )
    lists = exchange_lists(links, out_ref, factor_ref, left_ref, right_ref, all_factor_ref)
    steps = joined(*lists, *rings)
    steps[0]()
    mine = reversed_bits(m, mp_parts)
    left_ref[mine] = out_ref[...]
    all_factor_ref[mine] = factor_ref[...]
    for step in steps[1:]:
        step()


def solve(blocks, low, columns, y, selected, kept):
    row_parts, mp_parts = lax.axis_size("rows"), lax.axis_size("mp")
    copies = reduce_count() + 4 * bits_of(mp_parts) + 8 * (row_parts - 1)
    copies += 2 * (1 + bits_of(row_parts))
    chunk = (row_parts - 1, kept.shape[0] // row_parts, kept.shape[1] // 4)
    _, part, order = columns.shape
    tokens = y.shape[1]
    outs = (
        jax.ShapeDtypeStruct((mp_parts, tokens, part), jnp.bfloat16),
        jax.ShapeDtypeStruct((2, row_parts, tokens // 2, part), jnp.bfloat16),
        jax.ShapeDtypeStruct((mp_parts, part, order), jnp.bfloat16),
        jax.ShapeDtypeStruct(kept.shape, kept.dtype),
    )
    scratch = [
        ((part, order), jnp.bfloat16),
        ((tokens, part), jnp.bfloat16),
        ((order, order), jnp.float32),
        ((BLOCK, BLOCK), jnp.float32),
        ((6 * BLOCK, order), jnp.bfloat16),
        ((BLOCK, order), jnp.float32),
        ((part, order), jnp.float32),
        ((part, order), jnp.float32),
        (columns.shape, jnp.float32),
        ((mp_parts - 1, part, order), jnp.float32),
        ((tokens, part), jnp.float32),
        (y.shape, y.dtype),
        ((mp_parts - 1, tokens, part), y.dtype),
        (selected.shape, selected.dtype),
        (selected.shape, selected.dtype),
        ((reduce_sizes(selected.shape[0], False), BLOCK), selected.dtype),
        ((4,) + chunk, kept.dtype),
    ]
    return pl.pallas_call(
        solve_kernel,
        out_shape=outs,
        in_specs=[SMEM] + [VMEM] * 5,
        out_specs=(VMEM, VMEM, VMEM, VMEM),
        scratch_shapes=[pltpu.VMEM(*one) for one in scratch]
        + [pltpu.SemaphoreType.DMA((copies,)), pltpu.SemaphoreType.DMA((copies,))],
        compiler_params=pltpu.CompilerParams(
            collective_id=2,
            has_side_effects=True,
            vmem_limit_bytes=solve_room(
                described(outs) + described((low, columns, y, selected)), described((kept,)) + scratch
            ),
        ),
        cost_estimate=pl.CostEstimate(
            flops=60_000_000_000, bytes_accessed=2 * order * order * 4, transcendentals=0
        ),
    )(blocks, low, columns, y, selected, kept)


def gram_kernel(row_parts, mp_parts, left_ref, right_ref, out_ref):
    per = row_parts // mp_parts
    tokens, part = left_ref.shape[1:]
    first, second = right_orders(row_parts)
    left = left_ref[0]
    for at in range(row_parts):
        source_mp = (at // per - 1) % mp_parts
        column = (at % per) * mp_parts + reversed_bits(source_mp, mp_parts)
        right = jnp.concatenate(
            [right_ref[0, ordered_bits(at, first)], right_ref[1, ordered_bits(at, second)]], axis=0
        )
        value = lax.dot_general(
            left, right, (((0,), (0,)), ((), ())), preferred_element_type=jnp.float32
        )
        out_ref[:, column * part : (column + 1) * part] = value / tokens


def gram_of(left, right):
    mp_parts, tokens, part = left.shape
    row_parts = right.shape[1]
    width = row_parts * part
    return pl.pallas_call(
        functools.partial(gram_kernel, row_parts, mp_parts),
        grid=(mp_parts,),
        in_specs=[pl.BlockSpec((1, tokens, part), lambda i: (i, 0, 0)), VMEM],
        out_specs=pl.BlockSpec((part, width), lambda i: (i, 0)),
        out_shape=jax.ShapeDtypeStruct((mp_parts * part, width), jnp.float32),
        compiler_params=pltpu.CompilerParams(vmem_limit_bytes=32 * MIB),
    )(left, right)


def prune_kernel(blocks_ref, weight_ref, factor_ref, kept_ref, out_ref):
    step = pl.program_id(0)
    tile, width = weight_ref.shape
    row_block = lax.axis_index("rows") * pl.num_programs(0) * (tile // BLOCK)
    chunk = min(width, 512)
    for c in range(width // chunk):
        lanes = slice(c * chunk, (c + 1) * chunk)
        update = jnp.dot(factor_ref[...], kept_ref[:, lanes], preferred_element_type=jnp.float32)
        value = weight_ref[:, lanes].astype(jnp.float32) - update
        for s in range(tile // BLOCK):
            here = row_block + step * (tile // BLOCK) + s
            gone = blocks_ref[0] == here
            for i in range(1, blocks_ref.shape[0]):
                gone = gone | (blocks_ref[i] == here)
            rows = slice(s * BLOCK, (s + 1) * BLOCK)
            out_ref[rows, lanes] = jnp.where(gone, 0.0, value[rows, :]).astype(jnp.bfloat16)


def prune(blocks, weight, factor, kept_rows):
    rows, width = weight.shape
    order = factor.shape[1]
    tile = min(rows, 256)
    return pl.pallas_call(
        prune_kernel,
        out_shape=jax.ShapeDtypeStruct((rows, width), jnp.bfloat16),
        grid_spec=pltpu.PrefetchScalarGridSpec(
            num_scalar_prefetch=1,
            grid=(rows // tile,),
            in_specs=[
                pl.BlockSpec((tile, width), lambda i, blocks: (i, 0)),
                pl.BlockSpec((tile, order), lambda i, blocks: (i, 0)),
                pl.BlockSpec((order, width), lambda i, blocks: (0, 0)),
            ],
            out_specs=pl.BlockSpec((tile, width), lambda i, blocks: (i, 0)),
        ),
        compiler_params=pltpu.CompilerParams(vmem_limit_bytes=32 * MIB),
    )(blocks, weight, factor, kept_rows)


def shards(calib, weight, inverse_factor, pruned_blocks):
    rows_dev, width_dev = weight.shape
    mp_parts = lax.axis_size("mp")
    full_width = width_dev * mp_parts
    part = rows_dev // mp_parts
    m = lax.axis_index("mp")
    row_start = lax.axis_index("rows") * rows_dev
    col_start = m * width_dev
    starts = pruned_blocks * BLOCK
    col_offsets = starts - col_start
    row_offsets = starts - row_start
    places = jnp.stack(
        [
            jnp.clip(col_offsets, 0, width_dev - BLOCK) // BLOCK,
            ((col_offsets >= 0) & (col_offsets < width_dev)).astype(jnp.int32),
            jnp.clip(row_offsets, 0, rows_dev - BLOCK) // BLOCK,
            ((row_offsets >= 0) & (row_offsets < rows_dev)).astype(jnp.int32),
            row_offsets,
        ]
    ).astype(jnp.int32)
    columns, own_low = pick_columns(places, inverse_factor)
    columns = columns.reshape(mp_parts, part, columns.shape[1])
    low, own_kept, y, own_selected = gather(
        places, own_low, calib, weight, float(full_width) ** (-0.5)
    )
    left, right, all_factor, kept_rows = solve(
        pruned_blocks, low, columns, y, own_selected, own_kept
    )
    gram_block = gram_of(left, right)
    pruned_weight = prune(
        pruned_blocks, weight, all_factor.reshape(rows_dev, all_factor.shape[2]), kept_rows
    )
    return (pruned_weight, gram_block)


def solution(mesh):
    return jax.shard_map(
        shards,
        mesh=mesh,
        in_specs=(P("rows", "mp"), P("rows", "mp"), P("rows", "mp"), P()),
        out_specs=(P("rows", "mp"), P("rows", "mp")),
        check_vma=False,
    )
```

```python
import functools
import math

import jax
import jax.numpy as jnp
from jax import lax
from jax.experimental import pallas as pl
from jax.experimental.pallas import tpu as pltpu
from jax.sharding import PartitionSpec as P

BLOCK = 128
SUB = 8
GROUP = 4
TICKS = 4
RING_GAP = 2
MIB = 1024 * 1024
VMEM = pl.BlockSpec(memory_space=pltpu.VMEM)
SMEM = pl.BlockSpec(memory_space=pltpu.SMEM)


def split3(value):
    first = value.astype(jnp.bfloat16)
    rest = value - first.astype(jnp.float32)
    second = rest.astype(jnp.bfloat16)
    third = (rest - second.astype(jnp.float32)).astype(jnp.bfloat16)
    return first, second, third


def sweep_block(tiles, between):
    lane = lax.broadcasted_iota(jnp.int32, (SUB, BLOCK), 1)
    sublane = lax.broadcasted_iota(jnp.int32, (SUB, BLOCK), 0)
    wide = (SUB, BLOCK)
    for p in range(0, BLOCK, GROUP):
        if p == BLOCK // 2:
            between()
        own, s = p // SUB, p % SUB
        rows = [
            jnp.broadcast_to(tiles[own][s + a : s + a + 1, :], wide) for a in range(GROUP)
        ]
        small = {}
        for a in range(GROUP):
            for b in range(a, GROUP):
                small[a, b] = jnp.broadcast_to(rows[a][:, p + b : p + b + 1], wide)
        for k in range(GROUP):
            inv = 1.0 / small[k, k]
            old = {a: small[min(a, k), max(a, k)] for a in range(GROUP) if a != k}
            scaled = {a: value * inv for a, value in old.items()}
            for a in old:
                for b in old:
                    if a <= b:
                        small[a, b] = small[a, b] - old[a] * scaled[b]
                small[min(a, k), max(a, k)] = scaled[a]
            small[k, k] = -inv
        pivots = [lane == p + a for a in range(GROUP)]
        updates = []
        for a in range(GROUP):
            update = -small[0, a] * rows[0]
            for b in range(1, GROUP):
                update = update - small[min(a, b), max(a, b)] * rows[b]
            for b in range(GROUP):
                update = jnp.where(pivots[b], small[min(a, b), max(a, b)], update)
            updates.append(update)
        inside = (lane >= p) & (lane < p + GROUP)
        new = []
        for t in range(len(tiles)):
            value = jnp.where(inside, 0.0, tiles[t])
            for a in range(GROUP):
                column = jnp.broadcast_to(tiles[t][:, p + a : p + a + 1], wide)
                value = value - column * updates[a]
            if t == own:
                for a in range(GROUP):
                    value = jnp.where(sublane == s + a, updates[a], value)
            new.append(value)
        tiles = new
    return tiles


def bits_of(count):
    return count.bit_length() - 1


def flip(index, k):
    return index + (1 - 2 * ((index // 2**k) % 2)) * 2**k


def reversed_bits(index, count):
    value = 0
    for k in range(bits_of(count)):
        value = value * 2 + (index // 2**k) % 2
    return value


def ordered_bits(index, order):
    value = 0
    for k in order:
        value = value * 2 + (index // 2**k) % 2
    return value


def span(start, size, unit):
    return pl.ds(pl.multiple_of(start, unit), size)


class Links:
    def __init__(self, send_sem, recv_sem):
        self.send_sem = send_sem
        self.recv_sem = recv_sem
        self.used = 0

    def copy(self, src, dst, device):
        at = self.used
        self.used += 1
        return lambda: pltpu.make_async_remote_copy(
            src_ref=src,
            dst_ref=dst,
            send_sem=self.send_sem.at[at],
            recv_sem=self.recv_sem.at[at],
            device_id=device,
            device_id_type=pl.DeviceIdType.MESH,
        )


def room(*arrays):
    total = 0
    for shape, dtype in arrays:
        width = jnp.dtype(dtype).itemsize
        tile = SUB * 4 // width
        lanes = -(-shape[-1] // BLOCK) * BLOCK
        rows = -(-shape[-2] // tile) * tile
        total += math.prod(shape[:-2]) * rows * lanes * width
    return min(63 * MIB, total + total // 32 + MIB)


def solve_room(passed, held):
    whole = room(*passed, *held)
    return whole if whole > 56 * MIB else room(*held)


def described(arrays):
    return [(a.shape, a.dtype) for a in arrays]


def greet(devices):
    barrier = pltpu.get_barrier_semaphore()
    for device in devices:
        pl.semaphore_signal(
            barrier, inc=1, device_id=device, device_id_type=pl.DeviceIdType.MESH
        )
    pl.semaphore_wait(barrier, len(devices))


def everyone():
    row_parts, mp_parts = lax.axis_size("rows"), lax.axis_size("mp")
    r, m = lax.axis_index("rows"), lax.axis_index("mp")
    devices = [{"mp": flip(m, k)} for k in range(bits_of(mp_parts))]
    devices += [{"rows": lax.rem(r + d, row_parts)} for d in range(1, row_parts)]
    return devices


def reduce_plans(rows, split):
    pieces = lax.axis_size("rows") * lax.axis_size("mp")
    depth = bits_of(lax.axis_size("mp"))
    units = rows // (16 * pieces)
    first = max(1, min(units - 1, (2 * units + 1) // 3)) if split else units
    order = [f"mp{k}" for k in range(depth)]
    plans = [(0, 16 * first, order + ["rows"])]
    if units > first:
        plans.append((16 * first * pieces, 16 * (units - first), order[:1] + ["rows"] + order[1:]))
    return plans


def reduce_sizes(rows, split):
    row_parts, mp_parts = lax.axis_size("rows"), lax.axis_size("mp")
    total = 0
    for _, piece, order in reduce_plans(rows, split):
        size = piece * row_parts * mp_parts
        for dim in order:
            parts = row_parts if dim == "rows" else 2
            total += size - size // parts
            size //= parts
    return total


def reduce_count():
    return 4 * (bits_of(lax.axis_size("mp")) + lax.axis_size("rows") - 1)


def reduce_lists(links, src, acc, recv, out, split):
    lists, off = [], 0
    for start, piece, order in reduce_plans(src.shape[0], split):
        stages, off = reduce_stages(links, src, acc, recv, out, start, piece, order, off)
        lists.append(steps_of(stages))
    return joined(*lists)


def reduce_stages(links, src, acc, recv, out, start, piece, order, off):
    row_parts, mp_parts = lax.axis_size("rows"), lax.axis_size("mp")
    r, m = lax.axis_index("rows"), lax.axis_index("mp")
    stages, held = [], []
    base, size = start, piece * row_parts * mp_parts
    for at, dim in enumerate(order):
        parts = row_parts if dim == "rows" else 2
        k = None if dim == "rows" else int(dim[2:])
        size //= parts
        source = src if at == 0 else acc
        sink = out if at == len(order) - 1 else acc
        copies = []
        for d in range(1, parts):
            to = lax.rem(r + d, row_parts) if k is None else 1 - (m // 2**k) % 2
            device = {"rows": to} if k is None else {"mp": flip(m, k)}
            copies.append(
                links.copy(
                    source.at[span(base + to * size, size, 16)],
                    recv.at[pl.ds(off + (d - 1) * size, size)],
                    device,
                )
            )
        keep = base + (r if k is None else (m // 2**k) % 2) * size

        def merge(source=source, sink=sink, keep=keep, off=off, size=size, parts=parts):
            def body(t, carry):
                step = pl.multiple_of(t * piece, 16)
                value = source[span(keep + step, piece, 16), :].astype(jnp.float32)
                for d in range(1, parts):
                    landed = recv[span(off + (d - 1) * size + step, piece, 16), :]
                    value = value + landed.astype(jnp.float32)
                sink[span(keep + step, piece, 16), :] = value.astype(sink.dtype)
                return carry

            lax.fori_loop(0, size // piece, body, 0)

        stages.append((copies, merge))
        off += (parts - 1) * size
        base = keep
        held.append((dim, k, keep, size))
    for dim, k, keep, size in reversed(held):
        mine = out.at[span(keep, size, 16)]
        if k is None:
            devices = [{"rows": lax.rem(r + d, row_parts)} for d in range(1, row_parts)]
        else:
            devices = [{"mp": flip(m, k)}]
        stages.append(([links.copy(mine, mine, device) for device in devices], None))
    return stages, off


def steps_of(stages):
    steps = []
    for s in range(len(stages) + 1):

        def step(s=s):
            if s > 0:
                for copy in stages[s - 1][0]:
                    copy().wait()
                if stages[s - 1][1] is not None:
                    stages[s - 1][1]()
            if s < len(stages):
                for copy in stages[s][0]:
                    copy().start()

        steps.append(step)
    return steps


def joined(*lists):
    def step(s):
        for one in lists:
            if s < len(one):
                one[s]()

    return [functools.partial(step, s) for s in range(max(len(one) for one in lists))]


def placed(ticks, steps, start, gap):
    for at, step in enumerate(steps):
        if start + at * gap >= len(ticks):
            return steps[at:]
        ticks[start + at * gap].append(step)
    return []


def run_steps(*lists):
    for step in joined(*lists):
        step()


def ring_place(r):
    row_parts = lax.axis_size("rows")
    return (1 - r % 2) * (r // 2) + (r % 2) * (row_parts - 1 - r // 2)


def ring_member(place):
    row_parts = lax.axis_size("rows")
    place = lax.rem(place + 2 * row_parts, row_parts)
    second = (2 * place) // row_parts
    return (1 - second) * 2 * place + second * (2 * (row_parts - 1 - place) + 1)


def ring_devices():
    place = ring_place(lax.axis_index("rows"))
    return [{"rows": ring_member(place + 1)}, {"rows": ring_member(place - 1)}]


def ring_sum_stages(links, src, recv, out, sign, lanes):
    row_parts = lax.axis_size("rows")
    place = ring_place(lax.axis_index("rows"))
    to = {"rows": ring_member(place + sign)}
    size = src.shape[0] // row_parts

    def chunk(step):
        at = lax.rem(place - sign * step + 2 * row_parts, row_parts)
        return span(at * size, size, 16)

    stages = []
    for s in range(row_parts - 1):
        source = src.at[chunk(0), lanes] if s == 0 else recv.at[s - 1]
        last = s == row_parts - 2

        def merge(s=s, last=last, rows=chunk(s + 1)):
            value = src[rows, lanes] + recv[s]
            if last:
                out[rows, lanes] = value
            else:
                recv[s] = value

        stages.append(([links.copy(source, recv.at[s], to)], merge))
    for s in range(row_parts - 1):
        piece = out.at[chunk(s - 1), lanes]
        stages.append(([links.copy(piece, piece, to)], None))
    return stages


def ring_gather_stages(links, src, out, sign, hops):
    row_parts = lax.axis_size("rows")
    place = ring_place(lax.axis_index("rows"))
    to = {"rows": ring_member(place + sign)}
    size = src.shape[0]
    stages = []
    for s in range(hops):
        at = lax.rem(place - sign * s + 2 * row_parts, row_parts)
        piece = out.at[span(at * size, size, 16)]
        stages.append(([links.copy(src if s == 0 else piece, piece, to)], None))
    return stages


def gather_kernel(
    scale, places_ref, src_ref, calib_ref, weight_ref, out_ref, kept_ref, y_ref, sel_ref,
    all_calib_ref, weight_vmem, chosen_ref, y_vmem, acc_ref, recv_ref, weight_sem, send_sem, recv_sem,
):
    row_parts = lax.axis_size("rows")
    weight_copy = pltpu.make_async_copy(weight_ref, weight_vmem, weight_sem)
    weight_copy.start()
    greet(everyone())
    links = Links(send_sem, recv_sem)
    steps = reduce_lists(links, src_ref, acc_ref, recv_ref, out_ref, True)
    rings = joined(
        steps_of(ring_gather_stages(links, calib_ref, all_calib_ref, 1, row_parts // 2)),
        steps_of(ring_gather_stages(links, calib_ref, all_calib_ref, -1, row_parts // 2 - 1)),
    )
    steps[0]()
    rings[0]()
    place = ring_place(lax.axis_index("rows"))
    size = calib_ref.shape[0]
    all_calib_ref[span(place * size, size, 16), :] = calib_ref[...]
    steps[1]()
    weight_copy.wait()
    for i in range(places_ref.shape[1]):
        at = lax.broadcasted_iota(jnp.int32, (BLOCK, weight_vmem.shape[0]), 1)
        row = lax.broadcasted_iota(jnp.int32, (BLOCK, weight_vmem.shape[0]), 0)
        chosen = jnp.where(at == row + places_ref[4, i], 1.0, 0.0).astype(jnp.bfloat16)
        chosen_ref[i * BLOCK : (i + 1) * BLOCK, :] = chosen

    def pick(t, carry):
        rows = pl.ds(pl.multiple_of(t * BLOCK, BLOCK), BLOCK)
        value = jnp.dot(chosen_ref[rows, :], weight_vmem[...], preferred_element_type=jnp.float32)
        kept_ref[rows, :] = value.astype(kept_ref.dtype)
        return carry

    count = places_ref.shape[1]
    used = count * BLOCK
    if kept_ref.shape[0] > used:
        kept_ref[used:, :] = jnp.zeros((kept_ref.shape[0] - used, kept_ref.shape[1]), kept_ref.dtype)
    for at in range(max(len(steps) - 2, len(rings) - 1)):
        if at + 2 < len(steps):
            steps[at + 2]()
        if at + 1 < len(rings):
            rings[at + 1]()
        low_at, high_at = at * count // 4, (at + 1) * count // 4
        if high_at <= count:
            lax.fori_loop(low_at, high_at, pick, 0)
    project(scale, chosen_ref, all_calib_ref, weight_vmem, y_vmem, y_ref, sel_ref)


def project(scale, chosen_ref, calib_ref, weight_ref, all_ref, y_ref, sel_ref):
    mp_parts, tokens, part = y_ref.shape
    tile = max(part, BLOCK)

    def body(t, carry):
        rows = pl.ds(pl.multiple_of(t * tile, tile), tile)
        value = lax.dot_general(
            calib_ref[...],
            weight_ref[rows, :],
            (((1,), (1,)), ((), ())),
            preferred_element_type=jnp.float32,
        )
        value = (value * scale).astype(jnp.bfloat16)
        all_ref[:, rows] = value
        for s in range(tile // part):
            y_ref[t * (tile // part) + s] = value[:, s * part : (s + 1) * part]
        return carry

    lax.fori_loop(0, weight_ref.shape[0] // tile, body, 0)
    count = chosen_ref.shape[0] // BLOCK
    for i in range(count):
        value = lax.dot_general(
            all_ref[...],
            chosen_ref[i * BLOCK : (i + 1) * BLOCK, :],
            (((1,), (1,)), ((), ())),
            preferred_element_type=jnp.float32,
        )
        sel_ref[i * tokens : (i + 1) * tokens, :] = value.astype(sel_ref.dtype)
    used = count * tokens
    if sel_ref.shape[0] > used:
        sel_ref[used:, :] = jnp.zeros((sel_ref.shape[0] - used, BLOCK), sel_ref.dtype)


def gather(places, low, calib, weight, scale):
    row_parts, mp_parts = lax.axis_size("rows"), lax.axis_size("mp")
    tokens = calib.shape[0] * row_parts
    count = reduce_count() + row_parts - 1
    unit = 16 * row_parts
    kept = -(-places.shape[1] * BLOCK // unit) * unit
    outs = (
        jax.ShapeDtypeStruct(low.shape, low.dtype),
        jax.ShapeDtypeStruct((kept, weight.shape[1]), weight.dtype),
        jax.ShapeDtypeStruct((mp_parts, tokens, weight.shape[0] // mp_parts), weight.dtype),
        jax.ShapeDtypeStruct((padded(places.shape[1] * tokens), BLOCK), weight.dtype),
    )
    scratch = [
        ((tokens, calib.shape[1]), calib.dtype),
        (weight.shape, weight.dtype),
        ((places.shape[1] * BLOCK, weight.shape[0]), weight.dtype),
        ((tokens, weight.shape[0]), weight.dtype),
        (low.shape, low.dtype),
        ((reduce_sizes(low.shape[0], True), BLOCK), low.dtype),
    ]
    return pl.pallas_call(
        functools.partial(gather_kernel, scale),
        out_shape=outs,
        in_specs=[SMEM, VMEM, VMEM, pl.BlockSpec(memory_space=pltpu.HBM)],
        out_specs=(VMEM, VMEM, VMEM, VMEM),
        scratch_shapes=[pltpu.VMEM(*one) for one in scratch]
        + [
            pltpu.SemaphoreType.DMA,
            pltpu.SemaphoreType.DMA((count,)),
            pltpu.SemaphoreType.DMA((count,)),
        ],
        compiler_params=pltpu.CompilerParams(
            collective_id=1,
            has_side_effects=True,
            vmem_limit_bytes=room(*described(outs), *described((low, calib)), *scratch),
        ),
    )(places, low, calib, weight)


def scatter_steps(links, src, acc, recv, out):
    m, mp_parts = lax.axis_index("mp"), lax.axis_size("mp")
    stages = []
    size, base, off = mp_parts, 0, 0
    depth = bits_of(mp_parts)
    for k in range(depth):
        size //= 2
        bit = (m // 2**k) % 2
        keep, send = base + bit * size, base + (1 - bit) * size
        source = src if k == 0 else acc
        copy = links.copy(
            source.at[pl.ds(send, size)], recv.at[pl.ds(off, size)], {"mp": flip(m, k)}
        )

        def merge(source=source, keep=keep, off=off, size=size, k=k):
            for t in range(size):
                a = source[keep + t].astype(jnp.float32)
                b = recv[off + t].astype(jnp.float32)
                if k == depth - 1:
                    out[...] = a + b
                else:
                    acc[keep + t] = (a + b).astype(acc.dtype)

        stages.append(([copy], merge))
        base, off = keep, off + size
    return stages


def pick_columns_kernel(places_ref, factor_ref, columns_ref, low_ref):
    j = pl.program_id(0)
    count = places_ref.shape[1]
    used = count * (count + 1) // 2 * BLOCK
    own = places_ref[1, j] != 0
    columns_ref[...] = jnp.where(own, factor_ref[...], 0.0)
    if low_ref.shape[0] > used:
        low_ref[used:, :] = jnp.zeros((low_ref.shape[0] - used, BLOCK), low_ref.dtype)
    for i in range(count):

        @pl.when(i >= j)
        def _():
            rows = pl.ds(pl.multiple_of(places_ref[2, i] * BLOCK, BLOCK), BLOCK)
            to = pl.ds(pl.multiple_of((i * (i + 1) // 2 + j) * BLOCK, BLOCK), BLOCK)
            both = (places_ref[3, i] != 0) & own
            low_ref[to, :] = jnp.where(both, factor_ref[rows, :], 0.0)


def padded(used):
    pieces = lax.axis_size("rows") * lax.axis_size("mp")
    return -(-used // (pieces * 16)) * pieces * 16


def pick_columns(places, factor):
    count = places.shape[1]
    rows = factor.shape[0]
    low_rows = padded(count * (count + 1) // 2 * BLOCK)
    return pl.pallas_call(
        pick_columns_kernel,
        out_shape=(
            jax.ShapeDtypeStruct((rows, count * BLOCK), jnp.float32),
            jax.ShapeDtypeStruct((low_rows, BLOCK), jnp.float32),
        ),
        grid_spec=pltpu.PrefetchScalarGridSpec(
            num_scalar_prefetch=1,
            grid=(count,),
            in_specs=[pl.BlockSpec((rows, BLOCK), lambda j, places: (0, places[0, j]))],
            out_specs=(
                pl.BlockSpec((rows, BLOCK), lambda j, places: (0, j)),
                pl.BlockSpec((low_rows, BLOCK), lambda j, places: (0, 0)),
            ),
        ),
    )(places, factor)


def invert(low_ref, out_ref, neg_ref, rhs_ref, pivot_ref, ticks):
    count = out_ref.shape[0] // BLOCK
    at = 0
    for i in range(count):
        for j in range(i + 1):
            block = low_ref[at : at + BLOCK, :]
            at += BLOCK
            out_ref[i * BLOCK : (i + 1) * BLOCK, j * BLOCK : (j + 1) * BLOCK] = block
            if j < i:
                out_ref[j * BLOCK : (j + 1) * BLOCK, i * BLOCK : (i + 1) * BLOCK] = block.T

    def tick(k, at):
        for s in range(at, len(ticks), TICKS):
            if ticks[s]:
                pl.when(TICKS * k + at == s)(lambda s=s: [step() for step in ticks[s]] and None)

    def stage(k, carry):
        tick(k, 0)
        here = pl.ds(pl.multiple_of(k * BLOCK, BLOCK), BLOCK)
        diag = out_ref[here, here]
        tiles = [diag[t * SUB : (t + 1) * SUB, :] for t in range(BLOCK // SUB)]
        tiles = sweep_block(tiles, lambda: tick(k, 1))
        for t in range(BLOCK // SUB):
            neg_ref[t * SUB : (t + 1) * SUB, :] = tiles[t]
        tick(k, 2)
        neg = neg_ref[...]
        r1, r2, r3 = split3(out_ref[here, :])
        a1, a2, a3 = split3(-neg)
        pivot_ref[...] = jnp.dot(
            jnp.concatenate([a1, a1, a2, a2, a1, a3], axis=1),
            jnp.concatenate([r1, r2, r1, r2, r3, r1], axis=0),
            preferred_element_type=jnp.float32,
        )
        pivot_ref[:, here] = neg
        b1, b2, b3 = split3(pivot_ref[...])
        for slot, part in enumerate((b1, b2, b1, b2, b3, b1)):
            rhs_ref[slot * BLOCK : (slot + 1) * BLOCK, :] = part

        def update(i, inner):
            rows = pl.ds(pl.multiple_of(i * BLOCK, BLOCK), BLOCK)
            c1, c2, c3 = split3(out_ref[rows, here])
            out_ref[rows, here] = jnp.zeros((BLOCK, BLOCK), jnp.float32)
            out_ref[rows, :] -= jnp.dot(
                jnp.concatenate([c1, c1, c2, c2, c1, c3], axis=1),
                rhs_ref[...],
                preferred_element_type=jnp.float32,
            )
            return inner

        lax.fori_loop(0, count // 2, update, 0)
        tick(k, 3)
        lax.fori_loop(count // 2, count, update, 0)
        out_ref[here, :] = pivot_ref[...]
        return carry

    lax.fori_loop(0, count, stage, 0)


def outputs_from(square_ref, columns_ref, y_ref, sel_ref, gone, total_ref, factor_ref, out_ref):
    count = square_ref.shape[0] // BLOCK
    tokens = y_ref.shape[0]
    total_ref[...] = jnp.zeros(total_ref.shape, jnp.float32)

    def body(k, carry):
        here = pl.ds(pl.multiple_of(k * BLOCK, BLOCK), BLOCK)
        c1, c2, c3 = split3(columns_ref[:, here])
        n1, n2, n3 = split3(square_ref[here, :])
        total_ref[...] -= jnp.dot(
            jnp.concatenate([c1, c1, c2, c2, c1, c3], axis=1),
            jnp.concatenate([n1, n2, n1, n2, n3, n1], axis=0),
            preferred_element_type=jnp.float32,
        )
        return carry

    lax.fori_loop(0, count, body, 0)
    factor_ref[...] = total_ref[...].astype(jnp.bfloat16)
    selected = jnp.concatenate(
        [sel_ref[i * tokens : (i + 1) * tokens, :] for i in range(count)], axis=1
    )
    update = lax.dot_general(
        selected, factor_ref[...], (((1,), (1,)), ((), ())), preferred_element_type=jnp.float32
    )
    value = jnp.where(gone == 0, y_ref[...] - update, 0.0)
    out_ref[...] = value.astype(jnp.bfloat16)


def moved_to(r, m, row_parts, mp_parts):
    per = row_parts // mp_parts
    return ((m + 1) % mp_parts) * per + r % per, r // per


def right_orders(row_parts):
    count = bits_of(row_parts)
    first = list(range(count))
    second = [1, 0] + first[2:] if count > 1 else first
    return first, second


def exchange_lists(links, out_ref, factor_ref, left_ref, right_ref, all_factor_ref):
    row_parts, mp_parts = lax.axis_size("rows"), lax.axis_size("mp")
    r, m = lax.axis_index("rows"), lax.axis_index("mp")
    tokens = out_ref.shape[0]
    to_row, to_mp = moved_to(r, m, row_parts, mp_parts)
    target = {"rows": to_row, "mp": to_mp}
    lists = []
    for h, order in enumerate(right_orders(row_parts)):
        half = tokens // 2
        slot = ordered_bits(to_row, order)
        copy = links.copy(out_ref.at[pl.ds(h * half, half)], right_ref.at[h, slot], target)
        stages = [([copy], None)]
        base, size = ordered_bits(r, order), 1
        for k in reversed(order):
            region = right_ref.at[h, pl.ds(base, size)]
            stages.append(([links.copy(region, region, {"rows": flip(r, k)})], None))
            base = base - ((base // size) % 2) * size
            size *= 2
        lists.append(steps_of(stages))
    for src, dst in ((out_ref, left_ref), (factor_ref, all_factor_ref)):
        stages = []
        base, size = reversed_bits(m, mp_parts), 1
        for k in reversed(range(bits_of(mp_parts))):
            region = dst.at[pl.ds(base, size)]
            source = src if size == 1 else region
            sink = dst.at[base] if size == 1 else region
            stages.append(([links.copy(source, sink, {"mp": flip(m, k)})], None))
            base = base - ((base // size) % 2) * size
            size *= 2
        lists.append(steps_of(stages))
    return lists


def solve_kernel(
    blocks_ref, low_ref, columns_ref, y_ref, sel_ref, kept_ref,
    left_ref, right_ref, all_factor_ref, all_kept_ref,
    factor_ref, out_ref, square_ref, neg_ref, rhs_ref, pivot_ref, total_ref,
    own_columns_ref, c_acc, c_recv, own_ref, y_acc, y_recv, all_ref, acc_ref, recv_ref,
    k_recv, send_sem, recv_sem,
):
    row_parts, mp_parts = lax.axis_size("rows"), lax.axis_size("mp")
    r, m = lax.axis_index("rows"), lax.axis_index("mp")
    to_row, to_mp = moved_to(r, m, row_parts, mp_parts)
    from_row = m * (row_parts // mp_parts) + r % (row_parts // mp_parts)
    from_mp = lax.rem(r // (row_parts // mp_parts) + mp_parts - 1, mp_parts)
    greet(everyone() + [{"rows": to_row, "mp": to_mp}, {"rows": from_row, "mp": from_mp}])
    links = Links(send_sem, recv_sem)
    ticks = [[] for _ in range(TICKS * (square_ref.shape[0] // BLOCK))]
    sum_steps = joined(
        reduce_lists(links, sel_ref, acc_ref, recv_ref, all_ref, False),
        steps_of(scatter_steps(links, y_ref, y_acc, y_recv, own_ref)),
    )
    column_steps = steps_of(scatter_steps(links, columns_ref, c_acc, c_recv, own_columns_ref))
    late = placed(ticks, sum_steps, 0, TICKS) + placed(ticks, column_steps, 0, 3 * TICKS)
    lanes = kept_ref.shape[1] // 4
    rings = []
    for at in range(4):
        stages = ring_sum_stages(
            links,
            kept_ref,
            k_recv.at[at],
            all_kept_ref,
            1 - 2 * (at % 2),
            slice(at * lanes, (at + 1) * lanes),
        )
        rings.append(placed(ticks, steps_of(stages), RING_GAP // 2 * (at // 2), RING_GAP))
    invert(low_ref, square_ref, neg_ref, rhs_ref, pivot_ref, ticks)
    for step in late:
        step()
    part = own_ref.shape[1]
    start = (r * mp_parts + reversed_bits(m, mp_parts)) * part
    feature = start + lax.broadcasted_iota(jnp.int32, (1, part), 1)
    gone = jnp.zeros((1, part), jnp.int32)
    for i in range(blocks_ref.shape[0]):
        first = blocks_ref[i] * BLOCK
        gone = jnp.where((feature >= first) & (feature < first + BLOCK), 1, gone)
    outputs_from(
        square_ref, own_columns_ref, own_ref, all_ref, gone, total_ref, factor_ref, out_ref
    )
    lists = exchange_lists(links, out_ref, factor_ref, left_ref, right_ref, all_factor_ref)
    steps = joined(*lists, *rings)
    steps[0]()
    mine = reversed_bits(m, mp_parts)
    left_ref[mine] = out_ref[...]
    all_factor_ref[mine] = factor_ref[...]
    for step in steps[1:]:
        step()


def solve(blocks, low, columns, y, selected, kept):
    row_parts, mp_parts = lax.axis_size("rows"), lax.axis_size("mp")
    copies = reduce_count() + 4 * bits_of(mp_parts) + 8 * (row_parts - 1)
    copies += 2 * (1 + bits_of(row_parts))
    chunk = (row_parts - 1, kept.shape[0] // row_parts, kept.shape[1] // 4)
    _, part, order = columns.shape
    tokens = y.shape[1]
    outs = (
        jax.ShapeDtypeStruct((mp_parts, tokens, part), jnp.bfloat16),
        jax.ShapeDtypeStruct((2, row_parts, tokens // 2, part), jnp.bfloat16),
        jax.ShapeDtypeStruct((mp_parts, part, order), jnp.bfloat16),
        jax.ShapeDtypeStruct(kept.shape, kept.dtype),
    )
    scratch = [
        ((part, order), jnp.bfloat16),
        ((tokens, part), jnp.bfloat16),
        ((order, order), jnp.float32),
        ((BLOCK, BLOCK), jnp.float32),
        ((6 * BLOCK, order), jnp.bfloat16),
        ((BLOCK, order), jnp.float32),
        ((part, order), jnp.float32),
        ((part, order), jnp.float32),
        (columns.shape, jnp.float32),
        ((mp_parts - 1, part, order), jnp.float32),
        ((tokens, part), jnp.float32),
        (y.shape, y.dtype),
        ((mp_parts - 1, tokens, part), y.dtype),
        (selected.shape, selected.dtype),
        (selected.shape, selected.dtype),
        ((reduce_sizes(selected.shape[0], False), BLOCK), selected.dtype),
        ((4,) + chunk, kept.dtype),
    ]
    return pl.pallas_call(
        solve_kernel,
        out_shape=outs,
        in_specs=[SMEM] + [VMEM] * 5,
        out_specs=(VMEM, VMEM, VMEM, VMEM),
        scratch_shapes=[pltpu.VMEM(*one) for one in scratch]
        + [pltpu.SemaphoreType.DMA((copies,)), pltpu.SemaphoreType.DMA((copies,))],
        compiler_params=pltpu.CompilerParams(
            collective_id=2,
            has_side_effects=True,
            vmem_limit_bytes=solve_room(
                described(outs) + described((low, columns, y, selected)), described((kept,)) + scratch
            ),
        ),
        cost_estimate=pl.CostEstimate(
            flops=60_000_000_000, bytes_accessed=2 * order * order * 4, transcendentals=0
        ),
    )(blocks, low, columns, y, selected, kept)


def gram_kernel(row_parts, mp_parts, left_ref, right_ref, out_ref):
    per = row_parts // mp_parts
    tokens, part = left_ref.shape[1:]
    first, second = right_orders(row_parts)
    left = left_ref[0]
    for at in range(row_parts):
        source_mp = (at // per - 1) % mp_parts
        column = (at % per) * mp_parts + reversed_bits(source_mp, mp_parts)
        right = jnp.concatenate(
            [right_ref[0, ordered_bits(at, first)], right_ref[1, ordered_bits(at, second)]], axis=0
        )
        value = lax.dot_general(
            left, right, (((0,), (0,)), ((), ())), preferred_element_type=jnp.float32
        )
        out_ref[:, column * part : (column + 1) * part] = value / tokens


def gram_of(left, right):
    mp_parts, tokens, part = left.shape
    row_parts = right.shape[1]
    width = row_parts * part
    return pl.pallas_call(
        functools.partial(gram_kernel, row_parts, mp_parts),
        grid=(mp_parts,),
        in_specs=[pl.BlockSpec((1, tokens, part), lambda i: (i, 0, 0)), VMEM],
        out_specs=pl.BlockSpec((part, width), lambda i: (i, 0)),
        out_shape=jax.ShapeDtypeStruct((mp_parts * part, width), jnp.float32),
        compiler_params=pltpu.CompilerParams(vmem_limit_bytes=32 * MIB),
    )(left, right)


def prune_kernel(blocks_ref, weight_ref, factor_ref, kept_ref, out_ref):
    step = pl.program_id(0)
    tile, width = weight_ref.shape
    row_block = lax.axis_index("rows") * pl.num_programs(0) * (tile // BLOCK)
    chunk = min(width, 512)
    for c in range(width // chunk):
        lanes = slice(c * chunk, (c + 1) * chunk)
        update = jnp.dot(factor_ref[...], kept_ref[:, lanes], preferred_element_type=jnp.float32)
        value = weight_ref[:, lanes].astype(jnp.float32) - update
        for s in range(tile // BLOCK):
            here = row_block + step * (tile // BLOCK) + s
            gone = blocks_ref[0] == here
            for i in range(1, blocks_ref.shape[0]):
                gone = gone | (blocks_ref[i] == here)
            rows = slice(s * BLOCK, (s + 1) * BLOCK)
            out_ref[rows, lanes] = jnp.where(gone, 0.0, value[rows, :]).astype(jnp.bfloat16)


def prune(blocks, weight, factor, kept_rows):
    rows, width = weight.shape
    order = factor.shape[1]
    tile = min(rows, 256)
    return pl.pallas_call(
        prune_kernel,
        out_shape=jax.ShapeDtypeStruct((rows, width), jnp.bfloat16),
        grid_spec=pltpu.PrefetchScalarGridSpec(
            num_scalar_prefetch=1,
            grid=(rows // tile,),
            in_specs=[
                pl.BlockSpec((tile, width), lambda i, blocks: (i, 0)),
                pl.BlockSpec((tile, order), lambda i, blocks: (i, 0)),
                pl.BlockSpec((order, width), lambda i, blocks: (0, 0)),
            ],
            out_specs=pl.BlockSpec((tile, width), lambda i, blocks: (i, 0)),
        ),
        compiler_params=pltpu.CompilerParams(vmem_limit_bytes=32 * MIB),
    )(blocks, weight, factor, kept_rows)


def shards(calib, weight, inverse_factor, pruned_blocks):
    rows_dev, width_dev = weight.shape
    mp_parts = lax.axis_size("mp")
    full_width = width_dev * mp_parts
    part = rows_dev // mp_parts
    m = lax.axis_index("mp")
    row_start = lax.axis_index("rows") * rows_dev
    col_start = m * width_dev
    starts = pruned_blocks * BLOCK
    col_offsets = starts - col_start
    row_offsets = starts - row_start
    places = jnp.stack(
        [
            jnp.clip(col_offsets, 0, width_dev - BLOCK) // BLOCK,
            ((col_offsets >= 0) & (col_offsets < width_dev)).astype(jnp.int32),
            jnp.clip(row_offsets, 0, rows_dev - BLOCK) // BLOCK,
            ((row_offsets >= 0) & (row_offsets < rows_dev)).astype(jnp.int32),
            row_offsets,
        ]
    ).astype(jnp.int32)
    columns, own_low = pick_columns(places, inverse_factor)
    columns = columns.reshape(mp_parts, part, columns.shape[1])
    low, own_kept, y, own_selected = gather(
        places, own_low, calib, weight, float(full_width) ** (-0.5)
    )
    left, right, all_factor, kept_rows = solve(
        pruned_blocks, low, columns, y, own_selected, own_kept
    )
    gram_block = gram_of(left, right)
    pruned_weight = prune(
        pruned_blocks, weight, all_factor.reshape(rows_dev, all_factor.shape[2]), kept_rows
    )
    return (pruned_weight, gram_block)


def solution(mesh):
    return jax.shard_map(
        shards,
        mesh=mesh,
        in_specs=(P("rows", "mp"), P("rows", "mp"), P("rows", "mp"), P()),
        out_specs=(P("rows", "mp"), P("rows", "mp")),
        check_vma=False,
    )
```
